128 devices in a mesh: row: 8 (over z, core), col: 16 (over y, x).
Axes of the slice: x: 4, y: 4, z: 4, core: 2. Of those that a mesh axis runs over, the one named last changes fastest.
Arguments:
- front_entries: float32 [16384, 16384], P(None, ('row', 'col')), as said below
- child_updates: float32 [4096, 128, 128], P(('row', 'col')), may hold values from -1 to 1
- row_maps: int32 [4096, 128], P(('row', 'col')), may hold values from 0 to 127, each once within a row
- col_maps: int32 [4096, 128], P(('row', 'col')), may hold values from 0 to 127, each once within a row
- target_columns: int32 [4096, 1], P(('row', 'col')), may hold values from 0 to 127; in each aligned block of 32 rows (0 to 31, 32 to 63, ...) at most 2 rows name the same one
- row_offsets: int32 [4096, 1], P(('row', 'col')), may hold values from 0 to 127
Outputs:
- factored: float32 [16, 8, 8, 16, 128, 128], P(None, 'row', None, 'col')
The draws below stay inside these ranges and needn't reach their ends.
Inputs may be any that keep to these rules, and one draw needn't show every extreme that they name: `target_columns`: within the rows of one device (aligned blocks of 32 rows) no block column is named more than 2 times; some device names one block column exactly 2 times. `row_maps`: each row is a permutation of 0 to 127. `col_maps`: each row is a permutation of 0 to 127. `front_entries`: entries off the diagonal lie in [0, 2]; diagonal entries lie between 2.5 and 3.5 times the square root of 16384.
All inputs are finite; a program needn't handle non-finite values.
Results may differ from the reference program's by a relative error of at most 0.0001.
Values sent between devices are 32-bit elements; how exact they have to be, the bound alone decides.
A program may use at most 192 MiB of HBM per device.

```python
import math
import jax
import jax.numpy as jnp
import numpy as np
from jax import lax

BLOCK = 128
BLOCKS = 128
ORDER = 16384
TILES = 32
SLOTS = 2
PANELS = 2
N_ROW = 8
N_COL = 16


def draw_front_entries(key, part):
    key_one, key_two = jax.random.split(key)
    root_order = math.sqrt(ORDER)
    entries = jax.random.uniform(key_one, (ORDER, ORDER), jnp.float32, 0.0, 2.0)
    diagonal = jax.random.uniform(key_two, (ORDER,), jnp.float32, 2.5, 3.5) * root_order
    indices = jnp.arange(ORDER, dtype=jnp.int32)
    on_diagonal = indices[:, None] == indices[None, :]
    return jnp.where(on_diagonal, diagonal[None, :], entries).astype(jnp.float32)


def place_ends(values, key, smallest, top_value):
    place = [jax.random.randint(jax.random.fold_in(key, axis), (), 0, length) for axis, length in enumerate(values.shape)]
    widest = values.shape.index(max(values.shape))
    beside = place[:widest] + [(place[widest] + 1) % values.shape[widest]] + place[widest + 1:]
    return values.at[tuple(place)].set(smallest).at[tuple(beside)].set(top_value)


def shard_levels(rng, dims, cuts, low, top_value):
    factor_of, own = 1.0, jax.random.fold_in(rng, 6)
    for axis_at, parts in cuts:
        draws = jnp.exp(jax.random.uniform(jax.random.fold_in(own, axis_at), (parts,), jnp.float32, low / len(cuts), top_value / len(cuts)))
        factor_of = factor_of * jnp.repeat(draws, dims[axis_at] // parts).reshape([-1 if axis == axis_at else 1 for axis in range(len(dims))])
    return factor_of


def deal_out(rng, own, number, rows, number_of, top, limit, lean):
    ranking = jax.random.permutation(rng, number_of)
    crowded, usual = load_shares(number_of, rows * top, limit, lean, True), load_shares(number_of, rows * top, limit, lean, False)
    places = jnp.arange(number_of)

    def named(sizes, offset_by):
        used = int((sizes > 0).sum())
        fixed = max(1, used // 4)
        shifted = fixed + (places - fixed + offset_by * (used - fixed)) % max(1, number_of - fixed)
        return jnp.zeros((number_of,), jnp.int32).at[ranking[jnp.where(places < fixed, places, shifted)]].set(jnp.asarray(sizes, jnp.int32))

    sizes = jnp.where(number % 4 == 0, named(crowded, number // 4), named(usual, number - number // 4 - 1))
    mixed = jax.random.permutation(jax.random.fold_in(own, 3), number_of)
    giver, sink = mixed[0:number_of // 2 * 2:2], mixed[1:number_of // 2 * 2:2]
    margin = jnp.minimum(sizes[giver] - 1, limit - sizes[sink]) // 2
    margin = jnp.where((giver == ranking[0]) | (sink == ranking[0]) | (sizes[sink] == 0), 0, jnp.maximum(margin, 0))
    shifted = jax.random.randint(jax.random.fold_in(own, 4), (number_of // 2,), 0, 1 << 20) % (margin + 1)
    sizes = sizes.at[giver].add(-shifted).at[sink].add(shifted)
    labels = jnp.searchsorted(jnp.cumsum(sizes), jnp.arange(rows * top), side="right").astype(jnp.int32)
    grid = labels.reshape(top, rows).T
    grid = grid[jax.random.permutation(jax.random.fold_in(own, 1), rows)]
    offset_by = jax.random.randint(jax.random.fold_in(own, 2), (rows, 1), 0, top)
    return jnp.take_along_axis(grid, (jnp.arange(top)[None, :] + offset_by) % top, axis=1)


def load_shares(count, total, most, slope, full):
    weights = [(1 << 20) // math.isqrt(standing ** slope) + 1 for standing in range(1, count + 1)]
    largest = most if full else min(most, max(-(-total // count), total * weights[0] // sum(weights)))
    least = 1 if total - largest >= count - 1 else 0
    holding, surplus = [largest] + [least] * (count - 1), total - largest - least * (count - 1)
    while surplus > 0:
        free = [i for i in range(1, count) if holding[i] < largest] or [i for i in range(1, count) if holding[i] < most]
        mass, remaining = sum([weights[i] for i in free]), surplus
        for i in free:
            extra = min(most - holding[i], max(1, remaining * weights[i] // mass), surplus)
            holding[i] = holding[i] + extra
            surplus = surplus - extra
    return np.array(holding)


def setup_inputs(seed: int = 0) -> dict:
    streams_of = jax.random.split(jax.random.key(seed), 7)
    front_entries = draw_front_entries(jax.random.fold_in(streams_of[6], 71), 0)
    child_updates = jnp.clip(jax.random.uniform(streams_of[1], (BLOCKS * TILES, BLOCK, BLOCK), jnp.float32, -1.0, 1.0) * shard_levels(streams_of[1], (BLOCKS * TILES, BLOCK, BLOCK), ((0, 128),), -0.4, 0.0), -1.0, 1.0)
    row_maps = jax.vmap(lambda own: jax.random.permutation(own, BLOCK))(jax.random.split(streams_of[2], (BLOCKS * TILES))).reshape((BLOCKS * TILES, BLOCK)).astype(jnp.int32)
    col_maps = jax.vmap(lambda own: jax.random.permutation(own, BLOCK))(jax.random.split(streams_of[3], (BLOCKS * TILES))).reshape((BLOCKS * TILES, BLOCK)).astype(jnp.int32)
    target_columns_keys = jax.random.split(jax.random.fold_in(streams_of[4], 1), (BLOCKS * TILES) // TILES)
    target_columns_turns = jax.random.permutation(jax.random.fold_in(streams_of[4], 3), (BLOCKS * TILES) // TILES)
    target_columns = jax.vmap(lambda own, number: deal_out(jax.random.fold_in(streams_of[4], 2), own, number, TILES, BLOCKS, 1, SLOTS, 2))(target_columns_keys, target_columns_turns).reshape((BLOCKS * TILES, 1))
    row_offsets = place_ends(jax.random.randint(streams_of[5], (BLOCKS * TILES, 1), 0, BLOCKS), jax.random.fold_in(streams_of[5], 1), 0, BLOCKS - 1).astype(jnp.int32)
    return {"front_entries": front_entries, "child_updates": child_updates, "row_maps": row_maps, "col_maps": col_maps, "target_columns": target_columns, "row_offsets": row_offsets}


PRECISE = lax.Precision.HIGHEST

def place_tile(tile_data, row_map, col_map):
    return jnp.zeros(tile_data.shape, tile_data.dtype).at[row_map[:, None], col_map[None, :]].set(tile_data)

def reference(front_entries, child_updates, row_maps, col_maps, target_columns, row_offsets):
    columns = target_columns[:, 0]
    offsets = row_offsets[:, 0]
    target_rows = columns + offsets % (BLOCKS - columns)
    block_ids = (target_rows * BLOCKS + columns).astype(jnp.int32)
    blocks = front_entries.reshape(BLOCKS, BLOCK, BLOCKS, BLOCK).transpose(0, 2, 1, 3).reshape(BLOCKS * BLOCKS, BLOCK, BLOCK)
    senders = N_ROW * N_COL

    def grouped(values):
        return values.reshape((senders, TILES) + values.shape[1:])

    def add_group(accum, member):
        tile_set, row_set, col_set, id_set = member
        placed = jax.vmap(place_tile)(tile_set, row_set, col_set)
        return (accum.at[id_set].add(placed), None)
    blocks, _ = lax.scan(add_group, blocks, (grouped(child_updates), grouped(row_maps), grouped(col_maps), grouped(block_ids)))
    matrix = blocks.reshape(BLOCKS, BLOCKS, BLOCK, BLOCK).transpose(0, 2, 1, 3).reshape(ORDER, ORDER)
    for panel_idx in range(PANELS):
        start = panel_idx * BLOCK
        finish = start + BLOCK
        pivot_tile = matrix[start:finish, start:finish]
        symmetric = jnp.tril(pivot_tile) + jnp.tril(pivot_tile, -1).T
        pivot_factor = jnp.linalg.cholesky(symmetric)
        under_part = matrix[finish:, start:finish]
        panel_part = jax.scipy.linalg.solve_triangular(pivot_factor, under_part.T, lower=True).T
        matrix = matrix.at[finish:, finish:].add(-jnp.dot(panel_part, panel_part.T, precision=PRECISE))
        matrix = matrix.at[start:finish, start:finish].set(pivot_factor)
        matrix = matrix.at[finish:, start:finish].set(panel_part)
    matrix = jnp.tril(matrix)
    return matrix.reshape(BLOCKS // N_ROW, N_ROW, BLOCK, BLOCKS // N_COL, N_COL, BLOCK).transpose(0, 1, 3, 4, 2, 5)
```

```python
import functools

import jax
import jax.numpy as jnp
from jax import lax
from jax.experimental import pallas as pl
from jax.experimental.pallas import tpu as pltpu
from jax.sharding import PartitionSpec as P

SLOTS = 2
EDGE = 128
MESH = pl.DeviceIdType.MESH
PRECISE = lax.Precision.HIGHEST
F32 = jnp.float32


def dot(a, b, dims):
    return lax.dot_general(a, b, (dims, ((), ())), precision=PRECISE, preferred_element_type=F32)


NN = ((1,), (0,))
NT = ((1,), (1,))
TN = ((0,), (0,))


def pack_kernel(position, tile, row_map, col_map, out):
    t = pl.program_id(0)
    levels = lax.broadcasted_iota(jnp.int32, (EDGE, EDGE), 0)
    col_hot = (levels == col_map[pl.ds(t, 1), :]).astype(F32)
    row_hot = (levels == row_map[pl.ds(t, 1), :]).astype(F32)
    half = dot(tile[0], col_hot, NT)
    out[0] = dot(row_hot, half, NN)


def pack(position, tiles, row_map, col_map, slots):
    count = tiles.shape[0]
    whole = pl.BlockSpec((count, EDGE), lambda t, pos: (0, 0))
    return pl.pallas_call(
        pack_kernel,
        grid_spec=pltpu.PrefetchScalarGridSpec(
            num_scalar_prefetch=1,
            grid=(count,),
            in_specs=[pl.BlockSpec((1, EDGE, EDGE), lambda t, pos: (t, 0, 0)), whole, whole],
            out_specs=pl.BlockSpec((1, EDGE, EDGE), lambda t, pos: (pos[t], 0, 0)),
        ),
        out_shape=jax.ShapeDtypeStruct((slots, EDGE, EDGE), F32),
        name="pack",
    )(position, tiles, row_map, col_map)


DEPTH = 8


def gather_kernel(landing, front, arrived, out, acc, ring, index, sem, ring_sem):
    slots = arrived.shape[0]
    load = pltpu.make_async_copy(front, acc, sem)
    load.start()

    def note(k, n):
        valid = landing[k] >= 0

        @pl.when(valid)
        def _():
            index[n] = k

        return n + valid.astype(jnp.int32)

    count = lax.fori_loop(0, slots, note, 0)

    def fetch(k):
        slot = lax.rem(k, DEPTH)
        return pltpu.make_async_copy(arrived.at[index[k]], ring.at[slot], ring_sem.at[slot])

    def prime(k, _):
        fetch(k).start()
        return 0

    lax.fori_loop(0, jnp.minimum(count, DEPTH), prime, 0)
    load.wait()

    def step(k, _):
        fetch(k).wait()
        where = landing[index[k]]
        acc[where] = acc[where] + ring[lax.rem(k, DEPTH)]

        @pl.when(k + DEPTH < count)
        def _():
            fetch(k + DEPTH).start()

        return 0

    lax.fori_loop(0, count, step, 0)
    store = pltpu.make_async_copy(acc, out, sem)
    store.start()
    store.wait()


def gather(landing, front, arrived):
    hbm = pl.BlockSpec(memory_space=pltpu.HBM)
    return pl.pallas_call(
        gather_kernel,
        in_specs=[pl.BlockSpec(memory_space=pltpu.SMEM), hbm, hbm],
        out_specs=hbm,
        out_shape=jax.ShapeDtypeStruct(front.shape, F32),
        scratch_shapes=[
            pltpu.VMEM(front.shape, F32),
            pltpu.VMEM((DEPTH, EDGE, EDGE), F32),
            pltpu.SMEM(landing.shape, jnp.int32),
            pltpu.SemaphoreType.DMA,
            pltpu.SemaphoreType.DMA((DEPTH,)),
        ],
        compiler_params=pltpu.CompilerParams(vmem_limit_bytes=32 << 20),
        name="gather",
    )(landing, front, arrived)


STEP = 8


def factor(work, upper):
    rows8 = lax.broadcasted_iota(jnp.int32, (STEP, 2 * EDGE), 0)
    lanes = lax.broadcasted_iota(jnp.int32, (STEP, EDGE), 1)

    def block(b, _):
        first = pl.multiple_of(b * STEP, STEP)
        x = work[pl.ds(first, STEP), :]
        d = pltpu.roll(x[:, :EDGE], lax.rem(EDGE - first, EDGE), 1)
        for t in range(STEP):
            pivot = d[t : t + 1, t : t + 1]
            scale = lax.rsqrt(pivot)
            ratio = d[:, t : t + 1] / pivot
            below = rows8[:, :1] > t
            at = rows8[:, :1] == t
            ratio = jnp.where(below, ratio, jnp.where(at, 1.0 - scale, 0.0))
            x = x - ratio * x[t : t + 1, :]
            d = d - ratio * d[t : t + 1, :]
        upper[pl.ds(first, STEP), :] = x
        left = jnp.where(lanes >= first + STEP, x[:, :EDGE], 0.0)
        work[...] = work[...] - dot(left, x, TN)
        return 0

    lax.fori_loop(0, EDGE // STEP, block, 0)


def panel_kernel(
    R, C, col, grid, qrow, qcol,
    stage, diag, chunk, qc, qrow_v, work, upper, low,
    st_in, st_out, b_send, b_recv, dgr_send, dgc_send, dg_recv, sc_send, ck_recv,
    ag_send, ag_recv, rl_send, rl_recv, out_sem, qc_sem,
):
    r = lax.axis_index("row")
    c = lax.axis_index("col")
    NB = R * C
    ratio = C // R
    j = r * C + c
    start_of = lambda column: jnp.where(column < 2, 0, column)
    i0 = start_of(j)

    def remote(src, dst, ss, rs, rr, cc):
        return pltpu.make_async_remote_copy(
            src_ref=src, dst_ref=dst, send_sem=ss, recv_sem=rs, device_id=(rr, cc), device_id_type=MESH
        )

    barrier = pltpu.get_barrier_semaphore()
    for k in range(1, R):
        pl.semaphore_signal(barrier, inc=1, device_id=(lax.rem(r + k, R), c), device_id_type=MESH)
    for k in range(1, C):
        pl.semaphore_signal(barrier, inc=1, device_id=(r, lax.rem(c + k, C)), device_id_type=MESH)
    pl.semaphore_wait(barrier, R + C - 2)

    pieces = ((0, 0, 2), (1, 2, 1))

    def diag_row(p, k):
        owner, at, n = pieces[p]
        return remote(
            col.at[pl.ds(owner, n)], diag.at[pl.ds(at, n)], dgr_send.at[k], dg_recv.at[p], lax.rem(r + k, R), c
        )

    def diag_col(p, k):
        owner, at, n = pieces[p]
        here = diag.at[pl.ds(at, n)]
        return remote(here, here, dgc_send.at[k], dg_recv.at[p], r, lax.rem(c + k, C))

    def diag_own(p):
        owner, at, n = pieces[p]
        return pltpu.make_async_copy(col.at[pl.ds(owner, n)], diag.at[pl.ds(at, n)], dg_recv.at[p])

    for p in range(2):

        @pl.when((r == 0) & (c == pieces[p][0]))
        def _():
            for k in range(1, R):
                diag_row(p, k).start()
            diag_own(p).start()

    def b_copy(i):
        return remote(
            col.at[i], grid.at[i // R, r], b_send.at[i], b_recv.at[i // R, r], lax.rem(i, R), c
        )

    def b_wait(jl, s):
        remote(col.at[0], grid.at[jl, s], b_send.at[0], b_recv.at[jl, s], r, c).wait_recv()

    def own_in(jl):
        return pltpu.make_async_copy(col.at[jl * R + r], stage.at[jl], st_in.at[jl])

    def own_out(jl):
        return pltpu.make_async_copy(stage.at[jl], grid.at[jl, r], st_out.at[jl])

    def over(low_end, high_end, body):
        def run(i, _):
            body(i)
            return 0

        lax.fori_loop(low_end, high_end, run, 0)

    def own_blocks(body):
        def run(jl):
            @pl.when(jl * R + r >= i0)
            def _():
                body(jl)

        over(0, C, run)

    def sent_blocks(body):
        def run(i):
            @pl.when(lax.rem(i, R) != r)
            def _():
                body(i)

        over(i0, NB, run)

    late = (r == 1) & (c < 2)
    own_blocks(lambda jl: own_in(jl).start())

    @pl.when(jnp.logical_not(late))
    def _():
        sent_blocks(lambda i: b_copy(i).start())

    def own_turn(jl):
        own_in(jl).wait()
        own_out(jl).start()

    own_blocks(own_turn)

    def diag_wait(p):
        diag_own(p).wait()

    for p in range(2):

        @pl.when(c == pieces[p][0])
        def _():
            diag_wait(p)
            for k in range(1, C):
                diag_col(p, k).start()

    for p in range(2):

        @pl.when(c != pieces[p][0])
        def _():
            diag_wait(p)

    rows = lax.broadcasted_iota(jnp.int32, (EDGE, EDGE), 0)
    cols = lax.broadcasted_iota(jnp.int32, (EDGE, EDGE), 1)
    eye = (rows == cols).astype(F32)

    def pivot(block, at):
        work[:, :EDGE] = jnp.where(rows >= cols, block, block.T)
        work[:, EDGE:] = eye
        factor(work, upper)
        low[at] = jnp.where(rows >= cols, upper[:, :EDGE].T, 0.0)
        low[at + 1] = jnp.where(rows >= cols, upper[:, EDGE:], 0.0)

    pivot(diag[0], 0)
    low[2] = dot(diag[1], low[1], NT)
    pivot(diag[2] - dot(low[2], low[2], NT), 3)

    def scatter(jl, k):
        return remote(grid.at[jl, 0], chunk.at[k], sc_send.at[jl], ck_recv.at[k], r, jl)

    def scatter_own(jl, k):
        return pltpu.make_async_copy(grid.at[jl, 0], chunk.at[k], ck_recv.at[k])

    for k in range(2):

        @pl.when(c == k)
        def _():
            def run(jl):
                @pl.when(r == 0)
                def _():
                    own_out(jl).wait()

                @pl.when(r != 0)
                def _():
                    b_wait(jl, 0)

                @pl.when(jl == c)
                def _():
                    scatter_own(jl, k).start()

                @pl.when(jl != c)
                def _():
                    scatter(jl, k).start()

            over(0, C, run)

    @pl.when(late)
    def _():
        sent_blocks(lambda i: b_copy(i).start())

    scatter_own(0, 0).wait()
    scatter_own(0, 1).wait()

    i = c * R + r
    q0 = dot(chunk[0], low[1], NT)
    q1 = dot(chunk[1] - dot(q0, low[2], NT), low[4], NT)
    q0 = jnp.where(i == 0, low[0], jnp.where(i == 1, low[2], q0))
    q1 = jnp.where(i == 0, 0.0, jnp.where(i == 1, low[3], q1))
    qc[:, :EDGE] = q0
    qc[:, EDGE:] = q1

    def spread(k):
        return remote(qc, qrow_v.at[c], ag_send.at[k], ag_recv.at[c], r, lax.rem(c + k, C))

    own_q = pltpu.make_async_copy(qc, qrow_v.at[c], qc_sem)
    own_q.start()
    for k in range(1, C):
        spread(k).start()
    own_q.wait()

    def spread_wait(jl):
        @pl.when(jl != c)
        def _():
            remote(qc, qrow_v.at[jl], ag_send.at[0], ag_recv.at[jl], r, c).wait_recv()

    over(0, C, spread_wait)

    source = lax.rem(c, R)

    def relay(s, k):
        jl = s * ratio + c // R
        return remote(
            qrow_v.at[jl], qcol.at[s], rl_send.at[s, k], rl_recv.at[s], lax.rem(r + k, R), c
        )

    def relay_own(s):
        return pltpu.make_async_copy(qrow_v.at[s * ratio + c // R], qcol.at[s], rl_recv.at[s])

    @pl.when(r == source)
    def _():
        def run(s):
            for k in range(1, R):
                relay(s, k).start()
            relay_own(s).start()

        over(0, R, run)

    keep = pltpu.make_async_copy(qrow_v, qrow, out_sem)
    keep.start()

    over(0, R, lambda s: relay_own(s).wait())
    keep.wait()

    for s in range(R):
        begin = start_of(s * C + c)

        def run(jl):
            @pl.when((r != s) & (jl * R + r >= begin))
            def _():
                b_wait(jl, s)

        if s == 0:

            @pl.when(c >= 2)
            def _():
                over(0, C, run)
        else:
            over(0, C, run)

    @pl.when((r != 0) | (c >= 2))
    def _():
        own_blocks(lambda jl: own_out(jl).wait())

    sent_blocks(lambda i: b_copy(i).wait_send())

    for p in range(2):

        @pl.when((r == 0) & (c == pieces[p][0]))
        def _():
            for k in range(1, R):
                diag_row(p, k).wait_send()

        @pl.when(c == pieces[p][0])
        def _():
            for k in range(1, C):
                diag_col(p, k).wait_send()

    for k in range(2):

        @pl.when(c == k)
        def _():
            def run(jl):
                @pl.when(jl != c)
                def _():
                    scatter(jl, k).wait_send()

            over(0, C, run)

    for k in range(1, C):
        spread(k).wait_send()

    @pl.when(r == source)
    def _():
        def run(s):
            for k in range(1, R):
                relay(s, k).wait_send()

        over(0, R, run)


def panels(R, C, column):
    hbm = pl.BlockSpec(memory_space=pltpu.HBM)
    dma = pltpu.SemaphoreType.DMA
    return pl.pallas_call(
        functools.partial(panel_kernel, R, C),
        in_specs=[hbm],
        out_specs=[hbm, hbm, hbm],
        out_shape=[
            jax.ShapeDtypeStruct((C, R, EDGE, EDGE), F32),
            jax.ShapeDtypeStruct((C, EDGE, 2 * EDGE), F32),
            jax.ShapeDtypeStruct((R, EDGE, 2 * EDGE), F32),
        ],
        scratch_shapes=[
            pltpu.VMEM((C, EDGE, EDGE), F32),
            pltpu.VMEM((3, EDGE, EDGE), F32),
            pltpu.VMEM((2, EDGE, EDGE), F32),
            pltpu.VMEM((EDGE, 2 * EDGE), F32),
            pltpu.VMEM((C, EDGE, 2 * EDGE), F32),
            pltpu.VMEM((EDGE, 2 * EDGE), F32),
            pltpu.VMEM((EDGE, 2 * EDGE), F32),
            pltpu.VMEM((5, EDGE, EDGE), F32),
            dma((C,)), dma((C,)), dma((R * C,)), dma((C, R)),
            dma((R,)), dma((C,)), dma((2,)), dma((C,)), dma((2,)),
            dma((C,)), dma((C,)), dma((R, R)), dma((R,)), dma, dma,
        ],
        compiler_params=pltpu.CompilerParams(
            collective_id=0, has_side_effects=True, vmem_limit_bytes=32 << 20
        ),
        name="panels",
    )(column)


def update_kernel(R, C, place, grid, qrow, qcol, out):
    jl = pl.program_id(0)
    r, c = place[0], place[1]
    i = jl * R + r
    rows = lax.broadcasted_iota(jnp.int32, (EDGE, EDGE), 0)
    cols = lax.broadcasted_iota(jnp.int32, (EDGE, EDGE), 1)
    for s in range(R):
        j = s * C + c

        @pl.when(i < j)
        def _():
            out[0, s] = jnp.zeros((EDGE, EDGE), F32)

        @pl.when((i >= j) & (j < 2))
        def _():
            out[0, s] = jnp.where(j == 0, qrow[0, :, :EDGE], qrow[0, :, EDGE:])

        @pl.when((i >= j) & (j >= 2))
        def _():
            fresh = grid[0, s] - dot(qrow[0], qcol[s], NT)
            out[0, s] = jnp.where((i > j) | (rows >= cols), fresh, 0.0)


def update(R, C, place, grid, qrow, qcol):
    wide = pl.BlockSpec((1, R, EDGE, EDGE), lambda jl, place: (jl, 0, 0, 0))
    return pl.pallas_call(
        functools.partial(update_kernel, R, C),
        grid_spec=pltpu.PrefetchScalarGridSpec(
            num_scalar_prefetch=1,
            grid=(C,),
            in_specs=[
                wide,
                pl.BlockSpec((1, EDGE, 2 * EDGE), lambda jl, place: (jl, 0, 0)),
                pl.BlockSpec((R, EDGE, 2 * EDGE), lambda jl, place: (0, 0, 0)),
            ],
            out_specs=wide,
        ),
        out_shape=jax.ShapeDtypeStruct((C, R, EDGE, EDGE), F32),
        name="update",
    )(place, grid, qrow, qcol)


def local(front_entries, child_updates, row_maps, col_maps, target_columns, row_offsets):
    R = lax.axis_size("row")
    C = lax.axis_size("col")
    count = R * C
    held = child_updates.shape[0]
    columns = target_columns[:, 0]
    offsets = row_offsets[:, 0]
    target_rows = columns + offsets % (count - columns)
    serial = jnp.arange(held, dtype=jnp.int32)
    earlier = (columns[:, None] == columns[None, :]) & (serial[None, :] < serial[:, None])
    position = columns * SLOTS + jnp.sum(earlier.astype(jnp.int32), axis=1)
    hit = position[:, None] == jnp.arange(count * SLOTS, dtype=jnp.int32)[None, :]
    targets = jnp.max(jnp.where(hit, target_rows[:, None], -1), axis=0)
    outgoing = pack(position, child_updates, row_maps, col_maps, count * SLOTS)
    landing = lax.all_to_all(targets, ("row", "col"), split_axis=0, concat_axis=0, tiled=True)
    arrived = lax.all_to_all(outgoing, ("row", "col"), split_axis=0, concat_axis=0, tiled=True)
    column = gather(landing, front_entries.reshape(count, EDGE, EDGE), arrived)
    grid, qrow, qcol = panels(R, C, column)
    place = jnp.stack([lax.axis_index("row"), lax.axis_index("col")]).astype(jnp.int32)
    result = update(R, C, place, grid, qrow, qcol)
    return result.reshape(C, 1, R, 1, EDGE, EDGE)


def solution(mesh):
    return jax.shard_map(
        local,
        mesh=mesh,
        in_specs=(
            P(None, ("row", "col")),
            P(("row", "col"), None, None),
            P(("row", "col"), None),
            P(("row", "col"), None),
            P(("row", "col"), None),
            P(("row", "col"), None),
        ),
        out_specs=P(None, "row", None, "col", None, None),
        check_vma=False,
    )
```

```python
import functools
import math

import jax
import jax.numpy as jnp
from jax import lax
from jax.experimental import pallas as pl
from jax.experimental.pallas import tpu as pltpu
from jax.sharding import PartitionSpec as P

EDGE = 128
MESH = pl.DeviceIdType.MESH
PRECISE = lax.Precision.HIGHEST
F32 = jnp.float32
BF16 = jnp.bfloat16
NN = ((1,), (0,))
NT = ((1,), (1,))
TN = ((0,), (0,))


def dot(a, b, dims):
    return lax.dot_general(a, b, (dims, ((), ())), precision=PRECISE, preferred_element_type=F32)


def dot16(a, b, dims):
    return lax.dot_general(a, b, (dims, ((), ())), preferred_element_type=F32)


def remote(src, dst, ss, rs, rr, cc):
    return pltpu.make_async_remote_copy(
        src_ref=src, dst_ref=dst, send_sem=ss, recv_sem=rs, device_id=(rr, cc), device_id_type=MESH
    )


def over(low, high, body):
    def run(i, _):
        body(i)
        return 0

    lax.fori_loop(low, high, run, 0)


def greet(R, C, r, c):
    barrier = pltpu.get_barrier_semaphore()
    for k in range(1, R):
        pl.semaphore_signal(barrier, inc=1, device_id=(lax.rem(r + k, R), c), device_id_type=MESH)
    for k in range(1, C):
        pl.semaphore_signal(barrier, inc=1, device_id=(r, lax.rem(c + k, C)), device_id_type=MESH)
    pl.semaphore_wait(barrier, R + C - 2)


GROUP = 4


def place_kernel(C, tile, row_map, col_map, out):
    t = pl.program_id(0)
    levels = lax.broadcasted_iota(jnp.int32, (EDGE, EDGE), 0)
    for g in range(GROUP):
        k = t * GROUP + g
        col_hot = (levels == col_map[pl.ds(k, 1), :]).astype(F32).astype(BF16)
        row_hot = (levels == row_map[pl.ds(k, 1), :]).astype(F32).astype(BF16)
        x = tile[g]
        first = x.astype(BF16)
        rest = x - first.astype(F32)
        second = rest.astype(BF16)
        third = (rest - second.astype(F32)).astype(BF16)
        parts = [dot16(p, col_hot, NT).astype(BF16) for p in (first, second, third)]
        placed = (
            dot16(row_hot, parts[0], NN) + dot16(row_hot, parts[1], NN)
        ) + dot16(row_hot, parts[2], NN)
        for q in range(C):
            out[q, g] = placed[q * (EDGE // C) : (q + 1) * (EDGE // C), :]


def place_tiles(C, tiles, row_map, col_map):
    count = tiles.shape[0]
    whole = pl.BlockSpec((count, EDGE), lambda t: (0, 0))
    return pl.pallas_call(
        functools.partial(place_kernel, C),
        grid=(count // GROUP,),
        in_specs=[pl.BlockSpec((GROUP, EDGE, EDGE), lambda t: (t, 0, 0)), whole, whole],
        out_specs=pl.BlockSpec((C, GROUP, EDGE // C, EDGE), lambda t: (0, t, 0, 0)),
        out_shape=jax.ShapeDtypeStruct((C, count, EDGE // C, EDGE), F32),
        name="place",
    )(tiles, row_map, col_map)


def spread_kernel(
    R, C, cap2, cap3, placed, index2, index3, col, grid, out,
    r1, s2, r2, s3, stage,
    st_in, st_out, b_send, b_recv, p1_send, p1_recv, p2_send, p2_recv, p3_send, p3_recv,
):
    r = lax.axis_index("row")
    c = lax.axis_index("col")
    NB = R * C
    T = placed.shape[1]
    start_of = lambda column: jnp.where(column < 2, 0, column)
    i0 = start_of(r * C + c)
    greet(R, C, r, c)

    def first(k):
        to = lax.rem(c + k, C)
        return remote(placed.at[to], r1.at[pl.ds(c * T, T)], p1_send.at[k], p1_recv.at[c], r, to)

    def first_wait(k):
        src = lax.rem(c + k, C)
        remote(placed.at[0], r1.at[pl.ds(src * T, T)], p1_send.at[0], p1_recv.at[src], r, c).wait_recv()

    first_own = pltpu.make_async_copy(placed.at[c], r1.at[pl.ds(c * T, T)], p1_recv.at[c])
    first_own.start()
    for k in range(1, C):
        first(k).start()

    def b_copy(i):
        return remote(
            col.at[i], grid.at[i // R, r], b_send.at[i], b_recv.at[i // R, r], lax.rem(i, R), c
        )

    def own_in(jl):
        return pltpu.make_async_copy(col.at[jl * R + r], stage.at[jl], st_in.at[jl])

    def own_out(jl):
        return pltpu.make_async_copy(stage.at[jl], grid.at[jl, r], st_out.at[jl])

    def own_blocks(body):
        def run(jl):
            @pl.when(jl * R + r >= i0)
            def _():
                body(jl)

        over(0, C, run)

    def sent_blocks(low, high, body):
        def run(i):
            @pl.when(lax.rem(i, R) != r)
            def _():
                body(i)

        over(low, high, run)

    middle = i0 + (NB - i0) // 4
    own_blocks(lambda jl: own_in(jl).start())
    sent_blocks(i0, middle, lambda i: b_copy(i).start())

    def own_turn(jl):
        own_in(jl).wait()
        own_out(jl).start()

    own_blocks(own_turn)

    first_own.wait()
    for k in range(1, C):
        first_wait(k)

    def second(k):
        to = lax.rem(r + k, R)
        return remote(s2.at[to], r2.at[pl.ds(r * cap2, cap2)], p2_send.at[k], p2_recv.at[r], to, c)

    def second_wait(k):
        src = lax.rem(r + k, R)
        remote(s2.at[0], r2.at[pl.ds(src * cap2, cap2)], p2_send.at[0], p2_recv.at[src], r, c).wait_recv()

    UNROLL = 8

    def pack2(k):
        to = lax.rem(r + k, R)

        def run(n):
            for u in range(UNROLL):
                s2[to, n * UNROLL + u] = r1[index2[to * cap2 + n * UNROLL + u]]

        over(0, cap2 // UNROLL, run)

    for k in range(1, R):
        pack2(k)
        if k > 1:
            second(k - 1).start()

    def pack2_own(n):
        for u in range(UNROLL):
            r2[r * cap2 + n * UNROLL + u] = r1[index2[r * cap2 + n * UNROLL + u]]

    over(0, cap2 // UNROLL, pack2_own)
    second(R - 1).start()
    sent_blocks(middle, NB, lambda i: b_copy(i).start())

    for k in range(1, R):
        second_wait(k)

    def third(k):
        to = lax.rem(c + k, C)
        return remote(s3.at[to], out.at[c], p3_send.at[k], p3_recv.at[c], r, to)

    def third_wait(k):
        src = lax.rem(c + k, C)
        remote(s3.at[0], out.at[src], p3_send.at[0], p3_recv.at[src], r, c).wait_recv()

    third_own = pltpu.make_async_copy(s3.at[c], out.at[c], p3_recv.at[c])

    def pack3(k):
        to = lax.rem(c + k, C)

        def run(n):
            for u in range(UNROLL):
                s3[to, n * UNROLL + u] = r2[index3[to * cap3 + n * UNROLL + u]]

        over(0, cap3 // UNROLL, run)

    for k in range(1, C):
        pack3(k)
        if k > 1:
            third(k - 1).start()
    pack3(C)
    third(C - 1).start()

    own_blocks(lambda jl: own_out(jl).wait())
    for s in range(R):
        begin = start_of(s * C + c)

        def run(jl):
            @pl.when((r != s) & (jl * R + r >= begin))
            def _():
                remote(col.at[0], grid.at[jl, s], b_send.at[0], b_recv.at[jl, s], r, c).wait_recv()

        over(0, C, run)
    third_own.start()
    sent_blocks(i0, NB, lambda i: b_copy(i).wait_send())
    for k in range(1, C):
        first(k).wait_send()
    for k in range(1, R):
        second(k).wait_send()
    for k in range(1, C):
        third_wait(k)
    for k in range(1, C):
        third(k).wait_send()
    third_own.wait()


def spread(R, C, cap2, cap3, placed, index2, index3, front):
    hbm = pl.BlockSpec(memory_space=pltpu.HBM)
    smem = pl.BlockSpec(memory_space=pltpu.SMEM)
    dma = pltpu.SemaphoreType.DMA
    T, sub = placed.shape[1], placed.shape[2]
    return pl.pallas_call(
        functools.partial(spread_kernel, R, C, cap2, cap3),
        in_specs=[hbm, smem, smem, hbm],
        out_specs=[hbm, hbm],
        out_shape=[
            jax.ShapeDtypeStruct((C, R, EDGE, EDGE), F32),
            jax.ShapeDtypeStruct((C, cap3, sub, EDGE), F32),
        ],
        scratch_shapes=[
            pltpu.VMEM((C * T, sub, EDGE), F32),
            pltpu.VMEM((R, cap2, sub, EDGE), F32),
            pltpu.VMEM((R * cap2, sub, EDGE), F32),
            pltpu.VMEM((C, cap3, sub, EDGE), F32),
            pltpu.VMEM((C, EDGE, EDGE), F32),
            dma((C,)), dma((C,)), dma((R * C,)), dma((C, R)),
            dma((C,)), dma((C,)), dma((R,)), dma((R,)), dma((C,)), dma((C,)),
        ],
        compiler_params=pltpu.CompilerParams(
            collective_id=0, has_side_effects=True, vmem_limit_bytes=40 << 20
        ),
        name="spread",
    )(placed, index2, index3, front)


def slab_kernel(C, landing, grid, arrived, out, tile, sem):
    out[...] = grid[:, 0]
    slots = arrived.shape[1]

    def run(k):
        @pl.when(landing[1 + slots + k] == 0)
        def _():
            copy = pltpu.make_async_copy(arrived.at[:, k], tile, sem)
            copy.start()
            copy.wait()
            jl = landing[1 + k]
            out[jl] = out[jl] + tile[...].reshape(EDGE, EDGE)

    @pl.when(landing[0] < 2)
    def _():
        over(0, slots, run)


def slab_of(C, landing, grid, arrived):
    return pl.pallas_call(
        functools.partial(slab_kernel, C),
        grid=(1,),
        in_specs=[
            pl.BlockSpec(memory_space=pltpu.SMEM),
            pl.BlockSpec((C, 1, EDGE, EDGE), lambda t: (0, 0, 0, 0)),
            pl.BlockSpec(memory_space=pltpu.HBM),
        ],
        out_specs=pl.BlockSpec((C, EDGE, EDGE), lambda t: (0, 0, 0)),
        out_shape=jax.ShapeDtypeStruct((C, EDGE, EDGE), F32),
        scratch_shapes=[pltpu.VMEM((arrived.shape[0], EDGE // C, EDGE), F32), pltpu.SemaphoreType.DMA],
        name="slab",
    )(landing, grid, arrived)


STEP = 8


def factor(work, upper):
    rows8 = lax.broadcasted_iota(jnp.int32, (STEP, 1), 0)
    lanes = lax.broadcasted_iota(jnp.int32, (STEP, EDGE), 1)

    def block(b, _):
        first = pl.multiple_of(b * STEP, STEP)
        x = work[pl.ds(first, STEP), :]
        d = pltpu.roll(x[:, :EDGE], lax.rem(EDGE - first, EDGE), 1)
        for t in range(STEP):
            pivot = d[t : t + 1, t : t + 1]
            scale = lax.rsqrt(pivot)
            ratio = d[:, t : t + 1] / pivot
            ratio = jnp.where(rows8 > t, ratio, jnp.where(rows8 == t, 1.0 - scale, 0.0))
            x = x - ratio * x[t : t + 1, :]
            d = d - ratio * d[t : t + 1, :]
        upper[pl.ds(first, STEP), :] = x
        left = jnp.where(lanes >= first + STEP, x[:, :EDGE], 0.0)
        work[...] = work[...] - dot(left, x, TN)
        return 0

    lax.fori_loop(0, EDGE // STEP, block, 0)


def panel_kernel(
    R, C, slab, qrow, qcol,
    diag, rawrow, zbuf, rawcol, work, upper, low,
    dr_send, dr_recv, dx_send, dx_recv, dy_send, dy_recv, sc_send, ck_recv,
    ag_send, ag_recv, z_send, z_recv, v_send, v_recv, q_sem,
):
    r = lax.axis_index("row")
    c = lax.axis_index("col")
    X = math.isqrt(C)
    x, y = lax.rem(c, X), c // X
    ratio = C // R
    greet(R, C, r, c)

    owners = ((0, 0, 0), (1, 0, 1), (1, 1, 2))
    lines = ((0, 0, 2), (1, 2, 1))

    def diag_row(k, p):
        rr, cc, at = owners[p]
        return remote(slab.at[0], diag.at[at], dr_send.at[k], dr_recv.at[at], lax.rem(r + k, R), c)

    def diag_own(p):
        return pltpu.make_async_copy(slab.at[0], diag.at[owners[p][2]], dr_recv.at[owners[p][2]])

    for p in range(3):

        @pl.when((r == owners[p][0]) & (c == owners[p][1]))
        def _():
            for k in range(1, R):
                diag_row(k, p).start()
            diag_own(p).start()

    def scatter(jl, k):
        return remote(slab.at[jl], rawrow.at[k, jl], sc_send.at[jl], ck_recv.at[k], r, jl)

    def scatter_own(jl, k):
        return pltpu.make_async_copy(slab.at[jl], rawrow.at[k, jl], ck_recv.at[k])

    for k in range(2):

        @pl.when(c == k)
        def _():
            for jl in range(C):
                if jl == k:
                    scatter_own(jl, k).start()
                else:
                    scatter(jl, k).start()

    def diag_x(k, p):
        _, at, n = lines[p]
        here = diag.at[pl.ds(at, n)]
        return remote(here, here, dx_send.at[k], dx_recv.at[p], r, lax.rem(x + k, X))

    for p in range(2):
        owner, at, n = lines[p]

        @pl.when(c == owner)
        def _():
            for u in range(n):
                diag_own(at + u).wait()
            for k in range(1, X):
                diag_x(k, p).start()

    def diag_y(k):
        return remote(diag, diag, dy_send.at[k], dy_recv.at[0], r, k * X + x)

    @pl.when(y == 0)
    def _():
        for p in range(2):

            @pl.when(c != lines[p][0])
            def _():
                _, at, n = lines[p]
                here = diag.at[pl.ds(at, n)]
                remote(here, here, dx_send.at[0], dx_recv.at[p], r, c).wait_recv()

        for k in range(1, X):
            diag_y(k).start()

    for k in range(2):
        pltpu.make_async_copy(slab.at[0], rawrow.at[k, c], ck_recv.at[k]).wait()

    def gather(k, n):
        here = rawrow.at[n, c]
        return remote(here, here, ag_send.at[n, k], ag_recv.at[n, c], r, lax.rem(c + k, C))

    def along(k, n):
        return remote(
            rawrow.at[n, c], zbuf.at[n, r], z_send.at[n, k], z_recv.at[n, r], lax.rem(r + k, R), c
        )

    for k in range(1, R):
        for n in range(2):
            along(k, n).start()
    for k in range(1, C):
        for n in range(2):
            gather(k, n).start()

    mine = lax.rem(c, ratio) * R
    place = c // ratio

    def serve(p, n):
        return remote(
            zbuf.at[n, p], rawcol.at[n, place], v_send.at[n, p], v_recv.at[n, place], r, mine + p
        )

    def serve_own(p, n):
        return pltpu.make_async_copy(zbuf.at[n, p], rawcol.at[n, place], v_recv.at[n, place])

    own_z = [pltpu.make_async_copy(rawrow.at[n, c], zbuf.at[n, r], z_recv.at[n, r]) for n in range(2)]
    for copy in own_z:
        copy.start()
    for copy in own_z:
        copy.wait()

    def pass_on(p):
        for n in range(2):

            @pl.when(p != r)
            def _():
                remote(rawrow.at[n, 0], zbuf.at[n, p], z_send.at[n, 0], z_recv.at[n, p], r, c).wait_recv()

            @pl.when(mine + p == c)
            def _():
                serve_own(p, n).start()

            @pl.when(mine + p != c)
            def _():
                serve(p, n).start()

    over(0, R, pass_on)

    @pl.when(y != 0)
    def _():
        remote(diag, diag, dy_send.at[0], dy_recv.at[0], r, c).wait_recv()

    rows = lax.broadcasted_iota(jnp.int32, (EDGE, EDGE), 0)
    cols = lax.broadcasted_iota(jnp.int32, (EDGE, EDGE), 1)
    eye = (rows == cols).astype(F32)

    def pivot(block, at):
        work[:, :EDGE] = jnp.where(rows >= cols, block, block.T)
        work[:, EDGE:] = eye
        factor(work, upper)
        low[at] = jnp.where(rows >= cols, upper[:, :EDGE].T, 0.0)
        low[at + 1] = jnp.where(rows >= cols, upper[:, EDGE:], 0.0)

    pivot(diag[0], 0)
    low[2] = dot(diag[1], low[1], NT)
    pivot(diag[2] - dot(low[2], low[2], NT), 3)

    def solve(raw, at, count):
        a0 = raw[0, pl.ds(at, count)].reshape(count * EDGE, EDGE)
        a1 = raw[1, pl.ds(at, count)].reshape(count * EDGE, EDGE)
        q0 = dot(a0, low[1], NT)
        q1 = dot(a1 - dot(q0, low[2], NT), low[4], NT)
        raw[0, pl.ds(at, count)] = q0.reshape(count, EDGE, EDGE)
        raw[1, pl.ds(at, count)] = q1.reshape(count, EDGE, EDGE)

    def col_wait(s):
        for n in range(2):
            pltpu.make_async_copy(zbuf.at[n, 0], rawcol.at[n, s], v_recv.at[n, s]).wait()

    over(0, R, col_wait)
    many = min(4, R)
    over(0, R // many, lambda g: solve(rawcol, g * many, many))
    keep_col = pltpu.make_async_copy(rawcol, qcol, q_sem.at[0])
    keep_col.start()

    def row_wait(jl):
        @pl.when(jl != c)
        def _():
            for n in range(2):
                here = rawrow.at[n, jl]
                remote(here, here, ag_send.at[n, 0], ag_recv.at[n, jl], r, c).wait_recv()

    over(0, C, row_wait)
    for k in range(1, C):
        for n in range(2):
            gather(k, n).wait_send()
    for k in range(1, R):
        for n in range(2):
            along(k, n).wait_send()

    over(0, C // many, lambda g: solve(rawrow, g * many, many))

    @pl.when(r == 0)
    def _():
        rawrow[0, 0] = low[0]
        rawrow[1, 0] = jnp.zeros((EDGE, EDGE), F32)

    @pl.when(r == 1)
    def _():
        rawrow[0, 0] = low[2]
        rawrow[1, 0] = low[3]

    keep_row = pltpu.make_async_copy(rawrow, qrow, q_sem.at[1])
    keep_row.start()

    for p in range(3):

        @pl.when((r == owners[p][0]) & (c == owners[p][1]))
        def _():
            for k in range(1, R):
                diag_row(k, p).wait_send()

    for k in range(2):

        @pl.when(c == k)
        def _():
            for jl in range(C):
                if jl != k:
                    scatter(jl, k).wait_send()

            for s in range(1, X):
                diag_x(s, k).wait_send()

    @pl.when(y == 0)
    def _():
        for k in range(1, X):
            diag_y(k).wait_send()

    def served(p):
        @pl.when(mine + p != c)
        def _():
            for n in range(2):
                serve(p, n).wait_send()

    over(0, R, served)
    keep_col.wait()
    keep_row.wait()


def panels(R, C, slab):
    hbm = pl.BlockSpec(memory_space=pltpu.HBM)
    dma = pltpu.SemaphoreType.DMA
    X = math.isqrt(C)
    return pl.pallas_call(
        functools.partial(panel_kernel, R, C),
        in_specs=[hbm],
        out_specs=[hbm, hbm],
        out_shape=[
            jax.ShapeDtypeStruct((2, C, EDGE, EDGE), F32),
            jax.ShapeDtypeStruct((2, R, EDGE, EDGE), F32),
        ],
        scratch_shapes=[
            pltpu.VMEM((3, EDGE, EDGE), F32),
            pltpu.VMEM((2, C, EDGE, EDGE), F32),
            pltpu.VMEM((2, R, EDGE, EDGE), F32),
            pltpu.VMEM((2, R, EDGE, EDGE), F32),
            pltpu.VMEM((EDGE, 2 * EDGE), F32),
            pltpu.VMEM((EDGE, 2 * EDGE), F32),
            pltpu.VMEM((5, EDGE, EDGE), F32),
            dma((R,)), dma((3,)), dma((X,)), dma((2,)), dma((X,)), dma((1,)), dma((C,)), dma((2,)),
            dma((2, C)), dma((2, C)), dma((2, R)), dma((2, R)), dma((2, R)), dma((2, R)), dma((2,)),
        ],
        compiler_params=pltpu.CompilerParams(
            collective_id=1, has_side_effects=True, vmem_limit_bytes=40 << 20
        ),
        name="panels",
    )(slab)


def halves(x):
    high = x.astype(BF16)
    return high, (x - high.astype(F32)).astype(BF16)


def update_kernel(R, C, place, landing, grid, qrow, qcol, arrived, out, wide, head, follow):
    jl = pl.program_id(0)
    slots = arrived.shape[1]
    r, c = place[0], place[1]
    i = jl * R + r
    rows = lax.broadcasted_iota(jnp.int32, (EDGE, EDGE), 0)
    cols = lax.broadcasted_iota(jnp.int32, (EDGE, EDGE), 1)

    @pl.when(jl == 0)
    def _():
        def clear(k):
            head[k] = -1

        over(0, C, clear)

        def link(k):
            @pl.when(landing[1 + slots + k] >= 0)
            def _():
                where = landing[1 + k]
                follow[k] = head[where]
                head[where] = k

        over(0, slots, link)

        def split(s):
            for n in range(2):
                high, low = halves(qcol[n, s])
                for m, part in ((0, high), (2, low), (4, high)):
                    wide[s, :, (m + n) * EDGE : (m + n + 1) * EDGE] = part

        over(0, R, split)

    first, second = halves(qrow[0, 0]), halves(qrow[1, 0])
    left = jnp.concatenate([first[0], second[0], first[0], second[0], first[1], second[1]], axis=1)
    for s in range(R):
        j = s * C + c

        @pl.when(i < j)
        def _():
            out[0, s] = jnp.zeros((EDGE, EDGE), F32)

        @pl.when((i >= j) & (j < 2))
        def _():
            out[0, s] = jnp.where(j == 0, qrow[0, 0], qrow[1, 0])

        @pl.when((i >= j) & (j >= 2))
        def _():
            out[0, s] = grid[0, s] - dot16(left, wide[s], NT)

    def more(k):
        return k >= 0

    def add(k):
        s = landing[1 + slots + k]

        @pl.when(s * C + c >= 2)
        def _():
            out[0, s] = out[0, s] + arrived[:, k].reshape(EDGE, EDGE)

        return follow[k]

    lax.while_loop(more, add, head[jl])
    for s in range(R):

        @pl.when((i == s * C + c) & (i >= 2))
        def _():
            out[0, s] = jnp.where(rows >= cols, out[0, s], 0.0)


def update(R, C, place, landing, grid, qrow, qcol, arrived):
    cap3 = arrived.shape[1]
    block = pl.BlockSpec((1, R, EDGE, EDGE), lambda jl, *_: (jl, 0, 0, 0))
    return pl.pallas_call(
        functools.partial(update_kernel, R, C),
        grid_spec=pltpu.PrefetchScalarGridSpec(
            num_scalar_prefetch=2,
            grid=(C,),
            in_specs=[
                block,
                pl.BlockSpec((2, 1, EDGE, EDGE), lambda jl, *_: (0, jl, 0, 0)),
                pl.BlockSpec((2, R, EDGE, EDGE), lambda jl, *_: (0, 0, 0, 0)),
                pl.BlockSpec(
                    arrived.shape, lambda jl, *_: (0, 0, 0, 0),
                    pipeline_mode=pl.Buffered(1),
                ),
            ],
            out_specs=block,
            scratch_shapes=[
                pltpu.VMEM((R, EDGE, 6 * EDGE), BF16),
                pltpu.SMEM((C,), jnp.int32),
                pltpu.SMEM((cap3,), jnp.int32),
            ],
        ),
        out_shape=jax.ShapeDtypeStruct((C, R, EDGE, EDGE), F32),
        compiler_params=pltpu.CompilerParams(vmem_limit_bytes=40 << 20),
        name="update",
    )(place, landing, grid, qrow, qcol, arrived)


def capacities(R, C, T):
    if T < 32:
        return 8, 8
    return 104, 112


def hot(values, count):
    return (values[..., None] == jnp.arange(count, dtype=jnp.int32)).astype(BF16)


def before(marks):
    n = marks.shape[-2]
    serial = jnp.arange(n, dtype=jnp.int32)
    lower = (serial[:, None] > serial[None, :]).astype(BF16)
    return jnp.einsum("pq,...qk->...pk", lower, marks, preferred_element_type=F32)


def local(front_entries, child_updates, row_maps, col_maps, target_columns, row_offsets):
    R = lax.axis_size("row")
    C = lax.axis_size("col")
    count = R * C
    T = child_updates.shape[0]
    cap2, cap3 = capacities(R, C, T)
    my_row = lax.axis_index("row").astype(jnp.int32)
    my_col = lax.axis_index("col").astype(jnp.int32)

    told = jnp.concatenate([target_columns[:, 0], row_offsets[:, 0]])
    told = lax.all_to_all(
        jnp.broadcast_to(told, (count, 2 * T)), ("row", "col"), split_axis=0, concat_axis=0, tiled=True
    )
    columns, offsets = told[:, :T], told[:, T:]
    target_rows = columns + offsets % (count - columns)
    columns = columns.reshape(R, C * T)
    target_rows = target_rows.reshape(R, C * T)
    to_row, to_col = target_rows % R, columns % C

    row_hot = hot(to_row, R)
    rank2 = jnp.sum(before(row_hot) * row_hot.astype(F32), axis=-1).astype(jnp.int32)
    mine = to_row == my_row
    col_hot = hot(jnp.where(mine, to_col, -1), C)
    inside = before(col_hot)
    totals = jnp.sum(col_hot.astype(F32), axis=1)
    planes = jnp.arange(R, dtype=jnp.int32)
    ahead = jnp.sum(jnp.where((planes[:, None] > planes[None, :])[..., None], totals[None], 0.0), axis=1)
    rank3 = jnp.sum((inside + ahead[:, None, :]) * col_hot.astype(F32), axis=-1).astype(jnp.int32)
    loads2 = jnp.sum(row_hot.astype(F32), axis=1)
    loads3 = jnp.einsum("pqk,pql->kl", row_hot, hot(to_col, C), preferred_element_type=F32)
    passes2 = (jnp.max(loads2).astype(jnp.int32) + cap2 - 1) // cap2
    passes3 = (jnp.max(loads3).astype(jnp.int32) + cap3 - 1) // cap3

    def tables(a, b):
        own_hot = lax.dynamic_index_in_dim(row_hot, my_row, 0, keepdims=False)
        own_rank = lax.dynamic_index_in_dim(rank2, my_row, 0, keepdims=False)
        serial = jnp.arange(C * T, dtype=jnp.int32)
        values = jnp.stack([serial // T, serial % T], axis=0).astype(BF16)
        marked = values[:, :, None] * own_hot[None]
        found = jnp.einsum("vqk,qn->vkn", marked, hot(own_rank - a * cap2, cap2), preferred_element_type=F32)
        found = found.astype(jnp.int32)
        index2 = (found[0] * T + found[1]).reshape(-1)
        place2 = rank2 - a * cap2
        active = (place2 >= 0) & (place2 < cap2) & mine
        source = jnp.broadcast_to(planes[:, None], (R, C * T))
        values = jnp.stack(
            [source, place2, target_rows // R, columns // C, jnp.ones_like(source)], axis=0
        )
        values = jnp.where(active, values, 0).astype(BF16)
        marked = values[..., None] * col_hot[None]
        found = jnp.einsum(
            "vpqk,pqn->vkn", marked, hot(rank3 - b * cap3, cap3), preferred_element_type=F32
        ).astype(jnp.int32)
        index3 = (found[0] * cap2 + found[1]).reshape(-1)
        here = lax.dynamic_index_in_dim(found, my_col, 1, keepdims=False)
        return index2, index3, here[2], here[3], here[4]

    index2, index3, land_row, land_col, valid = tables(0, 0)
    placed = place_tiles(C, child_updates, row_maps, col_maps)
    grid, arrived = spread(
        R, C, cap2, cap3, placed, index2, index3, front_entries.reshape(count, EDGE, EDGE)
    )

    def another(carry):
        p, grid = carry
        index2, index3, land_row, land_col, valid = tables(p // passes3, p % passes3)
        held = lax.all_to_all(placed, "col", split_axis=0, concat_axis=0, tiled=True)
        held = held.reshape((C * T, EDGE // C, EDGE))[index2].reshape(R, cap2, EDGE // C, EDGE)
        held = lax.all_to_all(held, "row", split_axis=0, concat_axis=0, tiled=True)
        held = held.reshape((R * cap2, EDGE // C, EDGE))[index3].reshape(C, cap3, EDGE // C, EDGE)
        held = lax.all_to_all(held, "col", split_axis=0, concat_axis=0, tiled=True)
        tiles = held.transpose(1, 0, 2, 3).reshape(cap3, EDGE, EDGE)
        tiles = jnp.where((valid > 0)[:, None, None], tiles, 0.0)
        return p + 1, grid.at[land_row, land_col].add(tiles)

    _, grid = lax.while_loop(lambda carry: carry[0] < passes2 * passes3, another, (jnp.int32(1), grid))

    landing = jnp.concatenate([my_col[None], land_row, jnp.where(valid > 0, land_col, -1)])
    slab = slab_of(C, landing, grid, arrived)
    qrow, qcol = panels(R, C, slab)
    place = jnp.stack([my_row, my_col])
    result = update(R, C, place, landing, grid, qrow, qcol, arrived)
    return result.reshape(C, 1, R, 1, EDGE, EDGE)


def solution(mesh):
    return jax.shard_map(
        local,
        mesh=mesh,
        in_specs=(
            P(None, ("row", "col")),
            P(("row", "col"), None, None),
            P(("row", "col"), None),
            P(("row", "col"), None),
            P(("row", "col"), None),
            P(("row", "col"), None),
        ),
        out_specs=P(None, "row", None, "col", None, None),
        check_vma=False,
    )
```

```python
import functools
import math

import jax
import jax.numpy as jnp
from jax import lax
from jax.experimental import pallas as pl
from jax.experimental.pallas import tpu as pltpu
from jax.sharding import PartitionSpec as P

EDGE = 128
MESH = pl.DeviceIdType.MESH
PRECISE = lax.Precision.HIGHEST
F32 = jnp.float32
BF16 = jnp.bfloat16
NN = ((1,), (0,))
NT = ((1,), (1,))
TN = ((0,), (0,))


def dot(a, b, dims):
    return lax.dot_general(a, b, (dims, ((), ())), precision=PRECISE, preferred_element_type=F32)


def dot16(a, b, dims):
    return lax.dot_general(a, b, (dims, ((), ())), preferred_element_type=F32)


def remote(src, dst, ss, rs, rr, cc):
    return pltpu.make_async_remote_copy(
        src_ref=src, dst_ref=dst, send_sem=ss, recv_sem=rs, device_id=(rr, cc), device_id_type=MESH
    )


def over(low, high, body):
    def run(i, _):
        body(i)
        return 0

    lax.fori_loop(low, high, run, 0)


def greet(R, C, r, c):
    barrier = pltpu.get_barrier_semaphore()
    for k in range(1, R):
        pl.semaphore_signal(barrier, inc=1, device_id=(lax.rem(r + k, R), c), device_id_type=MESH)
    for k in range(1, C):
        pl.semaphore_signal(barrier, inc=1, device_id=(r, lax.rem(c + k, C)), device_id_type=MESH)
    pl.semaphore_wait(barrier, R + C - 2)


GROUP = 4


def place_kernel(C, tile, row_map, col_map, out):
    t = pl.program_id(0)
    levels = lax.broadcasted_iota(jnp.int32, (EDGE, EDGE), 0)
    for g in range(GROUP):
        k = t * GROUP + g
        col_hot = (levels == col_map[pl.ds(k, 1), :]).astype(F32).astype(BF16)
        row_hot = (levels == row_map[pl.ds(k, 1), :]).astype(F32).astype(BF16)
        x = tile[g]
        first = x.astype(BF16)
        rest = x - first.astype(F32)
        second = rest.astype(BF16)
        third = (rest - second.astype(F32)).astype(BF16)
        parts = [dot16(p, col_hot, NT).astype(BF16) for p in (first, second, third)]
        placed = (
            dot16(row_hot, parts[0], NN) + dot16(row_hot, parts[1], NN)
        ) + dot16(row_hot, parts[2], NN)
        for q in range(C):
            out[q, g] = placed[q * (EDGE // C) : (q + 1) * (EDGE // C), :]


def place_tiles(C, tiles, row_map, col_map):
    count = tiles.shape[0]
    whole = pl.BlockSpec((count, EDGE), lambda t: (0, 0))
    return pl.pallas_call(
        functools.partial(place_kernel, C),
        grid=(count // GROUP,),
        in_specs=[pl.BlockSpec((GROUP, EDGE, EDGE), lambda t: (t, 0, 0)), whole, whole],
        out_specs=pl.BlockSpec((C, GROUP, EDGE // C, EDGE), lambda t: (0, t, 0, 0)),
        out_shape=jax.ShapeDtypeStruct((C, count, EDGE // C, EDGE), F32),
        name="place",
    )(tiles, row_map, col_map)


PARTS = 4
PACK = 4


def spread_kernel(
    R, C, cap2, cap3, placed, index2, index3, col, grid, out,
    r1, s2, r2, s3, stage,
    st_in, st_out, b_send, b_recv, p1_send, p1_recv, p2_send, p2_recv, p3_send, p3_recv,
):
    r = lax.axis_index("row")
    c = lax.axis_index("col")
    NB = R * C
    T = placed.shape[1]
    start_of = lambda column: jnp.where(column < 2, 0, column)
    i0 = start_of(r * C + c)
    greet(R, C, r, c)

    part1 = T // PARTS

    def first(k, h):
        to = lax.rem(c + k, C)
        return remote(
            placed.at[to, pl.ds(h * part1, part1)], r1.at[pl.ds(c * T + h * part1, part1)],
            p1_send.at[k, h], p1_recv.at[c, h], r, to,
        )

    def first_wait(k, h):
        src = lax.rem(c + k, C)
        remote(
            placed.at[0, pl.ds(0, part1)], r1.at[pl.ds(src * T + h * part1, part1)],
            p1_send.at[0, h], p1_recv.at[src, h], r, c,
        ).wait_recv()

    first_own = pltpu.make_async_copy(placed.at[c], r1.at[pl.ds(c * T, T)], p1_recv.at[c, 0])
    first_own.start()
    for h in range(PARTS):
        for k in range(1, C):
            first(k, h).start()

    def b_copy(i):
        return remote(
            col.at[i], grid.at[i // R, r], b_send.at[i], b_recv.at[i // R, r], lax.rem(i, R), c
        )

    def own_in(jl):
        return pltpu.make_async_copy(col.at[jl * R + r], stage.at[jl], st_in.at[jl])

    def own_out(jl):
        return pltpu.make_async_copy(stage.at[jl], grid.at[jl, r], st_out.at[jl])

    def own_blocks(body):
        def run(jl):
            @pl.when(jl * R + r >= i0)
            def _():
                body(jl)

        over(0, C, run)

    def sent_blocks(low, high, body):
        def run(i):
            @pl.when(lax.rem(i, R) != r)
            def _():
                body(i)

        over(low, high, run)

    middle = i0 + (NB - i0) // 4
    own_blocks(lambda jl: own_in(jl).start())
    sent_blocks(i0, middle, lambda i: b_copy(i).start())

    def own_turn(jl):
        own_in(jl).wait()
        own_out(jl).start()

    own_blocks(own_turn)

    first_own.wait()
    for h in range(PARTS):
        for k in range(1, C):
            first_wait(k, h)

    def second(k):
        to = lax.rem(r + k, R)
        return remote(s2.at[to], r2.at[pl.ds(r * cap2, cap2)], p2_send.at[k], p2_recv.at[r], to, c)

    def second_wait(k):
        src = lax.rem(r + k, R)
        remote(s2.at[0], r2.at[pl.ds(src * cap2, cap2)], p2_send.at[0], p2_recv.at[src], r, c).wait_recv()

    def pack2(k):
        to = lax.rem(r + k, R)

        def run(n):
            for u in range(PACK):
                s2[to, n * PACK + u] = r1[index2[to * cap2 + n * PACK + u]]

        over(0, cap2 // PACK, run)

    for k in range(1, R):
        pack2(k)
        if k > 1:
            second(k - 1).start()

    def pack2_own(n):
        for u in range(PACK):
            r2[r * cap2 + n * PACK + u] = r1[index2[r * cap2 + n * PACK + u]]

    over(0, cap2 // PACK, pack2_own)
    second(R - 1).start()
    sent_blocks(middle, NB, lambda i: b_copy(i).start())

    for k in range(1, R):
        second_wait(k)

    part3 = cap3 // PARTS

    def third(k, h):
        to = lax.rem(c + k, C)
        at = pl.ds(h * part3, part3)
        return remote(s3.at[to, at], out.at[c, at], p3_send.at[k, h], p3_recv.at[c, h], r, to)

    def third_wait(k, h):
        src = lax.rem(c + k, C)
        at = pl.ds(h * part3, part3)
        remote(s3.at[0, at], out.at[src, at], p3_send.at[0, h], p3_recv.at[src, h], r, c).wait_recv()

    third_own = pltpu.make_async_copy(s3.at[c], out.at[c], p3_recv.at[c, 0])

    def pack3(k, h):
        to = lax.rem(c + k, C)

        def run(n):
            for u in range(PACK):
                at = h * part3 + n * PACK + u
                s3[to, at] = r2[index3[to * cap3 + at]]

        over(0, part3 // PACK, run)

    def third_part(h):
        def step(k):
            pack3(k, h)

            @pl.when(k > 1)
            def _():
                third(k - 1, h).start()

        over(1, C, step)
        pack3(C, h)
        third(C - 1, h).start()

    over(0, PARTS, third_part)

    own_blocks(lambda jl: own_out(jl).wait())
    for s in range(R):
        begin = start_of(s * C + c)

        def run(jl):
            @pl.when((r != s) & (jl * R + r >= begin))
            def _():
                remote(col.at[0], grid.at[jl, s], b_send.at[0], b_recv.at[jl, s], r, c).wait_recv()

        over(0, C, run)
    third_own.start()
    sent_blocks(i0, NB, lambda i: b_copy(i).wait_send())
    for h in range(PARTS):
        for k in range(1, C):
            first(k, h).wait_send()
    for k in range(1, R):
        second(k).wait_send()
    for h in range(PARTS):
        for k in range(1, C):
            third_wait(k, h)
        for k in range(1, C):
            third(k, h).wait_send()
    third_own.wait()


def spread(R, C, cap2, cap3, placed, index2, index3, front):
    hbm = pl.BlockSpec(memory_space=pltpu.HBM)
    smem = pl.BlockSpec(memory_space=pltpu.SMEM)
    dma = pltpu.SemaphoreType.DMA
    T, sub = placed.shape[1], placed.shape[2]
    return pl.pallas_call(
        functools.partial(spread_kernel, R, C, cap2, cap3),
        in_specs=[hbm, smem, smem, hbm],
        out_specs=[hbm, hbm],
        out_shape=[
            jax.ShapeDtypeStruct((C, R, EDGE, EDGE), F32),
            jax.ShapeDtypeStruct((C, cap3, sub, EDGE), F32),
        ],
        scratch_shapes=[
            pltpu.VMEM((C * T, sub, EDGE), F32),
            pltpu.VMEM((R, cap2, sub, EDGE), F32),
            pltpu.VMEM((R * cap2, sub, EDGE), F32),
            pltpu.VMEM((C, cap3, sub, EDGE), F32),
            pltpu.VMEM((C, EDGE, EDGE), F32),
            dma((C,)), dma((C,)), dma((R * C,)), dma((C, R)),
            dma((C, PARTS)), dma((C, PARTS)), dma((R,)), dma((R,)), dma((C, PARTS)), dma((C, PARTS)),
        ],
        compiler_params=pltpu.CompilerParams(
            collective_id=0, has_side_effects=True, vmem_limit_bytes=60 << 20
        ),
        name="spread",
    )(placed, index2, index3, front)


def slab_kernel(C, landing, grid, arrived, out, tile, sem):
    out[...] = grid[:, 0]
    slots = arrived.shape[1]

    def run(k):
        @pl.when(landing[1 + slots + k] == 0)
        def _():
            copy = pltpu.make_async_copy(arrived.at[:, k], tile, sem)
            copy.start()
            copy.wait()
            jl = landing[1 + k]
            out[jl] = out[jl] + tile[...].reshape(EDGE, EDGE)

    @pl.when(landing[0] < 2)
    def _():
        over(0, slots, run)


def slab_of(C, landing, grid, arrived):
    return pl.pallas_call(
        functools.partial(slab_kernel, C),
        grid=(1,),
        in_specs=[
            pl.BlockSpec(memory_space=pltpu.SMEM),
            pl.BlockSpec((C, 1, EDGE, EDGE), lambda t: (0, 0, 0, 0)),
            pl.BlockSpec(memory_space=pltpu.HBM),
        ],
        out_specs=pl.BlockSpec((C, EDGE, EDGE), lambda t: (0, 0, 0)),
        out_shape=jax.ShapeDtypeStruct((C, EDGE, EDGE), F32),
        scratch_shapes=[pltpu.VMEM((arrived.shape[0], EDGE // C, EDGE), F32), pltpu.SemaphoreType.DMA],
        compiler_params=pltpu.CompilerParams(vmem_limit_bytes=60 << 20),
        name="slab",
    )(landing, grid, arrived)


STEP = 8


def factor(work, upper):
    rows8 = lax.broadcasted_iota(jnp.int32, (STEP, 1), 0)
    lanes = lax.broadcasted_iota(jnp.int32, (STEP, EDGE), 1)

    def block(b, _):
        first = pl.multiple_of(b * STEP, STEP)
        x = work[pl.ds(first, STEP), :]
        d = pltpu.roll(x[:, :EDGE], lax.rem(EDGE - first, EDGE), 1)
        for t in range(STEP):
            pivot = d[t : t + 1, t : t + 1]
            scale = lax.rsqrt(pivot)
            ratio = d[:, t : t + 1] / pivot
            ratio = jnp.where(rows8 > t, ratio, jnp.where(rows8 == t, 1.0 - scale, 0.0))
            x = x - ratio * x[t : t + 1, :]
            d = d - ratio * d[t : t + 1, :]
        upper[pl.ds(first, STEP), :] = x
        left = jnp.where(lanes >= first + STEP, x[:, :EDGE], 0.0)
        work[...] = work[...] - dot(left, x, TN)
        return 0

    lax.fori_loop(0, EDGE // STEP, block, 0)


def panel_kernel(
    R, C, slab, qrow, qcol,
    diag, rawrow, zbuf, rawcol, work, upper, low,
    dr_send, dr_recv, dx_send, dx_recv, dy_send, dy_recv, sc_send, ck_recv,
    ag_send, ag_recv, z_send, z_recv, v_send, v_recv, q_sem,
):
    r = lax.axis_index("row")
    c = lax.axis_index("col")
    X = math.isqrt(C)
    x, y = lax.rem(c, X), c // X
    ratio = C // R
    greet(R, C, r, c)

    owners = ((0, 0, 0), (1, 0, 1), (1, 1, 2))
    lines = ((0, 0, 2), (1, 2, 1))

    def diag_row(k, p):
        rr, cc, at = owners[p]
        return remote(slab.at[0], diag.at[at], dr_send.at[k], dr_recv.at[at], lax.rem(r + k, R), c)

    def diag_own(p):
        return pltpu.make_async_copy(slab.at[0], diag.at[owners[p][2]], dr_recv.at[owners[p][2]])

    for p in range(3):

        @pl.when((r == owners[p][0]) & (c == owners[p][1]))
        def _():
            for k in range(1, R):
                diag_row(k, p).start()
            diag_own(p).start()

    def scatter(jl, k):
        return remote(slab.at[jl], rawrow.at[k, jl], sc_send.at[jl], ck_recv.at[k], r, jl)

    def scatter_own(jl, k):
        return pltpu.make_async_copy(slab.at[jl], rawrow.at[k, jl], ck_recv.at[k])

    for k in range(2):

        @pl.when(c == k)
        def _():
            for jl in range(C):
                if jl == k:
                    scatter_own(jl, k).start()
                else:
                    scatter(jl, k).start()

    def diag_x(k, p):
        _, at, n = lines[p]
        here = diag.at[pl.ds(at, n)]
        return remote(here, here, dx_send.at[k], dx_recv.at[p], r, lax.rem(x + k, X))

    for p in range(2):
        owner, at, n = lines[p]

        @pl.when(c == owner)
        def _():
            for u in range(n):
                diag_own(at + u).wait()
            for k in range(1, X):
                diag_x(k, p).start()

    def diag_y(k):
        return remote(diag, diag, dy_send.at[k], dy_recv.at[0], r, k * X + x)

    @pl.when(y == 0)
    def _():
        for p in range(2):

            @pl.when(c != lines[p][0])
            def _():
                _, at, n = lines[p]
                here = diag.at[pl.ds(at, n)]
                remote(here, here, dx_send.at[0], dx_recv.at[p], r, c).wait_recv()

        for k in range(1, X):
            diag_y(k).start()

    @pl.when(y != 0)
    def _():
        remote(diag, diag, dy_send.at[0], dy_recv.at[0], r, c).wait_recv()

    for k in range(2):
        pltpu.make_async_copy(slab.at[0], rawrow.at[k, c], ck_recv.at[k]).wait()

    def gather(k, n):
        here = rawrow.at[n, c]
        return remote(here, here, ag_send.at[n, k], ag_recv.at[n, c], r, lax.rem(c + k, C))

    def along(k, n):
        return remote(
            rawrow.at[n, c], zbuf.at[n, r], z_send.at[n, k], z_recv.at[n, r], lax.rem(r + k, R), c
        )

    for k in range(1, R):
        for n in range(2):
            along(k, n).start()
    for n in range(2):
        for k in range(1, C):
            gather(k, n).start()

    mine = lax.rem(c, ratio) * R
    place = c // ratio

    def serve(p, n):
        return remote(
            zbuf.at[n, p], rawcol.at[n, place], v_send.at[n, p], v_recv.at[n, place], r, mine + p
        )

    def serve_own(p, n):
        return pltpu.make_async_copy(zbuf.at[n, p], rawcol.at[n, place], v_recv.at[n, place])

    own_z = [pltpu.make_async_copy(rawrow.at[n, c], zbuf.at[n, r], z_recv.at[n, r]) for n in range(2)]
    for copy in own_z:
        copy.start()

    def pass_on(p):
        for n in range(2):

            @pl.when(p != r)
            def _():
                remote(rawrow.at[n, 0], zbuf.at[n, p], z_send.at[n, 0], z_recv.at[n, p], r, c).wait_recv()

            @pl.when(mine + p == c)
            def _():
                serve_own(p, n).start()

            @pl.when(mine + p != c)
            def _():
                serve(p, n).start()

    rows = lax.broadcasted_iota(jnp.int32, (EDGE, EDGE), 0)
    cols = lax.broadcasted_iota(jnp.int32, (EDGE, EDGE), 1)
    eye = (rows == cols).astype(F32)

    def pivot(block, at):
        work[:, :EDGE] = jnp.where(rows >= cols, block, block.T)
        work[:, EDGE:] = eye
        factor(work, upper)
        low[at] = jnp.where(rows >= cols, upper[:, :EDGE].T, 0.0)
        low[at + 1] = jnp.where(rows >= cols, upper[:, EDGE:], 0.0)

    pivot(diag[0], 0)
    for copy in own_z:
        copy.wait()
    over(0, R, pass_on)
    low[2] = dot(diag[1], low[1], NT)
    pivot(diag[2] - dot(low[2], low[2], NT), 3)

    def solve(raw, at, count):
        a0 = raw[0, pl.ds(at, count)].reshape(count * EDGE, EDGE)
        a1 = raw[1, pl.ds(at, count)].reshape(count * EDGE, EDGE)
        q0 = dot(a0, low[1], NT)
        q1 = dot(a1 - dot(q0, low[2], NT), low[4], NT)
        raw[0, pl.ds(at, count)] = q0.reshape(count, EDGE, EDGE)
        raw[1, pl.ds(at, count)] = q1.reshape(count, EDGE, EDGE)

    def col_wait(s):
        for n in range(2):
            pltpu.make_async_copy(zbuf.at[n, 0], rawcol.at[n, s], v_recv.at[n, s]).wait()

    over(0, R, col_wait)
    many = min(4, R)
    over(0, R // many, lambda g: solve(rawcol, g * many, many))
    keep_col = pltpu.make_async_copy(rawcol, qcol, q_sem.at[0])
    keep_col.start()

    def row_wait(jl):
        @pl.when(jl != c)
        def _():
            for n in range(2):
                here = rawrow.at[n, jl]
                remote(here, here, ag_send.at[n, 0], ag_recv.at[n, jl], r, c).wait_recv()

    over(0, C, row_wait)
    for k in range(1, C):
        for n in range(2):
            gather(k, n).wait_send()
    for k in range(1, R):
        for n in range(2):
            along(k, n).wait_send()

    over(0, C // many, lambda g: solve(rawrow, g * many, many))

    @pl.when(r == 0)
    def _():
        rawrow[0, 0] = low[0]
        rawrow[1, 0] = jnp.zeros((EDGE, EDGE), F32)

    @pl.when(r == 1)
    def _():
        rawrow[0, 0] = low[2]
        rawrow[1, 0] = low[3]

    keep_row = pltpu.make_async_copy(rawrow, qrow, q_sem.at[1])
    keep_row.start()

    for p in range(3):

        @pl.when((r == owners[p][0]) & (c == owners[p][1]))
        def _():
            for k in range(1, R):
                diag_row(k, p).wait_send()

    for k in range(2):

        @pl.when(c == k)
        def _():
            for jl in range(C):
                if jl != k:
                    scatter(jl, k).wait_send()

            for s in range(1, X):
                diag_x(s, k).wait_send()

    @pl.when(y == 0)
    def _():
        for k in range(1, X):
            diag_y(k).wait_send()

    def served(p):
        @pl.when(mine + p != c)
        def _():
            for n in range(2):
                serve(p, n).wait_send()

    over(0, R, served)
    keep_col.wait()
    keep_row.wait()


def panels(R, C, slab):
    hbm = pl.BlockSpec(memory_space=pltpu.HBM)
    dma = pltpu.SemaphoreType.DMA
    X = math.isqrt(C)
    return pl.pallas_call(
        functools.partial(panel_kernel, R, C),
        in_specs=[hbm],
        out_specs=[hbm, hbm],
        out_shape=[
            jax.ShapeDtypeStruct((2, C, EDGE, EDGE), F32),
            jax.ShapeDtypeStruct((2, R, EDGE, EDGE), F32),
        ],
        scratch_shapes=[
            pltpu.VMEM((3, EDGE, EDGE), F32),
            pltpu.VMEM((2, C, EDGE, EDGE), F32),
            pltpu.VMEM((2, R, EDGE, EDGE), F32),
            pltpu.VMEM((2, R, EDGE, EDGE), F32),
            pltpu.VMEM((EDGE, 2 * EDGE), F32),
            pltpu.VMEM((EDGE, 2 * EDGE), F32),
            pltpu.VMEM((5, EDGE, EDGE), F32),
            dma((R,)), dma((3,)), dma((X,)), dma((2,)), dma((X,)), dma((1,)), dma((C,)), dma((2,)),
            dma((2, C)), dma((2, C)), dma((2, R)), dma((2, R)), dma((2, R)), dma((2, R)), dma((2,)),
        ],
        compiler_params=pltpu.CompilerParams(
            collective_id=1, has_side_effects=True, vmem_limit_bytes=60 << 20
        ),
        name="panels",
    )(slab)


def halves(x):
    high = x.astype(BF16)
    return high, (x - high.astype(F32)).astype(BF16)


def update_kernel(R, C, place, landing, grid, qrow, qcol, arrived, out, wide, head, follow):
    jl = pl.program_id(0)
    slots = arrived.shape[1]
    r, c = place[0], place[1]
    i = jl * R + r
    rows = lax.broadcasted_iota(jnp.int32, (EDGE, EDGE), 0)
    cols = lax.broadcasted_iota(jnp.int32, (EDGE, EDGE), 1)

    @pl.when(jl == 0)
    def _():
        def clear(k):
            head[k] = -1

        over(0, C, clear)

        def link(k):
            @pl.when(landing[1 + slots + k] >= 0)
            def _():
                where = landing[1 + k]
                follow[k] = head[where]
                head[where] = k

        over(0, slots, link)

        def split(s):
            for n in range(2):
                high, low = halves(qcol[n, s])
                at = pl.ds(pl.multiple_of(s * EDGE, EDGE), EDGE)
                for m, part in ((0, high.T), (2, low.T), (4, high.T)):
                    wide[(m + n) * EDGE : (m + n + 1) * EDGE, at] = part

        over(0, R, split)

    first, second = halves(qrow[0, 0]), halves(qrow[1, 0])
    left = jnp.concatenate([first[0], second[0], first[0], second[0], first[1], second[1]], axis=1)
    for s in range(R):
        j = s * C + c

        @pl.when(i < j)
        def _():
            out[0, s] = jnp.zeros((EDGE, EDGE), F32)

        @pl.when((i >= j) & (j < 2))
        def _():
            out[0, s] = jnp.where(j == 0, qrow[0, 0], qrow[1, 0])

        @pl.when((i >= j) & (j >= 2))
        def _():
            out[0, s] = grid[0, s] - dot16(left, wide[:, s * EDGE : (s + 1) * EDGE], NN)

    def more(k):
        return k >= 0

    def add(k):
        s = landing[1 + slots + k]

        @pl.when(s * C + c >= 2)
        def _():
            out[0, s] = out[0, s] + arrived[:, k].reshape(EDGE, EDGE)

        return follow[k]

    lax.while_loop(more, add, head[jl])
    for s in range(R):

        @pl.when((i == s * C + c) & (i >= 2))
        def _():
            out[0, s] = jnp.where(rows >= cols, out[0, s], 0.0)


def update(R, C, place, landing, grid, qrow, qcol, arrived):
    cap3 = arrived.shape[1]
    block = pl.BlockSpec((1, R, EDGE, EDGE), lambda jl, *_: (jl, 0, 0, 0))
    return pl.pallas_call(
        functools.partial(update_kernel, R, C),
        grid_spec=pltpu.PrefetchScalarGridSpec(
            num_scalar_prefetch=2,
            grid=(C,),
            in_specs=[
                block,
                pl.BlockSpec((2, 1, EDGE, EDGE), lambda jl, *_: (0, jl, 0, 0)),
                pl.BlockSpec((2, R, EDGE, EDGE), lambda jl, *_: (0, 0, 0, 0)),
                pl.BlockSpec(
                    arrived.shape, lambda jl, *_: (0, 0, 0, 0),
                    pipeline_mode=pl.Buffered(1),
                ),
            ],
            out_specs=block,
            scratch_shapes=[
                pltpu.VMEM((6 * EDGE, R * EDGE), BF16),
                pltpu.SMEM((C,), jnp.int32),
                pltpu.SMEM((cap3,), jnp.int32),
            ],
        ),
        out_shape=jax.ShapeDtypeStruct((C, R, EDGE, EDGE), F32),
        compiler_params=pltpu.CompilerParams(vmem_limit_bytes=60 << 20),
        name="update",
    )(place, landing, grid, qrow, qcol, arrived)


def capacities(R, C, T):
    if T < 32:
        return 8, 16
    return 104, 112


def hot(values, count):
    return (values[..., None] == jnp.arange(count, dtype=jnp.int32)).astype(BF16)


def before(marks):
    n = marks.shape[-2]
    serial = jnp.arange(n, dtype=jnp.int32)
    lower = (serial[:, None] > serial[None, :]).astype(BF16)
    return jnp.einsum("pq,...qk->...pk", lower, marks, preferred_element_type=F32)


def local(front_entries, child_updates, row_maps, col_maps, target_columns, row_offsets):
    R = lax.axis_size("row")
    C = lax.axis_size("col")
    count = R * C
    T = child_updates.shape[0]
    cap2, cap3 = capacities(R, C, T)
    my_row = lax.axis_index("row").astype(jnp.int32)
    my_col = lax.axis_index("col").astype(jnp.int32)

    told = jnp.concatenate([target_columns[:, 0], row_offsets[:, 0]])
    told = lax.all_to_all(
        jnp.broadcast_to(told, (count, 2 * T)), ("row", "col"), split_axis=0, concat_axis=0, tiled=True
    )
    columns, offsets = told[:, :T], told[:, T:]
    target_rows = columns + offsets % (count - columns)
    columns = columns.reshape(R, C * T)
    target_rows = target_rows.reshape(R, C * T)
    to_row, to_col = target_rows % R, columns % C

    row_hot = hot(to_row, R)
    rank2 = jnp.sum(before(row_hot) * row_hot.astype(F32), axis=-1).astype(jnp.int32)
    mine = to_row == my_row
    col_hot = hot(jnp.where(mine, to_col, -1), C)
    inside = before(col_hot)
    totals = jnp.sum(col_hot.astype(F32), axis=1)
    planes = jnp.arange(R, dtype=jnp.int32)
    ahead = jnp.sum(jnp.where((planes[:, None] > planes[None, :])[..., None], totals[None], 0.0), axis=1)
    rank3 = jnp.sum((inside + ahead[:, None, :]) * col_hot.astype(F32), axis=-1).astype(jnp.int32)
    loads2 = jnp.sum(row_hot.astype(F32), axis=1)
    loads3 = jnp.einsum("pqk,pql->kl", row_hot, hot(to_col, C), preferred_element_type=F32)
    passes2 = (jnp.max(loads2).astype(jnp.int32) + cap2 - 1) // cap2
    passes3 = (jnp.max(loads3).astype(jnp.int32) + cap3 - 1) // cap3

    def tables(a, b):
        own_hot = lax.dynamic_index_in_dim(row_hot, my_row, 0, keepdims=False)
        own_rank = lax.dynamic_index_in_dim(rank2, my_row, 0, keepdims=False)
        serial = jnp.arange(C * T, dtype=jnp.int32)
        values = jnp.stack([serial // T, serial % T], axis=0).astype(BF16)
        marked = values[:, :, None] * own_hot[None]
        found = jnp.einsum("vqk,qn->vkn", marked, hot(own_rank - a * cap2, cap2), preferred_element_type=F32)
        found = found.astype(jnp.int32)
        index2 = (found[0] * T + found[1]).reshape(-1)
        place2 = rank2 - a * cap2
        active = (place2 >= 0) & (place2 < cap2) & mine
        source = jnp.broadcast_to(planes[:, None], (R, C * T))
        values = jnp.stack(
            [source, place2, target_rows // R, columns // C, jnp.ones_like(source)], axis=0
        )
        values = jnp.where(active, values, 0).astype(BF16)
        marked = values[..., None] * col_hot[None]
        found = jnp.einsum(
            "vpqk,pqn->vkn", marked, hot(rank3 - b * cap3, cap3), preferred_element_type=F32
        ).astype(jnp.int32)
        index3 = (found[0] * cap2 + found[1]).reshape(-1)
        here = lax.dynamic_index_in_dim(found, my_col, 1, keepdims=False)
        return index2, index3, here[2], here[3], here[4]

    index2, index3, land_row, land_col, valid = tables(0, 0)
    placed = place_tiles(C, child_updates, row_maps, col_maps)
    grid, arrived = spread(
        R, C, cap2, cap3, placed, index2, index3, front_entries.reshape(count, EDGE, EDGE)
    )

    def another(carry):
        p, grid = carry
        p, tiles = lax.optimization_barrier((p, placed))
        index2, index3, land_row, land_col, valid = tables(p // passes3, p % passes3)
        held = lax.all_to_all(tiles, "col", split_axis=0, concat_axis=0, tiled=True)
        held = held.reshape((C * T, EDGE // C, EDGE))[index2].reshape(R, cap2, EDGE // C, EDGE)
        held = lax.all_to_all(held, "row", split_axis=0, concat_axis=0, tiled=True)
        held = held.reshape((R * cap2, EDGE // C, EDGE))[index3].reshape(C, cap3, EDGE // C, EDGE)
        held = lax.all_to_all(held, "col", split_axis=0, concat_axis=0, tiled=True)
        tiles = held.transpose(1, 0, 2, 3).reshape(cap3, EDGE, EDGE)
        tiles = jnp.where((valid > 0)[:, None, None], tiles, 0.0)
        return p + 1, grid.at[land_row, land_col].add(tiles)

    _, grid = lax.while_loop(lambda carry: carry[0] < passes2 * passes3, another, (jnp.int32(1), grid))

    landing = jnp.concatenate([my_col[None], land_row, jnp.where(valid > 0, land_col, -1)])
    slab = slab_of(C, landing, grid, arrived)
    qrow, qcol = panels(R, C, slab)
    place = jnp.stack([my_row, my_col])
    result = update(R, C, place, landing, grid, qrow, qcol, arrived)
    return result.reshape(C, 1, R, 1, EDGE, EDGE)


def solution(mesh):
    return jax.shard_map(
        local,
        mesh=mesh,
        in_specs=(
            P(None, ("row", "col")),
            P(("row", "col"), None, None),
            P(("row", "col"), None),
            P(("row", "col"), None),
            P(("row", "col"), None),
            P(("row", "col"), None),
        ),
        out_specs=P(None, "row", None, "col", None, None),
        check_vma=False,
    )
```

```python
import functools
import math

import jax
import jax.numpy as jnp
from jax import lax
from jax.experimental import pallas as pl
from jax.experimental.pallas import tpu as pltpu
from jax.sharding import PartitionSpec as P

EDGE = 128
MESH = pl.DeviceIdType.MESH
PRECISE = lax.Precision.HIGHEST
F32 = jnp.float32
BF16 = jnp.bfloat16
NN = ((1,), (0,))
NT = ((1,), (1,))
TN = ((0,), (0,))


def dot(a, b, dims):
    return lax.dot_general(a, b, (dims, ((), ())), precision=PRECISE, preferred_element_type=F32)


def dot16(a, b, dims):
    return lax.dot_general(a, b, (dims, ((), ())), preferred_element_type=F32)


def remote(src, dst, ss, rs, rr, cc):
    return pltpu.make_async_remote_copy(
        src_ref=src, dst_ref=dst, send_sem=ss, recv_sem=rs, device_id=(rr, cc), device_id_type=MESH
    )


def over(low, high, body):
    def run(i, _):
        body(i)
        return 0

    lax.fori_loop(low, high, run, 0)


def greet(R, C, r, c):
    barrier = pltpu.get_barrier_semaphore()
    for k in range(1, R):
        pl.semaphore_signal(barrier, inc=1, device_id=(lax.rem(r + k, R), c), device_id_type=MESH)
    for k in range(1, C):
        pl.semaphore_signal(barrier, inc=1, device_id=(r, lax.rem(c + k, C)), device_id_type=MESH)
    pl.semaphore_wait(barrier, R + C - 2)


GROUP = 4


def place_kernel(C, tile, row_map, col_map, out):
    t = pl.program_id(0)
    levels = lax.broadcasted_iota(jnp.int32, (EDGE, EDGE), 0)
    for g in range(GROUP):
        k = t * GROUP + g
        col_hot = (levels == col_map[pl.ds(k, 1), :]).astype(F32).astype(BF16)
        row_hot = (levels == row_map[pl.ds(k, 1), :]).astype(F32).astype(BF16)
        x = tile[g]
        first = x.astype(BF16)
        rest = x - first.astype(F32)
        second = rest.astype(BF16)
        third = (rest - second.astype(F32)).astype(BF16)
        parts = [dot16(p, col_hot, NT).astype(BF16) for p in (first, second, third)]
        placed = (
            dot16(row_hot, parts[0], NN) + dot16(row_hot, parts[1], NN)
        ) + dot16(row_hot, parts[2], NN)
        for q in range(C):
            out[q, g] = placed[q * (EDGE // C) : (q + 1) * (EDGE // C), :]


def place_tiles(C, tiles, row_map, col_map):
    count = tiles.shape[0]
    whole = pl.BlockSpec((count, EDGE), lambda t: (0, 0))
    return pl.pallas_call(
        functools.partial(place_kernel, C),
        grid=(count // GROUP,),
        in_specs=[pl.BlockSpec((GROUP, EDGE, EDGE), lambda t: (t, 0, 0)), whole, whole],
        out_specs=pl.BlockSpec((C, GROUP, EDGE // C, EDGE), lambda t: (0, t, 0, 0)),
        out_shape=jax.ShapeDtypeStruct((C, count, EDGE // C, EDGE), F32),
        name="place",
    )(tiles, row_map, col_map)


STEP = 8


def factor(work, upper):
    rows8 = lax.broadcasted_iota(jnp.int32, (STEP, 1), 0)
    lanes = lax.broadcasted_iota(jnp.int32, (STEP, EDGE), 1)

    def block(b, _):
        first = pl.multiple_of(b * STEP, STEP)
        x = work[pl.ds(first, STEP), :]
        d = pltpu.roll(x[:, :EDGE], lax.rem(EDGE - first, EDGE), 1)
        for t in range(STEP):
            pivot = d[t : t + 1, t : t + 1]
            scale = lax.rsqrt(pivot)
            ratio = d[:, t : t + 1] / pivot
            ratio = jnp.where(rows8 > t, ratio, jnp.where(rows8 == t, 1.0 - scale, 0.0))
            x = x - ratio * x[t : t + 1, :]
            d = d - ratio * d[t : t + 1, :]
        upper[pl.ds(first, STEP), :] = x
        left = jnp.where(lanes >= first + STEP, x[:, :EDGE], 0.0)
        work[...] = work[...] - dot(left, x, TN)
        return 0

    lax.fori_loop(0, EDGE // STEP, block, 0)


PARTS = 4
PACK = 4


def spread_kernel(
    R, C, cap2, cap3, placed, index2, index3, pick, col, grid, out, low_out,
    r1, s2, r2, s3, stage, diag, mine, parts, work, upper, low,
    dr_send, dr_recv, dx_send, dx_recv, dy_send, dy_recv, m_send, m_recv, g_send, g_recv, low_sem,
    st_in, st_out, b_send, b_recv, p1_send, p1_recv, p2_send, p2_recv, p3_send, p3_recv,
):
    r = lax.axis_index("row")
    c = lax.axis_index("col")
    NB = R * C
    T = placed.shape[1]
    start_of = lambda column: jnp.where(column < 2, 0, column)
    i0 = start_of(r * C + c)
    X = math.isqrt(C)
    x, y = lax.rem(c, X), c // X
    greet(R, C, r, c)

    pieces = ((0, 0, 2), (1, 2, 1))

    def diag_row(p, k):
        owner, at, n = pieces[p]
        return remote(
            col.at[pl.ds(owner, n)], diag.at[pl.ds(at, n)], dr_send.at[k], dr_recv.at[p], lax.rem(r + k, R), c
        )

    def diag_own(p):
        owner, at, n = pieces[p]
        return pltpu.make_async_copy(col.at[pl.ds(owner, n)], diag.at[pl.ds(at, n)], dr_recv.at[p])

    def diag_x(p, k):
        _, at, n = pieces[p]
        here = diag.at[pl.ds(at, n)]
        return remote(here, here, dx_send.at[k], dx_recv.at[p], r, lax.rem(x + k, X))

    def diag_y(k):
        return remote(diag, diag, dy_send.at[k], dy_recv.at[0], r, k * X + x)

    for p in range(2):

        @pl.when((r == 0) & (c == pieces[p][0]))
        def _():
            for k in range(1, R):
                diag_row(p, k).start()
            diag_own(p).start()

    part1 = T // PARTS

    def first(k, h):
        to = lax.rem(c + k, C)
        return remote(
            placed.at[to, pl.ds(h * part1, part1)], r1.at[pl.ds(c * T + h * part1, part1)],
            p1_send.at[k, h], p1_recv.at[c, h], r, to,
        )

    def first_wait(k, h):
        src = lax.rem(c + k, C)
        remote(
            placed.at[0, pl.ds(0, part1)], r1.at[pl.ds(src * T + h * part1, part1)],
            p1_send.at[0, h], p1_recv.at[src, h], r, c,
        ).wait_recv()

    first_own = pltpu.make_async_copy(placed.at[c], r1.at[pl.ds(c * T, T)], p1_recv.at[c, 0])
    first_own.start()
    for h in range(PARTS):
        for k in range(1, C):
            first(k, h).start()

    def b_copy(i):
        return remote(
            col.at[i], grid.at[i // R, r], b_send.at[i], b_recv.at[i // R, r], lax.rem(i, R), c
        )

    def own_in(jl):
        return pltpu.make_async_copy(col.at[jl * R + r], stage.at[jl], st_in.at[jl])

    def own_out(jl):
        return pltpu.make_async_copy(stage.at[jl], grid.at[jl, r], st_out.at[jl])

    def own_blocks(body):
        def run(jl):
            @pl.when(jl * R + r >= i0)
            def _():
                body(jl)

        over(0, C, run)

    def sent_blocks(low, high, body):
        def run(i):
            @pl.when(lax.rem(i, R) != r)
            def _():
                body(i)

        over(low, high, run)

    middle = i0 + (NB - i0) // 3
    own_blocks(lambda jl: own_in(jl).start())
    sent_blocks(i0, middle, lambda i: b_copy(i).start())

    def own_turn(jl):
        own_in(jl).wait()
        own_out(jl).start()

    own_blocks(own_turn)

    first_own.wait()
    for h in range(PARTS):
        for k in range(1, C):
            first_wait(k, h)

    for p in range(2):

        @pl.when(c == pieces[p][0])
        def _():
            diag_own(p).wait()
            for k in range(1, X):
                diag_x(p, k).start()

    def second(k):
        to = lax.rem(r + k, R)
        return remote(s2.at[to], r2.at[pl.ds(r * cap2, cap2)], p2_send.at[k], p2_recv.at[r], to, c)

    def second_wait(k):
        src = lax.rem(r + k, R)
        remote(s2.at[0], r2.at[pl.ds(src * cap2, cap2)], p2_send.at[0], p2_recv.at[src], r, c).wait_recv()

    def pack2(k):
        to = lax.rem(r + k, R)

        def run(n):
            for u in range(PACK):
                s2[to, n * PACK + u] = r1[index2[to * cap2 + n * PACK + u]]

        over(0, cap2 // PACK, run)

    for k in range(1, R):
        pack2(k)
        if k > 1:
            second(k - 1).start()

    def pack2_own(n):
        for u in range(PACK):
            r2[r * cap2 + n * PACK + u] = r1[index2[r * cap2 + n * PACK + u]]

    over(0, cap2 // PACK, pack2_own)
    second(R - 1).start()

    @pl.when(y == 0)
    def _():
        for p in range(2):

            @pl.when(c != pieces[p][0])
            def _():
                _, at, n = pieces[p]
                here = diag.at[pl.ds(at, n)]
                remote(here, here, dx_send.at[0], dx_recv.at[p], r, c).wait_recv()

        for k in range(1, X):
            diag_y(k).start()

    for k in range(1, R):
        second_wait(k)

    owned = ((0, 1), (1, 2))

    def mine_own_rows(p):
        at, n = owned[p]
        return mine.at[pl.ds(at, n)]

    def mine_row(p, k):
        here = mine_own_rows(p)
        return remote(here, here, m_send.at[k], m_recv.at[p], lax.rem(r + k, R), c)

    for p in range(2):

        @pl.when(r == p)
        def _():
            at, n = owned[p]
            zero = jnp.zeros(mine.shape[1:], F32)

            def run(k, sums):
                for u in range(PACK):
                    slot = k * PACK + u
                    sums = tuple(
                        total + pick[b * R * cap2 + slot] * r2[slot] for b, total in enumerate(sums)
                    )
                return sums

            sums = lax.fori_loop(0, R * cap2 // PACK, run, (zero,) * n)
            for b in range(n):
                mine[at + b] = sums[b]
            for k in range(1, R):
                mine_row(p, k).start()

    for p in range(2):

        @pl.when(r != p)
        def _():
            here = mine_own_rows(p)
            remote(here, here, m_send.at[0], m_recv.at[p], r, c).wait_recv()

    def mine_col(k):
        to = lax.rem(c + k, C)
        return remote(mine, parts.at[c], g_send.at[k], g_recv.at[c], r, to)

    for k in range(1, C):
        mine_col(k).start()
    parts[c] = mine[...]
    sent_blocks(middle, NB, lambda i: b_copy(i).start())


    part3 = cap3 // PARTS

    def third(k, h):
        to = lax.rem(c + k, C)
        at = pl.ds(h * part3, part3)
        return remote(s3.at[to, at], out.at[c, at], p3_send.at[k, h], p3_recv.at[c, h], r, to)

    def third_wait(k, h):
        src = lax.rem(c + k, C)
        at = pl.ds(h * part3, part3)
        remote(s3.at[0, at], out.at[src, at], p3_send.at[0, h], p3_recv.at[src, h], r, c).wait_recv()

    third_own = pltpu.make_async_copy(s3.at[c], out.at[c], p3_recv.at[c, 0])

    def pack3(k, h):
        to = lax.rem(c + k, C)

        def run(n):
            for u in range(PACK):
                at = h * part3 + n * PACK + u
                s3[to, at] = r2[index3[to * cap3 + at]]

        over(0, part3 // PACK, run)

    def third_part(h):
        def step(k):
            pack3(k, h)

            @pl.when(k > 1)
            def _():
                third(k - 1, h).start()

        over(1, C, step)
        pack3(C, h)
        third(C - 1, h).start()

    over(0, PARTS, third_part)

    @pl.when(y != 0)
    def _():
        remote(diag, diag, dy_send.at[0], dy_recv.at[0], r, c).wait_recv()

    sub = mine.shape[1]

    def part_wait(q):
        @pl.when(q != c)
        def _():
            remote(mine, parts.at[q], g_send.at[0], g_recv.at[q], r, c).wait_recv()

    over(0, C, part_wait)
    for k in range(1, X):

        @pl.when(y == 0)
        def _():
            diag_y(k).wait_send()

    for p in range(2):

        @pl.when(c == pieces[p][0])
        def _():
            for k in range(1, X):
                diag_x(p, k).wait_send()

    rows = lax.broadcasted_iota(jnp.int32, (EDGE, EDGE), 0)
    cols = lax.broadcasted_iota(jnp.int32, (EDGE, EDGE), 1)
    eye = (rows == cols).astype(F32)
    for q in range(C):
        for b in range(3):
            at = pl.ds(q * sub, sub)
            diag[b, at, :] = diag[b, at, :] + parts[q, b]

    def pivot(block, at):
        work[:, :EDGE] = jnp.where(rows >= cols, block, block.T)
        work[:, EDGE:] = eye
        factor(work, upper)
        low[at] = jnp.where(rows >= cols, upper[:, :EDGE].T, 0.0)
        low[at + 1] = jnp.where(rows >= cols, upper[:, EDGE:], 0.0)

    pivot(diag[0], 0)
    low[2] = dot(diag[1], low[1], NT)
    pivot(diag[2] - dot(low[2], low[2], NT), 3)
    low_copy = pltpu.make_async_copy(low, low_out, low_sem)
    low_copy.start()

    own_blocks(lambda jl: own_out(jl).wait())
    for s in range(R):
        begin = start_of(s * C + c)

        def run(jl):
            @pl.when((r != s) & (jl * R + r >= begin))
            def _():
                remote(col.at[0], grid.at[jl, s], b_send.at[0], b_recv.at[jl, s], r, c).wait_recv()

        over(0, C, run)
    third_own.start()
    sent_blocks(i0, NB, lambda i: b_copy(i).wait_send())
    for h in range(PARTS):
        for k in range(1, C):
            first(k, h).wait_send()
    for k in range(1, R):
        second(k).wait_send()
    for h in range(PARTS):
        for k in range(1, C):
            third_wait(k, h)
        for k in range(1, C):
            third(k, h).wait_send()
    third_own.wait()
    low_copy.wait()
    for p in range(2):

        @pl.when((r == 0) & (c == pieces[p][0]))
        def _():
            for k in range(1, R):
                diag_row(p, k).wait_send()

        @pl.when(r == p)
        def _():
            for k in range(1, R):
                mine_row(p, k).wait_send()

    for k in range(1, C):
        mine_col(k).wait_send()


def spread(R, C, cap2, cap3, placed, index2, index3, pick, front):
    hbm = pl.BlockSpec(memory_space=pltpu.HBM)
    smem = pl.BlockSpec(memory_space=pltpu.SMEM)
    dma = pltpu.SemaphoreType.DMA
    T, sub = placed.shape[1], placed.shape[2]
    return pl.pallas_call(
        functools.partial(spread_kernel, R, C, cap2, cap3),
        in_specs=[hbm, smem, smem, smem, hbm],
        out_specs=[hbm, hbm, hbm],
        out_shape=[
            jax.ShapeDtypeStruct((C, R, EDGE, EDGE), F32),
            jax.ShapeDtypeStruct((C, cap3, sub, EDGE), F32),
            jax.ShapeDtypeStruct((5, EDGE, EDGE), F32),
        ],
        scratch_shapes=[
            pltpu.VMEM((C * T, sub, EDGE), F32),
            pltpu.VMEM((R, cap2, sub, EDGE), F32),
            pltpu.VMEM((R * cap2, sub, EDGE), F32),
            pltpu.VMEM((C, cap3, sub, EDGE), F32),
            pltpu.VMEM((C, EDGE, EDGE), F32),
            pltpu.VMEM((3, EDGE, EDGE), F32),
            pltpu.VMEM((3, sub, EDGE), F32),
            pltpu.VMEM((C, 3, sub, EDGE), F32),
            pltpu.VMEM((EDGE, 2 * EDGE), F32),
            pltpu.VMEM((EDGE, 2 * EDGE), F32),
            pltpu.VMEM((5, EDGE, EDGE), F32),
            dma((R,)), dma((2,)), dma((C,)), dma((2,)), dma((C,)), dma((1,)),
            dma((R,)), dma((2,)), dma((C,)), dma((C,)), dma,
            dma((C,)), dma((C,)), dma((R * C,)), dma((C, R)),
            dma((C, PARTS)), dma((C, PARTS)), dma((R,)), dma((R,)), dma((C, PARTS)), dma((C, PARTS)),
        ],
        compiler_params=pltpu.CompilerParams(
            collective_id=0, has_side_effects=True, vmem_limit_bytes=60 << 20
        ),
        name="spread",
    )(placed, index2, index3, pick, front)


def slab_kernel(C, landing, grid, arrived, out, tile, sem):
    out[...] = grid[:, 0]
    slots = arrived.shape[1]

    def run(k):
        @pl.when(landing[1 + slots + k] == 0)
        def _():
            copy = pltpu.make_async_copy(arrived.at[:, k], tile, sem)
            copy.start()
            copy.wait()
            jl = landing[1 + k]
            out[jl] = out[jl] + tile[...].reshape(EDGE, EDGE)

    @pl.when(landing[0] < 2)
    def _():
        over(0, slots, run)


def slab_of(C, landing, grid, arrived):
    return pl.pallas_call(
        functools.partial(slab_kernel, C),
        grid=(1,),
        in_specs=[
            pl.BlockSpec(memory_space=pltpu.SMEM),
            pl.BlockSpec((C, 1, EDGE, EDGE), lambda t: (0, 0, 0, 0)),
            pl.BlockSpec(memory_space=pltpu.HBM),
        ],
        out_specs=pl.BlockSpec((C, EDGE, EDGE), lambda t: (0, 0, 0)),
        out_shape=jax.ShapeDtypeStruct((C, EDGE, EDGE), F32),
        scratch_shapes=[pltpu.VMEM((arrived.shape[0], EDGE // C, EDGE), F32), pltpu.SemaphoreType.DMA],
        compiler_params=pltpu.CompilerParams(vmem_limit_bytes=60 << 20),
        name="slab",
    )(landing, grid, arrived)


def panel_kernel(
    R, C, slab, low, qrow, qcol,
    chunk, rows_q, zbuf, cols_q,
    sc_send, ck_recv, ag_send, ag_recv, z_send, z_recv, v_send, v_recv, q_sem,
):
    r = lax.axis_index("row")
    c = lax.axis_index("col")
    ratio = C // R
    greet(R, C, r, c)

    def scatter(jl, k):
        return remote(slab.at[jl], chunk.at[k], sc_send.at[jl], ck_recv.at[k], r, jl)

    def scatter_own(jl, k):
        return pltpu.make_async_copy(slab.at[jl], chunk.at[k], ck_recv.at[k])

    for k in range(2):

        @pl.when(c == k)
        def _():
            for jl in range(C):
                if jl == k:
                    scatter_own(jl, k).start()
                else:
                    scatter(jl, k).start()

    i = c * R + r
    scatter_own(0, 0).wait()
    q0 = dot(chunk[0], low[1], NT)
    scatter_own(0, 1).wait()
    q1 = dot(chunk[1] - dot(q0, low[2], NT), low[4], NT)
    rows_q[0, c] = jnp.where(i == 0, low[0], jnp.where(i == 1, low[2], q0))
    rows_q[1, c] = jnp.where(i == 0, 0.0, jnp.where(i == 1, low[3], q1))

    def gather(k, n):
        here = rows_q.at[n, c]
        return remote(here, here, ag_send.at[n, k], ag_recv.at[n, c], r, lax.rem(c + k, C))

    def along(k, n):
        return remote(
            rows_q.at[n, c], zbuf.at[n, r], z_send.at[n, k], z_recv.at[n, r], lax.rem(r + k, R), c
        )

    for n in range(2):
        for k in range(1, R):
            along(k, n).start()
    for n in range(2):
        for k in range(1, C):
            gather(k, n).start()

    mine = lax.rem(c, ratio) * R
    place = c // ratio

    def serve(p, n):
        return remote(
            zbuf.at[n, p], cols_q.at[n, place], v_send.at[n, p], v_recv.at[n, place], r, mine + p
        )

    def serve_own(p, n):
        return pltpu.make_async_copy(zbuf.at[n, p], cols_q.at[n, place], v_recv.at[n, place])

    own_z = [pltpu.make_async_copy(rows_q.at[n, c], zbuf.at[n, r], z_recv.at[n, r]) for n in range(2)]
    for copy in own_z:
        copy.start()
    for copy in own_z:
        copy.wait()

    def pass_on(p):
        for n in range(2):

            @pl.when(p != r)
            def _():
                remote(rows_q.at[n, 0], zbuf.at[n, p], z_send.at[n, 0], z_recv.at[n, p], r, c).wait_recv()

            @pl.when(mine + p == c)
            def _():
                serve_own(p, n).start()

            @pl.when(mine + p != c)
            def _():
                serve(p, n).start()

    over(0, R, pass_on)

    def row_wait(jl):
        @pl.when(jl != c)
        def _():
            for n in range(2):
                here = rows_q.at[n, jl]
                remote(here, here, ag_send.at[n, 0], ag_recv.at[n, jl], r, c).wait_recv()

    over(0, C, row_wait)
    keep_row = pltpu.make_async_copy(rows_q, qrow, q_sem.at[1])
    keep_row.start()

    def col_wait(s):
        for n in range(2):
            pltpu.make_async_copy(zbuf.at[n, 0], cols_q.at[n, s], v_recv.at[n, s]).wait()

    over(0, R, col_wait)
    keep_col = pltpu.make_async_copy(cols_q, qcol, q_sem.at[0])
    keep_col.start()

    for k in range(2):

        @pl.when(c == k)
        def _():
            for jl in range(C):
                if jl != k:
                    scatter(jl, k).wait_send()

    for n in range(2):
        for k in range(1, C):
            gather(k, n).wait_send()
        for k in range(1, R):
            along(k, n).wait_send()

    def served(p):
        @pl.when(mine + p != c)
        def _():
            for n in range(2):
                serve(p, n).wait_send()

    over(0, R, served)
    keep_col.wait()
    keep_row.wait()


def panels(R, C, slab, low):
    hbm = pl.BlockSpec(memory_space=pltpu.HBM)
    dma = pltpu.SemaphoreType.DMA
    return pl.pallas_call(
        functools.partial(panel_kernel, R, C),
        in_specs=[hbm, pl.BlockSpec(memory_space=pltpu.VMEM)],
        out_specs=[hbm, hbm],
        out_shape=[
            jax.ShapeDtypeStruct((2, C, EDGE, EDGE), F32),
            jax.ShapeDtypeStruct((2, R, EDGE, EDGE), F32),
        ],
        scratch_shapes=[
            pltpu.VMEM((2, EDGE, EDGE), F32),
            pltpu.VMEM((2, C, EDGE, EDGE), F32),
            pltpu.VMEM((2, R, EDGE, EDGE), F32),
            pltpu.VMEM((2, R, EDGE, EDGE), F32),
            dma((C,)), dma((2,)), dma((2, C)), dma((2, C)),
            dma((2, R)), dma((2, R)), dma((2, R)), dma((2, R)), dma((2,)),
        ],
        compiler_params=pltpu.CompilerParams(
            collective_id=1, has_side_effects=True, vmem_limit_bytes=60 << 20
        ),
        name="panels",
    )(slab, low)


def halves(x):
    high = x.astype(BF16)
    return high, (x - high.astype(F32)).astype(BF16)


def update_kernel(R, C, place, landing, grid, qrow, qcol, arrived, out, left, right, head, follow):
    s = pl.program_id(0)
    slots = arrived.shape[1]
    r, c = place[0], place[1]
    j = s * C + c
    rows = lax.broadcasted_iota(jnp.int32, (EDGE, EDGE), 0)
    cols = lax.broadcasted_iota(jnp.int32, (EDGE, EDGE), 1)

    @pl.when(s == 0)
    def _():
        def clear(k):
            head[k] = -1

        over(0, R, clear)

        def link(k):
            where = landing[1 + slots + k]

            @pl.when(where >= 0)
            def _():
                follow[k] = head[where]
                head[where] = k

        over(0, slots, link)

        def split(jl):
            at = pl.ds(pl.multiple_of(jl * EDGE, EDGE), EDGE)
            for n in range(2):
                high, low = halves(qrow[n, jl])
                for m, part in ((0, high), (2, high), (4, low)):
                    left[at, (m + n) * EDGE : (m + n + 1) * EDGE] = part

        over(0, C, split)

    for n in range(2):
        high, low = halves(qcol[n, 0])
        for m, part in ((0, high.T), (2, low.T), (4, high.T)):
            right[(m + n) * EDGE : (m + n + 1) * EDGE, :] = part

    many = min(4, C)
    for g in range(C // many):
        last = (g * many + many - 1) * R + r

        @pl.when((last >= j) & (j >= 2))
        def _():
            product = dot16(left[g * many * EDGE : (g + 1) * many * EDGE, :], right[...], NN)
            for u in range(many):
                out[g * many + u, 0] = grid[g * many + u, 0] - product[u * EDGE : (u + 1) * EDGE, :]

    @pl.when(j < 2)
    def _():
        for jl in range(C):
            out[jl, 0] = jnp.where(j == 0, qrow[0, jl], qrow[1, jl])

    def more(k):
        return k >= 0

    def add(k):
        jl = landing[1 + k]
        out[jl, 0] = out[jl, 0] + arrived[:, k].reshape(EDGE, EDGE)
        return follow[k]

    lax.while_loop(more, add, jnp.where(j >= 2, head[s], -1))
    for jl in range(C):
        i = jl * R + r

        @pl.when(i < j)
        def _():
            out[jl, 0] = jnp.zeros((EDGE, EDGE), F32)

        @pl.when((i == j) & (j >= 2))
        def _():
            out[jl, 0] = jnp.where(rows >= cols, out[jl, 0], 0.0)


def update(R, C, place, landing, grid, qrow, qcol, arrived):
    cap3 = arrived.shape[1]
    block = pl.BlockSpec((C, 1, EDGE, EDGE), lambda s, *_: (0, s, 0, 0))
    return pl.pallas_call(
        functools.partial(update_kernel, R, C),
        grid_spec=pltpu.PrefetchScalarGridSpec(
            num_scalar_prefetch=2,
            grid=(R,),
            in_specs=[
                block,
                pl.BlockSpec((2, C, EDGE, EDGE), lambda s, *_: (0, 0, 0, 0)),
                pl.BlockSpec((2, 1, EDGE, EDGE), lambda s, *_: (0, s, 0, 0)),
                pl.BlockSpec(arrived.shape, lambda s, *_: (0, 0, 0, 0), pipeline_mode=pl.Buffered(1)),
            ],
            out_specs=block,
            scratch_shapes=[
                pltpu.VMEM((C * EDGE, 6 * EDGE), BF16),
                pltpu.VMEM((6 * EDGE, EDGE), BF16),
                pltpu.SMEM((R,), jnp.int32),
                pltpu.SMEM((cap3,), jnp.int32),
            ],
        ),
        out_shape=jax.ShapeDtypeStruct((C, R, EDGE, EDGE), F32),
        compiler_params=pltpu.CompilerParams(vmem_limit_bytes=60 << 20),
        name="update",
    )(place, landing, grid, qrow, qcol, arrived)


def capacities(R, C, T):
    if T < 32:
        return 8, 16
    return 104, 112


def hot(values, count):
    return (values[..., None] == jnp.arange(count, dtype=jnp.int32)).astype(BF16)


def before(marks):
    n = marks.shape[-2]
    serial = jnp.arange(n, dtype=jnp.int32)
    lower = (serial[:, None] > serial[None, :]).astype(BF16)
    return jnp.einsum("pq,...qk->...pk", lower, marks, preferred_element_type=F32)


def local(front_entries, child_updates, row_maps, col_maps, target_columns, row_offsets):
    R = lax.axis_size("row")
    C = lax.axis_size("col")
    count = R * C
    T = child_updates.shape[0]
    cap2, cap3 = capacities(R, C, T)
    my_row = lax.axis_index("row").astype(jnp.int32)
    my_col = lax.axis_index("col").astype(jnp.int32)

    told = jnp.concatenate([target_columns[:, 0], row_offsets[:, 0]])
    told = lax.all_to_all(
        jnp.broadcast_to(told, (count, 2 * T)), ("row", "col"), split_axis=0, concat_axis=0, tiled=True
    )
    columns, offsets = told[:, :T], told[:, T:]
    target_rows = columns + offsets % (count - columns)
    columns = columns.reshape(R, C * T)
    target_rows = target_rows.reshape(R, C * T)
    to_row, to_col = target_rows % R, columns % C

    row_hot = hot(to_row, R)
    pivotal = (target_rows < 2) & (columns < 2)
    lead = row_hot * pivotal[..., None].astype(BF16)
    rest = row_hot - lead
    leads = jnp.sum(lead.astype(F32), axis=1, keepdims=True)
    rank2 = before(lead) * lead.astype(F32) + (before(rest) + leads) * rest.astype(F32)
    rank2 = jnp.sum(rank2, axis=-1).astype(jnp.int32)
    mine = to_row == my_row
    col_hot = hot(jnp.where(mine, to_col, -1), C)
    inside = before(col_hot)
    totals = jnp.sum(col_hot.astype(F32), axis=1)
    planes = jnp.arange(R, dtype=jnp.int32)
    ahead = jnp.sum(jnp.where((planes[:, None] > planes[None, :])[..., None], totals[None], 0.0), axis=1)
    rank3 = jnp.sum((inside + ahead[:, None, :]) * col_hot.astype(F32), axis=-1).astype(jnp.int32)
    loads2 = jnp.sum(row_hot.astype(F32), axis=1)
    loads3 = jnp.einsum("pqk,pql->kl", row_hot, hot(to_col, C), preferred_element_type=F32)
    passes2 = (jnp.max(loads2).astype(jnp.int32) + cap2 - 1) // cap2
    passes3 = (jnp.max(loads3).astype(jnp.int32) + cap3 - 1) // cap3

    def tables(a, b):
        own_hot = lax.dynamic_index_in_dim(row_hot, my_row, 0, keepdims=False)
        own_rank = lax.dynamic_index_in_dim(rank2, my_row, 0, keepdims=False)
        serial = jnp.arange(C * T, dtype=jnp.int32)
        values = jnp.stack([serial // T, serial % T], axis=0).astype(BF16)
        marked = values[:, :, None] * own_hot[None]
        found = jnp.einsum("vqk,qn->vkn", marked, hot(own_rank - a * cap2, cap2), preferred_element_type=F32)
        found = found.astype(jnp.int32)
        index2 = (found[0] * T + found[1]).reshape(-1)
        place2 = rank2 - a * cap2
        active = (place2 >= 0) & (place2 < cap2) & mine
        source = jnp.broadcast_to(planes[:, None], (R, C * T))
        values = jnp.stack(
            [source, place2, target_rows // R, columns // C, jnp.ones_like(source)], axis=0
        )
        values = jnp.where(active, values, 0).astype(BF16)
        marked = values[..., None] * col_hot[None]
        found = jnp.einsum(
            "vpqk,pqn->vkn", marked, hot(rank3 - b * cap3, cap3), preferred_element_type=F32
        ).astype(jnp.int32)
        index3 = (found[0] * cap2 + found[1]).reshape(-1)
        here = lax.dynamic_index_in_dim(found, my_col, 1, keepdims=False)
        return index2, index3, here[2], here[3], here[4]

    index2, index3, land_row, land_col, valid = tables(0, 0)
    marks = jnp.stack([mine & pivotal & (columns == k) & (rank2 < cap2) for k in range(2)])
    pick = jnp.einsum("vpq,pqn->vpn", marks.astype(BF16), hot(rank2, cap2), preferred_element_type=F32)
    placed = place_tiles(C, child_updates, row_maps, col_maps)
    grid, arrived, low = spread(
        R, C, cap2, cap3, placed, index2, index3, pick.reshape(-1), front_entries.reshape(count, EDGE, EDGE)
    )

    def another(carry):
        p, grid = carry
        p, tiles = lax.optimization_barrier((p, placed))
        index2, index3, land_row, land_col, valid = tables(p // passes3, p % passes3)
        held = lax.all_to_all(tiles, "col", split_axis=0, concat_axis=0, tiled=True)
        held = held.reshape((C * T, EDGE // C, EDGE))[index2].reshape(R, cap2, EDGE // C, EDGE)
        held = lax.all_to_all(held, "row", split_axis=0, concat_axis=0, tiled=True)
        held = held.reshape((R * cap2, EDGE // C, EDGE))[index3].reshape(C, cap3, EDGE // C, EDGE)
        held = lax.all_to_all(held, "col", split_axis=0, concat_axis=0, tiled=True)
        tiles = held.transpose(1, 0, 2, 3).reshape(cap3, EDGE, EDGE)
        tiles = jnp.where((valid > 0)[:, None, None], tiles, 0.0)
        return p + 1, grid.at[land_row, land_col].add(tiles)

    _, grid = lax.while_loop(lambda carry: carry[0] < passes2 * passes3, another, (jnp.int32(1), grid))

    landing = jnp.concatenate([my_col[None], land_row, jnp.where(valid > 0, land_col, -1)])
    slab = slab_of(C, landing, grid, arrived)
    qrow, qcol = panels(R, C, slab, low)
    place = jnp.stack([my_row, my_col])
    result = update(R, C, place, landing, grid, qrow, qcol, arrived)
    return result.reshape(C, 1, R, 1, EDGE, EDGE)


def solution(mesh):
    return jax.shard_map(
        local,
        mesh=mesh,
        in_specs=(
            P(None, ("row", "col")),
            P(("row", "col"), None, None),
            P(("row", "col"), None),
            P(("row", "col"), None),
            P(("row", "col"), None),
            P(("row", "col"), None),
        ),
        out_specs=P(None, "row", None, "col", None, None),
        check_vma=False,
    )
```

```python
import functools
import math

import jax
import jax.numpy as jnp
from jax import lax
from jax.experimental import pallas as pl
from jax.experimental.pallas import tpu as pltpu
from jax.sharding import PartitionSpec as P

EDGE = 128
MESH = pl.DeviceIdType.MESH
PRECISE = lax.Precision.HIGHEST
F32 = jnp.float32
BF16 = jnp.bfloat16
NN = ((1,), (0,))
NT = ((1,), (1,))
TN = ((0,), (0,))


def dot(a, b, dims):
    return lax.dot_general(a, b, (dims, ((), ())), precision=PRECISE, preferred_element_type=F32)


def dot16(a, b, dims):
    return lax.dot_general(a, b, (dims, ((), ())), preferred_element_type=F32)


def remote(src, dst, ss, rs, rr, cc):
    return pltpu.make_async_remote_copy(
        src_ref=src, dst_ref=dst, send_sem=ss, recv_sem=rs, device_id=(rr, cc), device_id_type=MESH
    )


def over(low, high, body):
    def run(i, _):
        body(i)
        return 0

    lax.fori_loop(low, high, run, 0)


def greet(R, C, r, c):
    barrier = pltpu.get_barrier_semaphore()
    for k in range(1, R):
        pl.semaphore_signal(barrier, inc=1, device_id=(lax.rem(r + k, R), c), device_id_type=MESH)
    for k in range(1, C):
        pl.semaphore_signal(barrier, inc=1, device_id=(r, lax.rem(c + k, C)), device_id_type=MESH)
    pl.semaphore_wait(barrier, R + C - 2)


PARTS = 4
GROUP = 4


def begin_kernel(
    R, C, tiles, row_map, col_map, told, r1, told_all,
    held, placed, told_row,
    t_sem, tr_send, tr_recv, tc_send, tc_recv, send, recv,
):
    r = lax.axis_index("row")
    c = lax.axis_index("col")
    T = tiles.shape[0]
    sub = EDGE // C
    part = T // PARTS
    load = pltpu.make_async_copy(tiles, held, t_sem)
    load.start()
    greet(R, C, r, c)

    def tell_row(k):
        return remote(told, told_row.at[r], tr_send.at[k], tr_recv.at[r], lax.rem(r + k, R), c)

    def tell_col(k):
        return remote(told_row, told_all.at[c], tc_send.at[k], tc_recv.at[c], r, lax.rem(c + k, C))

    tell_own = pltpu.make_async_copy(told, told_row.at[r], tr_recv.at[r])
    tell_own.start()
    for k in range(1, R):
        tell_row(k).start()

    levels = lax.broadcasted_iota(jnp.int32, (EDGE, EDGE), 0)

    def place(t):
        for g in range(GROUP):
            k = t * GROUP + g
            col_hot = (levels == col_map[pl.ds(k, 1), :]).astype(F32).astype(BF16)
            row_hot = (levels == row_map[pl.ds(k, 1), :]).astype(F32).astype(BF16)
            x = held[k]
            first = x.astype(BF16)
            rest = x - first.astype(F32)
            second = rest.astype(BF16)
            third = (rest - second.astype(F32)).astype(BF16)
            moved = [dot16(p, col_hot, NT).astype(BF16) for p in (first, second, third)]
            full = (dot16(row_hot, moved[0], NN) + dot16(row_hot, moved[1], NN)) + dot16(
                row_hot, moved[2], NN
            )
            for q in range(C):
                placed[q, k] = full[q * sub : (q + 1) * sub, :]

    def slices(k, h):
        to = lax.rem(c + k, C)
        return remote(
            placed.at[to, pl.ds(h * part, part)], r1.at[pl.ds(c * T + h * part, part)],
            send.at[k, h], recv.at[c, h], r, to,
        )

    def slices_wait(k, h):
        src = lax.rem(c + k, C)
        remote(
            placed.at[0, pl.ds(0, part)], r1.at[pl.ds(src * T + h * part, part)],
            send.at[0, h], recv.at[src, h], r, c,
        ).wait_recv()

    load.wait()
    for h in range(PARTS):
        over(h * part // GROUP, (h + 1) * part // GROUP, place)
        if h == 0:
            tell_own.wait()
            for k in range(1, R):
                src = lax.rem(r + k, R)
                remote(told, told_row.at[src], tr_send.at[0], tr_recv.at[src], r, c).wait_recv()
            for k in range(1, C):
                tell_col(k).start()
            tell_kept = pltpu.make_async_copy(told_row, told_all.at[c], tc_recv.at[c])
            tell_kept.start()
        for k in range(1, C):
            slices(k, h).start()
    own = pltpu.make_async_copy(placed.at[c], r1.at[pl.ds(c * T, T)], recv.at[c, 0])
    own.start()
    tell_kept.wait()
    for k in range(1, C):
        src = lax.rem(c + k, C)
        remote(told_row, told_all.at[src], tc_send.at[0], tc_recv.at[src], r, c).wait_recv()
    for h in range(PARTS):
        for k in range(1, C):
            slices_wait(k, h)
    own.wait()
    for k in range(1, R):
        tell_row(k).wait_send()
    for k in range(1, C):
        tell_col(k).wait_send()
    for h in range(PARTS):
        for k in range(1, C):
            slices(k, h).wait_send()


def begin(R, C, tiles, row_map, col_map, told):
    hbm = pl.BlockSpec(memory_space=pltpu.HBM)
    vmem = pl.BlockSpec(memory_space=pltpu.VMEM)
    dma = pltpu.SemaphoreType.DMA
    T, sub = tiles.shape[0], EDGE // C
    return pl.pallas_call(
        functools.partial(begin_kernel, R, C),
        in_specs=[hbm, vmem, vmem, hbm],
        out_specs=[hbm, hbm],
        out_shape=[
            jax.ShapeDtypeStruct((C * T, sub, EDGE), F32),
            jax.ShapeDtypeStruct((C, R, 1, EDGE), jnp.int32),
        ],
        scratch_shapes=[
            pltpu.VMEM((T, EDGE, EDGE), F32),
            pltpu.VMEM((C, T, sub, EDGE), F32),
            pltpu.VMEM((R, 1, EDGE), jnp.int32),
            dma, dma((R,)), dma((R,)), dma((C,)), dma((C,)), dma((C, PARTS)), dma((C, PARTS)),
        ],
        compiler_params=pltpu.CompilerParams(
            collective_id=4, has_side_effects=True, vmem_limit_bytes=60 << 20
        ),
        name="begin",
    )(tiles, row_map, col_map, told)


STEP = 8


def factor(work, upper):
    rows8 = lax.broadcasted_iota(jnp.int32, (STEP, 1), 0)
    lanes = lax.broadcasted_iota(jnp.int32, (STEP, EDGE), 1)

    def block(b, _):
        first = pl.multiple_of(b * STEP, STEP)
        x = work[pl.ds(first, STEP), :]
        d = pltpu.roll(x[:, :EDGE], lax.rem(EDGE - first, EDGE), 1)
        for t in range(STEP):
            pivot = d[t : t + 1, t : t + 1]
            scale = lax.rsqrt(pivot)
            ratio = d[:, t : t + 1] / pivot
            ratio = jnp.where(rows8 > t, ratio, jnp.where(rows8 == t, 1.0 - scale, 0.0))
            x = x - ratio * x[t : t + 1, :]
            d = d - ratio * d[t : t + 1, :]
        upper[pl.ds(first, STEP), :] = x
        left = jnp.where(lanes >= first + STEP, x[:, :EDGE], 0.0)
        work[...] = work[...] - dot(left, x, TN)
        return 0

    lax.fori_loop(0, EDGE // STEP, block, 0)


PACK = 4


def spread_kernel(
    R, C, cap2, cap3, parts3, held, index2, index3, pick, col, grid, out, low_out,
    r1, s2, r2, s3, stage, diag, mine, parts, work, upper, low,
    dr_send, dr_recv, dx_send, dx_recv, dy_send, dy_recv, m_send, m_recv, g_send, g_recv, low_sem,
    st_in, st_out, b_send, b_recv, load_sem, p2_send, p2_recv, p3_send, p3_recv,
):
    r = lax.axis_index("row")
    c = lax.axis_index("col")
    NB = R * C
    start_of = lambda column: jnp.where(column < 2, 0, column)
    i0 = start_of(r * C + c)
    X = math.isqrt(C)
    x, y = lax.rem(c, X), c // X
    greet(R, C, r, c)

    pieces = ((0, 0, 2), (1, 2, 1))

    def diag_row(p, k):
        owner, at, n = pieces[p]
        return remote(
            col.at[pl.ds(owner, n)], diag.at[pl.ds(at, n)], dr_send.at[k], dr_recv.at[p], lax.rem(r + k, R), c
        )

    def diag_own(p):
        owner, at, n = pieces[p]
        return pltpu.make_async_copy(col.at[pl.ds(owner, n)], diag.at[pl.ds(at, n)], dr_recv.at[p])

    def diag_x(p, k):
        _, at, n = pieces[p]
        here = diag.at[pl.ds(at, n)]
        return remote(here, here, dx_send.at[k], dx_recv.at[p], r, lax.rem(x + k, X))

    def diag_y(k):
        return remote(diag, diag, dy_send.at[k], dy_recv.at[0], r, k * X + x)

    for p in range(2):

        @pl.when((r == 0) & (c == pieces[p][0]))
        def _():
            for k in range(1, R):
                diag_row(p, k).start()
            diag_own(p).start()

    load = pltpu.make_async_copy(held, r1, load_sem)
    load.start()

    def b_copy(i):
        return remote(
            col.at[i], grid.at[i // R, r], b_send.at[i], b_recv.at[i // R, r], lax.rem(i, R), c
        )

    def own_in(jl):
        return pltpu.make_async_copy(col.at[jl * R + r], stage.at[jl], st_in.at[jl])

    def own_out(jl):
        return pltpu.make_async_copy(stage.at[jl], grid.at[jl, r], st_out.at[jl])

    def own_blocks(body):
        def run(jl):
            @pl.when(jl * R + r >= i0)
            def _():
                body(jl)

        over(0, C, run)

    def sent_blocks(low, high, body):
        def run(i):
            @pl.when(lax.rem(i, R) != r)
            def _():
                body(i)

        over(low, high, run)

    own_blocks(lambda jl: own_in(jl).start())

    def own_turn(jl):
        own_in(jl).wait()
        own_out(jl).start()

    own_blocks(own_turn)

    load.wait()

    for p in range(2):

        @pl.when(c == pieces[p][0])
        def _():
            diag_own(p).wait()
            for k in range(1, X):
                diag_x(p, k).start()

    def second(k):
        to = lax.rem(r + k, R)
        return remote(s2.at[to], r2.at[pl.ds(r * cap2, cap2)], p2_send.at[k], p2_recv.at[r], to, c)

    def second_wait(k):
        src = lax.rem(r + k, R)
        remote(s2.at[0], r2.at[pl.ds(src * cap2, cap2)], p2_send.at[0], p2_recv.at[src], r, c).wait_recv()

    def pack2(k):
        to = lax.rem(r + k, R)

        def run(n):
            for u in range(PACK):
                s2[to, n * PACK + u] = r1[index2[to * cap2 + n * PACK + u]]

        over(0, cap2 // PACK, run)

    for k in range(1, R):
        pack2(k)
        if k > 1:
            second(k - 1).start()

    def pack2_own(n):
        for u in range(PACK):
            r2[r * cap2 + n * PACK + u] = r1[index2[r * cap2 + n * PACK + u]]

    over(0, cap2 // PACK, pack2_own)
    second(R - 1).start()

    @pl.when(y == 0)
    def _():
        for p in range(2):

            @pl.when(c != pieces[p][0])
            def _():
                _, at, n = pieces[p]
                here = diag.at[pl.ds(at, n)]
                remote(here, here, dx_send.at[0], dx_recv.at[p], r, c).wait_recv()

        for k in range(1, X):
            diag_y(k).start()

    for k in range(1, R):
        second_wait(k)

    owned = ((0, 1), (1, 2))

    def mine_own_rows(p):
        at, n = owned[p]
        return mine.at[pl.ds(at, n)]

    def mine_row(p, k):
        here = mine_own_rows(p)
        return remote(here, here, m_send.at[k], m_recv.at[p], lax.rem(r + k, R), c)

    for p in range(2):

        @pl.when(r == p)
        def _():
            at, n = owned[p]
            zero = jnp.zeros(mine.shape[1:], F32)

            def run(k, sums):
                for u in range(PACK):
                    slot = k * PACK + u
                    sums = tuple(
                        total + pick[b * R * cap2 + slot] * r2[slot] for b, total in enumerate(sums)
                    )
                return sums

            sums = lax.fori_loop(0, R * cap2 // PACK, run, (zero,) * n)
            for b in range(n):
                mine[at + b] = sums[b]
            for k in range(1, R):
                mine_row(p, k).start()

    for p in range(2):

        @pl.when(r != p)
        def _():
            here = mine_own_rows(p)
            remote(here, here, m_send.at[0], m_recv.at[p], r, c).wait_recv()

    def mine_col(k):
        to = lax.rem(c + k, C)
        return remote(mine, parts.at[c], g_send.at[k], g_recv.at[c], r, to)

    for k in range(1, C):
        mine_col(k).start()
    parts[c] = mine[...]
    sent_blocks(i0, NB, lambda i: b_copy(i).start())


    part3 = PACK * 4

    def third(k, h):
        to = lax.rem(c + k, C)
        at = pl.ds(h * part3, part3)
        return remote(s3.at[to, at], out.at[c, at], p3_send.at[k, h], p3_recv.at[c, h], r, to)

    def third_wait(k, h):
        src = lax.rem(c + k, C)
        at = pl.ds(h * part3, part3)
        remote(s3.at[0, at], out.at[src, at], p3_send.at[0, h], p3_recv.at[src, h], r, c).wait_recv()

    kept = pl.ds(0, parts3 * part3)
    third_own = pltpu.make_async_copy(s3.at[c, kept], out.at[c, kept], p3_recv.at[c, 0])

    def pack3(k, h):
        to = lax.rem(c + k, C)

        def run(n):
            for u in range(PACK):
                at = h * part3 + n * PACK + u
                s3[to, at] = r2[index3[to * cap3 + at]]

        over(0, part3 // PACK, run)

    def third_part(h):
        def step(k):
            pack3(k, h)

            @pl.when(k > 1)
            def _():
                third(k - 1, h).start()

        over(1, C, step)
        pack3(C, h)
        third(C - 1, h).start()

    over(0, parts3, third_part)

    @pl.when(y != 0)
    def _():
        remote(diag, diag, dy_send.at[0], dy_recv.at[0], r, c).wait_recv()

    sub = mine.shape[1]

    def part_wait(q):
        @pl.when(q != c)
        def _():
            remote(mine, parts.at[q], g_send.at[0], g_recv.at[q], r, c).wait_recv()

    over(0, C, part_wait)
    for k in range(1, X):

        @pl.when(y == 0)
        def _():
            diag_y(k).wait_send()

    for p in range(2):

        @pl.when(c == pieces[p][0])
        def _():
            for k in range(1, X):
                diag_x(p, k).wait_send()

    rows = lax.broadcasted_iota(jnp.int32, (EDGE, EDGE), 0)
    cols = lax.broadcasted_iota(jnp.int32, (EDGE, EDGE), 1)
    eye = (rows == cols).astype(F32)
    for q in range(C):
        for b in range(3):
            at = pl.ds(q * sub, sub)
            diag[b, at, :] = diag[b, at, :] + parts[q, b]

    def pivot(block, at):
        work[:, :EDGE] = jnp.where(rows >= cols, block, block.T)
        work[:, EDGE:] = eye
        factor(work, upper)
        low[at] = jnp.where(rows >= cols, upper[:, :EDGE].T, 0.0)
        low[at + 1] = jnp.where(rows >= cols, upper[:, EDGE:], 0.0)

    pivot(diag[0], 0)
    low[2] = dot(diag[1], low[1], NT)
    pivot(diag[2] - dot(low[2], low[2], NT), 3)
    low_copy = pltpu.make_async_copy(low, low_out, low_sem)
    low_copy.start()

    own_blocks(lambda jl: own_out(jl).wait())
    for s in range(R):
        begin = start_of(s * C + c)

        def run(jl):
            @pl.when((r != s) & (jl * R + r >= begin))
            def _():
                remote(col.at[0], grid.at[jl, s], b_send.at[0], b_recv.at[jl, s], r, c).wait_recv()

        over(0, C, run)
    third_own.start()
    sent_blocks(i0, NB, lambda i: b_copy(i).wait_send())
    for k in range(1, R):
        second(k).wait_send()
    for h in range(parts3):
        for k in range(1, C):
            third_wait(k, h)
        for k in range(1, C):
            third(k, h).wait_send()
    third_own.wait()
    low_copy.wait()
    for p in range(2):

        @pl.when((r == 0) & (c == pieces[p][0]))
        def _():
            for k in range(1, R):
                diag_row(p, k).wait_send()

        @pl.when(r == p)
        def _():
            for k in range(1, R):
                mine_row(p, k).wait_send()

    for k in range(1, C):
        mine_col(k).wait_send()


def spread(R, C, cap2, cap3, parts3, name, held, index2, index3, pick, front):
    hbm = pl.BlockSpec(memory_space=pltpu.HBM)
    smem = pl.BlockSpec(memory_space=pltpu.SMEM)
    dma = pltpu.SemaphoreType.DMA
    sub = held.shape[1]
    return pl.pallas_call(
        functools.partial(spread_kernel, R, C, cap2, cap3, parts3),
        in_specs=[hbm, smem, smem, smem, hbm],
        out_specs=[hbm, hbm, hbm],
        out_shape=[
            jax.ShapeDtypeStruct((C, R, EDGE, EDGE), F32),
            jax.ShapeDtypeStruct((C, cap3, sub, EDGE), F32),
            jax.ShapeDtypeStruct((5, EDGE, EDGE), F32),
        ],
        scratch_shapes=[
            pltpu.VMEM(held.shape, F32),
            pltpu.VMEM((R, cap2, sub, EDGE), F32),
            pltpu.VMEM((R * cap2, sub, EDGE), F32),
            pltpu.VMEM((C, cap3, sub, EDGE), F32),
            pltpu.VMEM((C, EDGE, EDGE), F32),
            pltpu.VMEM((3, EDGE, EDGE), F32),
            pltpu.VMEM((3, sub, EDGE), F32),
            pltpu.VMEM((C, 3, sub, EDGE), F32),
            pltpu.VMEM((EDGE, 2 * EDGE), F32),
            pltpu.VMEM((EDGE, 2 * EDGE), F32),
            pltpu.VMEM((5, EDGE, EDGE), F32),
            dma((R,)), dma((2,)), dma((C,)), dma((2,)), dma((C,)), dma((1,)),
            dma((R,)), dma((2,)), dma((C,)), dma((C,)), dma,
            dma((C,)), dma((C,)), dma((R * C,)), dma((C, R)),
            dma, dma((R,)), dma((R,)), dma((C, parts3)), dma((C, parts3)),
        ],
        compiler_params=pltpu.CompilerParams(
            collective_id=name, has_side_effects=True, vmem_limit_bytes=60 << 20
        ),
        name="spread",
    )(held, index2, index3, pick, front)


def slab_kernel(C, landing, grid, arrived, out, tile, sem):
    out[...] = grid[:, 0]
    slots = arrived.shape[1]

    def run(k):
        @pl.when(landing[1 + slots + k] == 0)
        def _():
            copy = pltpu.make_async_copy(arrived.at[:, k], tile, sem)
            copy.start()
            copy.wait()
            jl = landing[1 + k]
            out[jl] = out[jl] + tile[...].reshape(EDGE, EDGE)

    @pl.when(landing[0] < 2)
    def _():
        over(0, slots, run)


def slab_of(C, landing, grid, arrived):
    return pl.pallas_call(
        functools.partial(slab_kernel, C),
        grid=(1,),
        in_specs=[
            pl.BlockSpec(memory_space=pltpu.SMEM),
            pl.BlockSpec((C, 1, EDGE, EDGE), lambda t: (0, 0, 0, 0)),
            pl.BlockSpec(memory_space=pltpu.HBM),
        ],
        out_specs=pl.BlockSpec((C, EDGE, EDGE), lambda t: (0, 0, 0)),
        out_shape=jax.ShapeDtypeStruct((C, EDGE, EDGE), F32),
        scratch_shapes=[pltpu.VMEM((arrived.shape[0], EDGE // C, EDGE), F32), pltpu.SemaphoreType.DMA],
        compiler_params=pltpu.CompilerParams(vmem_limit_bytes=60 << 20),
        name="slab",
    )(landing, grid, arrived)


def panel_kernel(
    R, C, slab, low, qrow, qcol,
    chunk, rows_q, zbuf, cols_q,
    sc_send, ck_recv, ag_send, ag_recv, z_send, z_recv, v_send, v_recv, q_sem,
):
    r = lax.axis_index("row")
    c = lax.axis_index("col")
    ratio = C // R
    greet(R, C, r, c)

    def scatter(jl, k):
        return remote(slab.at[jl], chunk.at[k], sc_send.at[jl], ck_recv.at[k], r, jl)

    def scatter_own(jl, k):
        return pltpu.make_async_copy(slab.at[jl], chunk.at[k], ck_recv.at[k])

    for k in range(2):

        @pl.when(c == k)
        def _():
            for jl in range(C):
                if jl == k:
                    scatter_own(jl, k).start()
                else:
                    scatter(jl, k).start()

    i = c * R + r
    scatter_own(0, 0).wait()
    q0 = dot(chunk[0], low[1], NT)
    scatter_own(0, 1).wait()
    q1 = dot(chunk[1] - dot(q0, low[2], NT), low[4], NT)
    rows_q[0, c] = jnp.where(i == 0, low[0], jnp.where(i == 1, low[2], q0))
    rows_q[1, c] = jnp.where(i == 0, 0.0, jnp.where(i == 1, low[3], q1))

    def gather(k, n):
        here = rows_q.at[n, c]
        return remote(here, here, ag_send.at[n, k], ag_recv.at[n, c], r, lax.rem(c + k, C))

    def along(k, n):
        return remote(
            rows_q.at[n, c], zbuf.at[n, r], z_send.at[n, k], z_recv.at[n, r], lax.rem(r + k, R), c
        )

    for n in range(2):
        for k in range(1, R):
            along(k, n).start()
    for n in range(2):
        for k in range(1, C):
            gather(k, n).start()

    mine = lax.rem(c, ratio) * R
    place = c // ratio

    def serve(p, n):
        return remote(
            zbuf.at[n, p], cols_q.at[n, place], v_send.at[n, p], v_recv.at[n, place], r, mine + p
        )

    def serve_own(p, n):
        return pltpu.make_async_copy(zbuf.at[n, p], cols_q.at[n, place], v_recv.at[n, place])

    own_z = [pltpu.make_async_copy(rows_q.at[n, c], zbuf.at[n, r], z_recv.at[n, r]) for n in range(2)]
    for copy in own_z:
        copy.start()
    for copy in own_z:
        copy.wait()

    def pass_on(p):
        for n in range(2):

            @pl.when(p != r)
            def _():
                remote(rows_q.at[n, 0], zbuf.at[n, p], z_send.at[n, 0], z_recv.at[n, p], r, c).wait_recv()

            @pl.when(mine + p == c)
            def _():
                serve_own(p, n).start()

            @pl.when(mine + p != c)
            def _():
                serve(p, n).start()

    over(0, R, pass_on)

    def row_wait(jl):
        @pl.when(jl != c)
        def _():
            for n in range(2):
                here = rows_q.at[n, jl]
                remote(here, here, ag_send.at[n, 0], ag_recv.at[n, jl], r, c).wait_recv()

    over(0, C, row_wait)
    keep_row = pltpu.make_async_copy(rows_q, qrow, q_sem.at[1])
    keep_row.start()

    def col_wait(s):
        for n in range(2):
            pltpu.make_async_copy(zbuf.at[n, 0], cols_q.at[n, s], v_recv.at[n, s]).wait()

    over(0, R, col_wait)
    keep_col = pltpu.make_async_copy(cols_q, qcol, q_sem.at[0])
    keep_col.start()

    for k in range(2):

        @pl.when(c == k)
        def _():
            for jl in range(C):
                if jl != k:
                    scatter(jl, k).wait_send()

    for n in range(2):
        for k in range(1, C):
            gather(k, n).wait_send()
        for k in range(1, R):
            along(k, n).wait_send()

    def served(p):
        @pl.when(mine + p != c)
        def _():
            for n in range(2):
                serve(p, n).wait_send()

    over(0, R, served)
    keep_col.wait()
    keep_row.wait()


def panels(R, C, slab, low):
    hbm = pl.BlockSpec(memory_space=pltpu.HBM)
    dma = pltpu.SemaphoreType.DMA
    return pl.pallas_call(
        functools.partial(panel_kernel, R, C),
        in_specs=[hbm, pl.BlockSpec(memory_space=pltpu.VMEM)],
        out_specs=[hbm, hbm],
        out_shape=[
            jax.ShapeDtypeStruct((2, C, EDGE, EDGE), F32),
            jax.ShapeDtypeStruct((2, R, EDGE, EDGE), F32),
        ],
        scratch_shapes=[
            pltpu.VMEM((2, EDGE, EDGE), F32),
            pltpu.VMEM((2, C, EDGE, EDGE), F32),
            pltpu.VMEM((2, R, EDGE, EDGE), F32),
            pltpu.VMEM((2, R, EDGE, EDGE), F32),
            dma((C,)), dma((2,)), dma((2, C)), dma((2, C)),
            dma((2, R)), dma((2, R)), dma((2, R)), dma((2, R)), dma((2,)),
        ],
        compiler_params=pltpu.CompilerParams(
            collective_id=1, has_side_effects=True, vmem_limit_bytes=60 << 20
        ),
        name="panels",
    )(slab, low)


def halves(x):
    high = x.astype(BF16)
    return high, (x - high.astype(F32)).astype(BF16)


def update_kernel(R, C, place, landing, grid, qrow, qcol, arrived, out, left, right, head, follow):
    s = pl.program_id(0)
    slots = arrived.shape[1]
    r, c = place[0], place[1]
    j = s * C + c
    rows = lax.broadcasted_iota(jnp.int32, (EDGE, EDGE), 0)
    cols = lax.broadcasted_iota(jnp.int32, (EDGE, EDGE), 1)

    @pl.when(s == 0)
    def _():
        def clear(k):
            head[k] = -1

        over(0, R, clear)

        def link(k):
            where = landing[1 + slots + k]

            @pl.when(where >= 0)
            def _():
                follow[k] = head[where]
                head[where] = k

        over(0, slots, link)

        def split(jl):
            at = pl.ds(pl.multiple_of(jl * EDGE, EDGE), EDGE)
            for n in range(2):
                high, low = halves(qrow[n, jl])
                for m, part in ((0, high), (2, high), (4, low)):
                    left[at, (m + n) * EDGE : (m + n + 1) * EDGE] = part

        over(0, C, split)

    for n in range(2):
        high, low = halves(qcol[n, 0])
        for m, part in ((0, high.T), (2, low.T), (4, high.T)):
            right[(m + n) * EDGE : (m + n + 1) * EDGE, :] = part

    many = min(4, C)
    for g in range(C // many):
        last = (g * many + many - 1) * R + r

        @pl.when((last >= j) & (j >= 2))
        def _():
            product = dot16(left[g * many * EDGE : (g + 1) * many * EDGE, :], right[...], NN)
            for u in range(many):
                out[g * many + u, 0] = grid[g * many + u, 0] - product[u * EDGE : (u + 1) * EDGE, :]

    @pl.when(j < 2)
    def _():
        for jl in range(C):
            out[jl, 0] = jnp.where(j == 0, qrow[0, jl], qrow[1, jl])

    def more(k):
        return k >= 0

    def add(k):
        jl = landing[1 + k]
        out[jl, 0] = out[jl, 0] + arrived[:, k].reshape(EDGE, EDGE)
        return follow[k]

    lax.while_loop(more, add, jnp.where(j >= 2, head[s], -1))
    for jl in range(C):
        i = jl * R + r

        @pl.when(i < j)
        def _():
            out[jl, 0] = jnp.zeros((EDGE, EDGE), F32)

        @pl.when((i == j) & (j >= 2))
        def _():
            out[jl, 0] = jnp.where(rows >= cols, out[jl, 0], 0.0)


def update(R, C, place, landing, grid, qrow, qcol, arrived):
    cap3 = arrived.shape[1]
    block = pl.BlockSpec((C, 1, EDGE, EDGE), lambda s, *_: (0, s, 0, 0))
    return pl.pallas_call(
        functools.partial(update_kernel, R, C),
        grid_spec=pltpu.PrefetchScalarGridSpec(
            num_scalar_prefetch=2,
            grid=(R,),
            in_specs=[
                block,
                pl.BlockSpec((2, C, EDGE, EDGE), lambda s, *_: (0, 0, 0, 0)),
                pl.BlockSpec((2, 1, EDGE, EDGE), lambda s, *_: (0, s, 0, 0)),
                pl.BlockSpec(arrived.shape, lambda s, *_: (0, 0, 0, 0), pipeline_mode=pl.Buffered(1)),
            ],
            out_specs=block,
            scratch_shapes=[
                pltpu.VMEM((C * EDGE, 6 * EDGE), BF16),
                pltpu.VMEM((6 * EDGE, EDGE), BF16),
                pltpu.SMEM((R,), jnp.int32),
                pltpu.SMEM((cap3,), jnp.int32),
            ],
        ),
        out_shape=jax.ShapeDtypeStruct((C, R, EDGE, EDGE), F32),
        compiler_params=pltpu.CompilerParams(vmem_limit_bytes=60 << 20),
        name="update",
    )(place, landing, grid, qrow, qcol, arrived)


def capacities(R, C, T):
    if T < 32:
        return 16, (PACK * 4, PACK * 8)
    return 104, (80, 96, 128)


def hot(values, count):
    return (values[..., None] == jnp.arange(count, dtype=jnp.int32)).astype(BF16)


def before(marks):
    n = marks.shape[-2]
    serial = jnp.arange(n, dtype=jnp.int32)
    lower = (serial[:, None] > serial[None, :]).astype(BF16)
    return jnp.einsum("pq,...qk->...pk", lower, marks, preferred_element_type=F32)


def local(front_entries, child_updates, row_maps, col_maps, target_columns, row_offsets):
    R = lax.axis_size("row")
    C = lax.axis_size("col")
    count = R * C
    T = child_updates.shape[0]
    cap2, choices = capacities(R, C, T)
    cap3 = choices[-1]
    my_row = lax.axis_index("row").astype(jnp.int32)
    my_col = lax.axis_index("col").astype(jnp.int32)

    told = jnp.concatenate([target_columns[:, 0], row_offsets[:, 0]])
    told = jnp.pad(told, (0, EDGE - 2 * T)).reshape(1, EDGE)
    held, told = begin(R, C, child_updates, row_maps, col_maps, told)
    told = told.reshape(C, R, EDGE).transpose(1, 0, 2).reshape(count, EDGE)
    columns, offsets = told[:, :T], told[:, T : 2 * T]
    target_rows = columns + offsets % (count - columns)
    columns = columns.reshape(R, C * T)
    target_rows = target_rows.reshape(R, C * T)
    to_row, to_col = target_rows % R, columns % C

    row_hot = hot(to_row, R)
    pivotal = (target_rows < 2) & (columns < 2)
    lead = row_hot * pivotal[..., None].astype(BF16)
    rest = row_hot - lead
    leads = jnp.sum(lead.astype(F32), axis=1, keepdims=True)
    rank2 = before(lead) * lead.astype(F32) + (before(rest) + leads) * rest.astype(F32)
    rank2 = jnp.sum(rank2, axis=-1).astype(jnp.int32)
    mine = to_row == my_row
    col_hot = hot(jnp.where(mine, to_col, -1), C)
    inside = before(col_hot)
    totals = jnp.sum(col_hot.astype(F32), axis=1)
    planes = jnp.arange(R, dtype=jnp.int32)
    ahead = jnp.sum(jnp.where((planes[:, None] > planes[None, :])[..., None], totals[None], 0.0), axis=1)
    rank3 = jnp.sum((inside + ahead[:, None, :]) * col_hot.astype(F32), axis=-1).astype(jnp.int32)
    loads2 = jnp.sum(row_hot.astype(F32), axis=1)
    loads3 = jnp.einsum("pqk,pql->kl", row_hot, hot(to_col, C), preferred_element_type=F32)
    passes2 = (jnp.max(loads2).astype(jnp.int32) + cap2 - 1) // cap2
    most3 = jnp.max(loads3).astype(jnp.int32)
    passes3 = (most3 + cap3 - 1) // cap3

    def tables(a, b):
        own_hot = lax.dynamic_index_in_dim(row_hot, my_row, 0, keepdims=False)
        own_rank = lax.dynamic_index_in_dim(rank2, my_row, 0, keepdims=False)
        serial = jnp.arange(C * T, dtype=jnp.int32)
        values = jnp.stack([serial // T, serial % T], axis=0).astype(BF16)
        marked = values[:, :, None] * own_hot[None]
        found = jnp.einsum("vqk,qn->vkn", marked, hot(own_rank - a * cap2, cap2), preferred_element_type=F32)
        found = found.astype(jnp.int32)
        index2 = (found[0] * T + found[1]).reshape(-1)
        place2 = rank2 - a * cap2
        active = (place2 >= 0) & (place2 < cap2) & mine
        source = jnp.broadcast_to(planes[:, None], (R, C * T))
        values = jnp.stack(
            [source, place2, target_rows // R, columns // C, jnp.ones_like(source)], axis=0
        )
        values = jnp.where(active, values, 0).astype(BF16)
        marked = values[..., None] * col_hot[None]
        found = jnp.einsum(
            "vpqk,pqn->vkn", marked, hot(rank3 - b * cap3, cap3), preferred_element_type=F32
        ).astype(jnp.int32)
        index3 = (found[0] * cap2 + found[1]).reshape(-1)
        here = lax.dynamic_index_in_dim(found, my_col, 1, keepdims=False)
        return index2, index3, here[2], here[3], here[4]

    index2, index3, land_row, land_col, valid = tables(0, 0)
    marks = jnp.stack([mine & pivotal & (columns == k) & (rank2 < cap2) for k in range(2)])
    pick = jnp.einsum("vpq,pqn->vpn", marks.astype(BF16), hot(rank2, cap2), preferred_element_type=F32)
    runs = [
        functools.partial(spread, R, C, cap2, cap3, size // (PACK * 4), 10 + at)
        for at, size in enumerate(choices)
    ]
    choice = sum((most3 > size).astype(jnp.int32) for size in choices[:-1])
    grid, arrived, low = lax.switch(
        choice, runs, held, index2, index3, pick.reshape(-1), front_entries.reshape(count, EDGE, EDGE)
    )

    def another(carry):
        p, grid = carry
        index2, index3, land_row, land_col, valid = tables(p // passes3, p % passes3)
        moved = held[index2].reshape(R, cap2, EDGE // C, EDGE)
        moved = lax.all_to_all(moved, "row", split_axis=0, concat_axis=0, tiled=True)
        moved = moved.reshape((R * cap2, EDGE // C, EDGE))[index3].reshape(C, cap3, EDGE // C, EDGE)
        moved = lax.all_to_all(moved, "col", split_axis=0, concat_axis=0, tiled=True)
        tiles = moved.transpose(1, 0, 2, 3).reshape(cap3, EDGE, EDGE)
        tiles = jnp.where((valid > 0)[:, None, None], tiles, 0.0)
        return p + 1, grid.at[land_row, land_col].add(tiles)

    _, grid = lax.while_loop(lambda carry: carry[0] < passes2 * passes3, another, (jnp.int32(1), grid))

    landing = jnp.concatenate([my_col[None], land_row, jnp.where(valid > 0, land_col, -1)])
    slab = slab_of(C, landing, grid, arrived)
    qrow, qcol = panels(R, C, slab, low)
    place = jnp.stack([my_row, my_col])
    result = update(R, C, place, landing, grid, qrow, qcol, arrived)
    return result.reshape(C, 1, R, 1, EDGE, EDGE)


def solution(mesh):
    return jax.shard_map(
        local,
        mesh=mesh,
        in_specs=(
            P(None, ("row", "col")),
            P(("row", "col"), None, None),
            P(("row", "col"), None),
            P(("row", "col"), None),
            P(("row", "col"), None),
            P(("row", "col"), None),
        ),
        out_specs=P(None, "row", None, "col", None, None),
        check_vma=False,
    )
```

```python
import functools
import math

import jax
import jax.numpy as jnp
from jax import lax
from jax.experimental import pallas as pl
from jax.experimental.pallas import tpu as pltpu
from jax.sharding import PartitionSpec as P

EDGE = 128
MESH = pl.DeviceIdType.MESH
PRECISE = lax.Precision.HIGHEST
F32 = jnp.float32
BF16 = jnp.bfloat16
NN = ((1,), (0,))
NT = ((1,), (1,))
TN = ((0,), (0,))


def dot(a, b, dims):
    return lax.dot_general(a, b, (dims, ((), ())), precision=PRECISE, preferred_element_type=F32)


def dot16(a, b, dims):
    return lax.dot_general(a, b, (dims, ((), ())), preferred_element_type=F32)


def remote(src, dst, ss, rs, rr, cc):
    return pltpu.make_async_remote_copy(
        src_ref=src, dst_ref=dst, send_sem=ss, recv_sem=rs, device_id=(rr, cc), device_id_type=MESH
    )


def over(low, high, body):
    def run(i, _):
        body(i)
        return 0

    lax.fori_loop(low, high, run, 0)


def greet(R, C, r, c):
    barrier = pltpu.get_barrier_semaphore()
    for k in range(1, R):
        pl.semaphore_signal(barrier, inc=1, device_id=(lax.rem(r + k, R), c), device_id_type=MESH)
    for k in range(1, C):
        pl.semaphore_signal(barrier, inc=1, device_id=(r, lax.rem(c + k, C)), device_id_type=MESH)
    pl.semaphore_wait(barrier, R + C - 2)


PARTS = 4
GROUP = 4


def begin_kernel(
    R, C, tiles, row_map, col_map, told, col, r1, told_all, slab,
    held, placed, told_row, stage,
    st_in, st_out, f_send, f_recv, t_sem, tr_send, tr_recv, tc_send, tc_recv, send, recv,
):
    r = lax.axis_index("row")
    c = lax.axis_index("col")
    T = tiles.shape[0]
    sub = EDGE // C
    part = T // PARTS
    load = pltpu.make_async_copy(tiles, held, t_sem)
    load.start()
    greet(R, C, r, c)

    def tell_row(k):
        return remote(told, told_row.at[r], tr_send.at[k], tr_recv.at[r], lax.rem(r + k, R), c)

    def tell_col(k):
        return remote(told_row, told_all.at[c], tc_send.at[k], tc_recv.at[c], r, lax.rem(c + k, C))

    tell_own = pltpu.make_async_copy(told, told_row.at[r], tr_recv.at[r])
    tell_own.start()
    for k in range(1, R):
        tell_row(k).start()

    def ahead(i):
        return remote(col.at[i], slab.at[i // R], f_send.at[i], f_recv.at[i // R], lax.rem(i, R), c)

    def others(body):
        def run(i):
            @pl.when(lax.rem(i, R) != 0)
            def _():
                body(i)

        over(0, R * C, run)

    def own_in(jl):
        return pltpu.make_async_copy(col.at[jl * R], stage.at[jl], st_in.at[jl])

    def own_out(jl):
        return pltpu.make_async_copy(stage.at[jl], slab.at[jl], st_out.at[jl])

    panel = (r == 0) & (c < 2)

    @pl.when(panel)
    def _():
        over(0, C, lambda jl: own_in(jl).start())
        others(lambda i: ahead(i).start())

    levels = lax.broadcasted_iota(jnp.int32, (EDGE, EDGE), 0)

    def place(t):
        for g in range(GROUP):
            k = t * GROUP + g
            col_hot = (levels == col_map[pl.ds(k, 1), :]).astype(F32).astype(BF16)
            row_hot = (levels == row_map[pl.ds(k, 1), :]).astype(F32).astype(BF16)
            x = held[k]
            first = x.astype(BF16)
            rest = x - first.astype(F32)
            second = rest.astype(BF16)
            third = (rest - second.astype(F32)).astype(BF16)
            moved = [dot16(p, col_hot, NT).astype(BF16) for p in (first, second, third)]
            full = (dot16(row_hot, moved[0], NN) + dot16(row_hot, moved[1], NN)) + dot16(
                row_hot, moved[2], NN
            )
            for q in range(C):
                placed[q, k] = full[q * sub : (q + 1) * sub, :]

    def slices(k, h):
        to = lax.rem(c + k, C)
        return remote(
            placed.at[to, pl.ds(h * part, part)], r1.at[pl.ds(c * T + h * part, part)],
            send.at[k, h], recv.at[c, h], r, to,
        )

    def slices_wait(k, h):
        src = lax.rem(c + k, C)
        remote(
            placed.at[0, pl.ds(0, part)], r1.at[pl.ds(src * T + h * part, part)],
            send.at[0, h], recv.at[src, h], r, c,
        ).wait_recv()

    load.wait()
    for h in range(PARTS):
        over(h * part // GROUP, (h + 1) * part // GROUP, place)
        if h == 0:
            tell_own.wait()
            for k in range(1, R):
                src = lax.rem(r + k, R)
                remote(told, told_row.at[src], tr_send.at[0], tr_recv.at[src], r, c).wait_recv()
            for k in range(1, C):
                tell_col(k).start()
            tell_kept = pltpu.make_async_copy(told_row, told_all.at[c], tc_recv.at[c])
            tell_kept.start()
        for k in range(1, C):
            slices(k, h).start()
    own = pltpu.make_async_copy(placed.at[c], r1.at[pl.ds(c * T, T)], recv.at[c, 0])
    own.start()

    @pl.when(panel)
    def _():
        def turn(jl):
            own_in(jl).wait()
            own_out(jl).start()

        over(0, C, turn)
        over(0, C, lambda jl: own_out(jl).wait())
        others(lambda i: ahead(i).wait_send())

    @pl.when((r != 0) & (c < 2))
    def _():
        def landed(jl):
            remote(col.at[0], slab.at[jl], f_send.at[0], f_recv.at[jl], r, c).wait_recv()

        over(0, C, landed)

    tell_kept.wait()
    for k in range(1, C):
        src = lax.rem(c + k, C)
        remote(told_row, told_all.at[src], tc_send.at[0], tc_recv.at[src], r, c).wait_recv()
    for h in range(PARTS):
        for k in range(1, C):
            slices_wait(k, h)
    own.wait()
    for k in range(1, R):
        tell_row(k).wait_send()
    for k in range(1, C):
        tell_col(k).wait_send()
    for h in range(PARTS):
        for k in range(1, C):
            slices(k, h).wait_send()


def begin(R, C, tiles, row_map, col_map, told, front):
    hbm = pl.BlockSpec(memory_space=pltpu.HBM)
    vmem = pl.BlockSpec(memory_space=pltpu.VMEM)
    dma = pltpu.SemaphoreType.DMA
    T, sub = tiles.shape[0], EDGE // C
    return pl.pallas_call(
        functools.partial(begin_kernel, R, C),
        in_specs=[hbm, vmem, vmem, hbm, hbm],
        out_specs=[hbm, hbm, hbm],
        out_shape=[
            jax.ShapeDtypeStruct((C * T, sub, EDGE), F32),
            jax.ShapeDtypeStruct((C, R, 1, EDGE), jnp.int32),
            jax.ShapeDtypeStruct((C, EDGE, EDGE), F32),
        ],
        scratch_shapes=[
            pltpu.VMEM((T, EDGE, EDGE), F32),
            pltpu.VMEM((C, T, sub, EDGE), F32),
            pltpu.VMEM((R, 1, EDGE), jnp.int32),
            pltpu.VMEM((C, EDGE, EDGE), F32),
            dma((C,)), dma((C,)), dma((R * C,)), dma((C,)),
            dma, dma((R,)), dma((R,)), dma((C,)), dma((C,)), dma((C, PARTS)), dma((C, PARTS)),
        ],
        compiler_params=pltpu.CompilerParams(
            collective_id=4, has_side_effects=True, vmem_limit_bytes=60 << 20
        ),
        name="begin",
    )(tiles, row_map, col_map, told, front)


STEP = 8


def factor(work, upper):
    rows8 = lax.broadcasted_iota(jnp.int32, (STEP, 1), 0)
    lanes = lax.broadcasted_iota(jnp.int32, (STEP, EDGE), 1)

    def block(b, _):
        first = pl.multiple_of(b * STEP, STEP)
        x = work[pl.ds(first, STEP), :]
        d = pltpu.roll(x[:, :EDGE], lax.rem(EDGE - first, EDGE), 1)
        for t in range(STEP):
            pivot = d[t : t + 1, t : t + 1]
            scale = lax.rsqrt(pivot)
            ratio = d[:, t : t + 1] / pivot
            ratio = jnp.where(rows8 > t, ratio, jnp.where(rows8 == t, 1.0 - scale, 0.0))
            x = x - ratio * x[t : t + 1, :]
            d = d - ratio * d[t : t + 1, :]
        upper[pl.ds(first, STEP), :] = x
        left = jnp.where(lanes >= first + STEP, x[:, :EDGE], 0.0)
        work[...] = work[...] - dot(left, x, TN)
        return 0

    lax.fori_loop(0, EDGE // STEP, block, 0)


PACK = 4


def spread_kernel(
    R, C, cap2, cap3, parts3, held, index2, index3, pick, chosen, slab, col, grid, out, low_out, chunk_out,
    r1, s2, r2, s3, stage, chunk, sums, child, c_send, ck_recv, ch_send, ch_recv, chunk_sem, diag, mine, parts, work, upper, low,
    dr_send, dr_recv, dx_send, dx_recv, dy_send, dy_recv, m_send, m_recv, g_send, g_recv, low_sem,
    st_in, st_out, b_send, b_recv, load_sem, p2_send, p2_recv, p3_send, p3_recv,
):
    r = lax.axis_index("row")
    c = lax.axis_index("col")
    NB = R * C
    start_of = lambda column: jnp.where(column < 2, NB, column)
    i0 = start_of(r * C + c)
    X = math.isqrt(C)
    x, y = lax.rem(c, X), c // X
    greet(R, C, r, c)

    pieces = ((0, 0, 2), (1, 2, 1))

    def diag_row(p, k):
        owner, at, n = pieces[p]
        return remote(
            col.at[pl.ds(owner, n)], diag.at[pl.ds(at, n)], dr_send.at[k], dr_recv.at[p], lax.rem(r + k, R), c
        )

    def diag_own(p):
        owner, at, n = pieces[p]
        return pltpu.make_async_copy(col.at[pl.ds(owner, n)], diag.at[pl.ds(at, n)], dr_recv.at[p])

    def diag_x(p, k):
        _, at, n = pieces[p]
        here = diag.at[pl.ds(at, n)]
        return remote(here, here, dx_send.at[k], dx_recv.at[p], r, lax.rem(x + k, X))

    def diag_y(k):
        return remote(diag, diag, dy_send.at[k], dy_recv.at[0], r, k * X + x)

    for p in range(2):

        @pl.when((r == 0) & (c == pieces[p][0]))
        def _():
            for k in range(1, R):
                diag_row(p, k).start()
            diag_own(p).start()

    load = pltpu.make_async_copy(held, r1, load_sem)
    load.start()

    def b_copy(i):
        return remote(
            col.at[i], grid.at[i // R, r], b_send.at[i], b_recv.at[i // R, r], lax.rem(i, R), c
        )

    def own_in(jl):
        return pltpu.make_async_copy(col.at[jl * R + r], stage.at[jl], st_in.at[jl])

    def own_out(jl):
        return pltpu.make_async_copy(stage.at[jl], grid.at[jl, r], st_out.at[jl])

    def own_blocks(body):
        def run(jl):
            @pl.when(jl * R + r >= i0)
            def _():
                body(jl)

        over(0, C, run)

    def sent_blocks(low, high, body):
        def run(i):
            @pl.when(lax.rem(i, R) != r)
            def _():
                body(i)

        over(low, high, run)

    own_blocks(lambda jl: own_in(jl).start())

    def own_turn(jl):
        own_in(jl).wait()
        own_out(jl).start()

    own_blocks(own_turn)

    load.wait()

    for p in range(2):

        @pl.when(c == pieces[p][0])
        def _():
            diag_own(p).wait()
            for k in range(1, X):
                diag_x(p, k).start()

    def second(k):
        to = lax.rem(r + k, R)
        return remote(s2.at[to], r2.at[pl.ds(r * cap2, cap2)], p2_send.at[k], p2_recv.at[r], to, c)

    def second_wait(k):
        src = lax.rem(r + k, R)
        remote(s2.at[0], r2.at[pl.ds(src * cap2, cap2)], p2_send.at[0], p2_recv.at[src], r, c).wait_recv()

    def pack2(k):
        to = lax.rem(r + k, R)

        def run(n):
            for u in range(PACK):
                s2[to, n * PACK + u] = r1[index2[to * cap2 + n * PACK + u]]

        over(0, cap2 // PACK, run)

    for k in range(1, R):
        pack2(k)
        if k > 1:
            second(k - 1).start()

    def pack2_own(n):
        for u in range(PACK):
            r2[r * cap2 + n * PACK + u] = r1[index2[r * cap2 + n * PACK + u]]

    over(0, cap2 // PACK, pack2_own)
    second(R - 1).start()

    def scatter(jl, k):
        return remote(slab.at[jl], chunk.at[k], c_send.at[jl], ck_recv.at[k], r, jl)

    def scatter_own(jl, k):
        return pltpu.make_async_copy(slab.at[jl], chunk.at[k], ck_recv.at[k])

    for k in range(2):

        @pl.when(c == k)
        def _():
            for jl in range(C):
                if jl == k:
                    scatter_own(jl, k).start()
                else:
                    scatter(jl, k).start()

    @pl.when(y == 0)
    def _():
        for p in range(2):

            @pl.when(c != pieces[p][0])
            def _():
                _, at, n = pieces[p]
                here = diag.at[pl.ds(at, n)]
                remote(here, here, dx_send.at[0], dx_recv.at[p], r, c).wait_recv()

        for k in range(1, X):
            diag_y(k).start()

    for k in range(1, R):
        second_wait(k)

    owned = ((0, 1), (1, 2))

    def mine_own_rows(p):
        at, n = owned[p]
        return mine.at[pl.ds(at, n)]

    def mine_row(p, k):
        here = mine_own_rows(p)
        return remote(here, here, m_send.at[k], m_recv.at[p], lax.rem(r + k, R), c)

    for p in range(2):

        @pl.when(r == p)
        def _():
            at, n = owned[p]
            zero = jnp.zeros(mine.shape[1:], F32)

            def run(k, sums):
                for u in range(PACK):
                    slot = k * PACK + u
                    sums = tuple(
                        total + pick[b * R * cap2 + slot] * r2[slot] for b, total in enumerate(sums)
                    )
                return sums

            sums = lax.fori_loop(0, R * cap2 // PACK, run, (zero,) * n)
            for b in range(n):
                mine[at + b] = sums[b]
            for k in range(1, R):
                mine_row(p, k).start()

    for p in range(2):

        @pl.when(r != p)
        def _():
            here = mine_own_rows(p)
            remote(here, here, m_send.at[0], m_recv.at[p], r, c).wait_recv()

    def mine_col(k):
        to = lax.rem(c + k, C)
        return remote(mine, parts.at[c], g_send.at[k], g_recv.at[c], r, to)

    for k in range(1, C):
        mine_col(k).start()
    parts[c] = mine[...]
    sent_blocks(i0, NB, lambda i: b_copy(i).start())


    part3 = PACK * 4

    def third(k, h):
        to = lax.rem(c + k, C)
        at = pl.ds(h * part3, part3)
        return remote(s3.at[to, at], out.at[c, at], p3_send.at[k, h], p3_recv.at[c, h], r, to)

    def third_wait(k, h):
        src = lax.rem(c + k, C)
        at = pl.ds(h * part3, part3)
        remote(s3.at[0, at], out.at[src, at], p3_send.at[0, h], p3_recv.at[src, h], r, c).wait_recv()

    kept = pl.ds(0, parts3 * part3)
    third_own = pltpu.make_async_copy(s3.at[c, kept], out.at[c, kept], p3_recv.at[c, 0])

    def pack3(k, h):
        to = lax.rem(c + k, C)

        def run(n):
            for u in range(PACK):
                at = h * part3 + n * PACK + u
                s3[to, at] = r2[index3[to * cap3 + at]]

        over(0, part3 // PACK, run)

    def third_part(h):
        def step(k):
            pack3(k, h)

            @pl.when(k > 1)
            def _():
                third(k - 1, h).start()

        over(1, C, step)
        pack3(C, h)
        third(C - 1, h).start()

    over(0, parts3, third_part)

    def send_sums(k):
        to = lax.rem(c + k, C)
        return remote(sums.at[pl.ds(2 * to, 2)], child.at[c], ch_send.at[k], ch_recv.at[c], r, to)

    sums[...] = jnp.zeros(sums.shape, F32)

    def add_up(p):
        for u in range(sums.shape[1]):
            rest = r2[pl.ds(p * cap2, cap2), u, :]
            total = sums[:, u, :]
            for _ in range(3):
                piece = rest.astype(BF16)
                rest = rest - piece.astype(F32)
                total = total + dot16(chosen[p], piece, NN)
            sums[:, u, :] = total

    over(0, R, add_up)
    for k in range(1, C):
        send_sums(k).start()
    for b in range(2):
        child[c, b] = sums[2 * c + b]

    @pl.when(y != 0)
    def _():
        remote(diag, diag, dy_send.at[0], dy_recv.at[0], r, c).wait_recv()

    sub = mine.shape[1]

    def part_wait(q):
        @pl.when(q != c)
        def _():
            remote(mine, parts.at[q], g_send.at[0], g_recv.at[q], r, c).wait_recv()

    over(0, C, part_wait)
    for k in range(1, X):

        @pl.when(y == 0)
        def _():
            diag_y(k).wait_send()

    for p in range(2):

        @pl.when(c == pieces[p][0])
        def _():
            for k in range(1, X):
                diag_x(p, k).wait_send()

    rows = lax.broadcasted_iota(jnp.int32, (EDGE, EDGE), 0)
    cols = lax.broadcasted_iota(jnp.int32, (EDGE, EDGE), 1)
    eye = (rows == cols).astype(F32)
    for q in range(C):
        for b in range(3):
            at = pl.ds(q * sub, sub)
            diag[b, at, :] = diag[b, at, :] + parts[q, b]

    def pivot(block, at):
        work[:, :EDGE] = jnp.where(rows >= cols, block, block.T)
        work[:, EDGE:] = eye
        factor(work, upper)
        low[at] = jnp.where(rows >= cols, upper[:, :EDGE].T, 0.0)
        low[at + 1] = jnp.where(rows >= cols, upper[:, EDGE:], 0.0)

    pivot(diag[0], 0)
    low[2] = dot(diag[1], low[1], NT)
    pivot(diag[2] - dot(low[2], low[2], NT), 3)
    low_copy = pltpu.make_async_copy(low, low_out, low_sem)
    low_copy.start()

    scatter_own(0, 0).wait()
    scatter_own(0, 1).wait()

    def child_wait(q):
        @pl.when(q != c)
        def _():
            remote(sums.at[pl.ds(0, 2)], child.at[q], ch_send.at[0], ch_recv.at[q], r, c).wait_recv()

    over(0, C, child_wait)
    for q in range(C):
        for b in range(2):
            at = pl.ds(q * sub, sub)
            chunk[b, at, :] = chunk[b, at, :] + child[q, b]
    chunk_copy = pltpu.make_async_copy(chunk, chunk_out, chunk_sem)
    chunk_copy.start()

    own_blocks(lambda jl: own_out(jl).wait())
    for s in range(R):
        begin = start_of(s * C + c)

        def run(jl):
            @pl.when((r != s) & (jl * R + r >= begin))
            def _():
                remote(col.at[0], grid.at[jl, s], b_send.at[0], b_recv.at[jl, s], r, c).wait_recv()

        over(0, C, run)
    third_own.start()
    sent_blocks(i0, NB, lambda i: b_copy(i).wait_send())
    for k in range(1, R):
        second(k).wait_send()
    for h in range(parts3):
        for k in range(1, C):
            third_wait(k, h)
        for k in range(1, C):
            third(k, h).wait_send()
    third_own.wait()
    low_copy.wait()
    chunk_copy.wait()
    for k in range(1, C):
        send_sums(k).wait_send()
    for k in range(2):

        @pl.when(c == k)
        def _():
            for jl in range(C):
                if jl != k:
                    scatter(jl, k).wait_send()

    for p in range(2):

        @pl.when((r == 0) & (c == pieces[p][0]))
        def _():
            for k in range(1, R):
                diag_row(p, k).wait_send()

        @pl.when(r == p)
        def _():
            for k in range(1, R):
                mine_row(p, k).wait_send()

    for k in range(1, C):
        mine_col(k).wait_send()


def spread(R, C, cap2, cap3, parts3, name, held, index2, index3, pick, chosen, slab, front):
    hbm = pl.BlockSpec(memory_space=pltpu.HBM)
    smem = pl.BlockSpec(memory_space=pltpu.SMEM)
    dma = pltpu.SemaphoreType.DMA
    sub = held.shape[1]
    return pl.pallas_call(
        functools.partial(spread_kernel, R, C, cap2, cap3, parts3),
        in_specs=[hbm, smem, smem, smem, pl.BlockSpec(memory_space=pltpu.VMEM), hbm, hbm],
        out_specs=[hbm, hbm, hbm, hbm],
        out_shape=[
            jax.ShapeDtypeStruct((C, R, EDGE, EDGE), F32),
            jax.ShapeDtypeStruct((C, cap3, sub, EDGE), F32),
            jax.ShapeDtypeStruct((5, EDGE, EDGE), F32),
            jax.ShapeDtypeStruct((2, EDGE, EDGE), F32),
        ],
        scratch_shapes=[
            pltpu.VMEM(held.shape, F32),
            pltpu.VMEM((R, cap2, sub, EDGE), F32),
            pltpu.VMEM((R * cap2, sub, EDGE), F32),
            pltpu.VMEM((C, cap3, sub, EDGE), F32),
            pltpu.VMEM((C, EDGE, EDGE), F32),
            pltpu.VMEM((2, EDGE, EDGE), F32),
            pltpu.VMEM((2 * C, sub, EDGE), F32),
            pltpu.VMEM((C, 2, sub, EDGE), F32),
            dma((C,)), dma((2,)), dma((C,)), dma((C,)), dma,
            pltpu.VMEM((3, EDGE, EDGE), F32),
            pltpu.VMEM((3, sub, EDGE), F32),
            pltpu.VMEM((C, 3, sub, EDGE), F32),
            pltpu.VMEM((EDGE, 2 * EDGE), F32),
            pltpu.VMEM((EDGE, 2 * EDGE), F32),
            pltpu.VMEM((5, EDGE, EDGE), F32),
            dma((R,)), dma((2,)), dma((C,)), dma((2,)), dma((C,)), dma((1,)),
            dma((R,)), dma((2,)), dma((C,)), dma((C,)), dma,
            dma((C,)), dma((C,)), dma((R * C,)), dma((C, R)),
            dma, dma((R,)), dma((R,)), dma((C, parts3)), dma((C, parts3)),
        ],
        compiler_params=pltpu.CompilerParams(
            collective_id=name, has_side_effects=True, vmem_limit_bytes=60 << 20
        ),
        name="spread",
    )(held, index2, index3, pick, chosen, slab, front)


def panel_kernel(
    R, C, chunk, low, qrow, qcol,
    rows_q, zbuf, cols_q,
    ag_send, ag_recv, z_send, z_recv, v_send, v_recv, q_sem,
):
    r = lax.axis_index("row")
    c = lax.axis_index("col")
    ratio = C // R
    greet(R, C, r, c)

    i = c * R + r
    q0 = dot(chunk[0], low[1], NT)
    q1 = dot(chunk[1] - dot(q0, low[2], NT), low[4], NT)
    rows_q[0, c] = jnp.where(i == 0, low[0], jnp.where(i == 1, low[2], q0))
    rows_q[1, c] = jnp.where(i == 0, 0.0, jnp.where(i == 1, low[3], q1))

    def gather(k, n):
        here = rows_q.at[n, c]
        return remote(here, here, ag_send.at[n, k], ag_recv.at[n, c], r, lax.rem(c + k, C))

    def along(k, n):
        return remote(
            rows_q.at[n, c], zbuf.at[n, r], z_send.at[n, k], z_recv.at[n, r], lax.rem(r + k, R), c
        )

    for n in range(2):
        for k in range(1, R):
            along(k, n).start()
    for n in range(2):
        for k in range(1, C):
            gather(k, n).start()

    mine = lax.rem(c, ratio) * R
    place = c // ratio

    def serve(p, n):
        return remote(
            zbuf.at[n, p], cols_q.at[n, place], v_send.at[n, p], v_recv.at[n, place], r, mine + p
        )

    def serve_own(p, n):
        return pltpu.make_async_copy(zbuf.at[n, p], cols_q.at[n, place], v_recv.at[n, place])

    own_z = [pltpu.make_async_copy(rows_q.at[n, c], zbuf.at[n, r], z_recv.at[n, r]) for n in range(2)]
    for copy in own_z:
        copy.start()
    for copy in own_z:
        copy.wait()

    def pass_on(p):
        for n in range(2):

            @pl.when(p != r)
            def _():
                remote(rows_q.at[n, 0], zbuf.at[n, p], z_send.at[n, 0], z_recv.at[n, p], r, c).wait_recv()

            @pl.when(mine + p == c)
            def _():
                serve_own(p, n).start()

            @pl.when(mine + p != c)
            def _():
                serve(p, n).start()

    over(0, R, pass_on)

    def row_wait(jl):
        @pl.when(jl != c)
        def _():
            for n in range(2):
                here = rows_q.at[n, jl]
                remote(here, here, ag_send.at[n, 0], ag_recv.at[n, jl], r, c).wait_recv()

    over(0, C, row_wait)
    keep_row = pltpu.make_async_copy(rows_q, qrow, q_sem.at[1])
    keep_row.start()

    def col_wait(s):
        for n in range(2):
            pltpu.make_async_copy(zbuf.at[n, 0], cols_q.at[n, s], v_recv.at[n, s]).wait()

    over(0, R, col_wait)
    keep_col = pltpu.make_async_copy(cols_q, qcol, q_sem.at[0])
    keep_col.start()

    for n in range(2):
        for k in range(1, C):
            gather(k, n).wait_send()
        for k in range(1, R):
            along(k, n).wait_send()

    def served(p):
        @pl.when(mine + p != c)
        def _():
            for n in range(2):
                serve(p, n).wait_send()

    over(0, R, served)
    keep_col.wait()
    keep_row.wait()


def panels(R, C, chunk, low):
    hbm = pl.BlockSpec(memory_space=pltpu.HBM)
    dma = pltpu.SemaphoreType.DMA
    return pl.pallas_call(
        functools.partial(panel_kernel, R, C),
        in_specs=[pl.BlockSpec(memory_space=pltpu.VMEM)] * 2,
        out_specs=[hbm, hbm],
        out_shape=[
            jax.ShapeDtypeStruct((2, C, EDGE, EDGE), F32),
            jax.ShapeDtypeStruct((2, R, EDGE, EDGE), F32),
        ],
        scratch_shapes=[
            pltpu.VMEM((2, C, EDGE, EDGE), F32),
            pltpu.VMEM((2, R, EDGE, EDGE), F32),
            pltpu.VMEM((2, R, EDGE, EDGE), F32),
            dma((2, C)), dma((2, C)),
            dma((2, R)), dma((2, R)), dma((2, R)), dma((2, R)), dma((2,)),
        ],
        compiler_params=pltpu.CompilerParams(
            collective_id=1, has_side_effects=True, vmem_limit_bytes=60 << 20
        ),
        name="panels",
    )(chunk, low)


def halves(x):
    high = x.astype(BF16)
    return high, (x - high.astype(F32)).astype(BF16)


def update_kernel(R, C, place, landing, grid, qrow, qcol, source, out, arrived, left, right, head, follow, sem):
    s = pl.program_id(0)
    slots = arrived.shape[1]
    batch = PACK * 4
    r, c = place[0], place[1]
    j = s * C + c
    rows = lax.broadcasted_iota(jnp.int32, (EDGE, EDGE), 0)
    cols = lax.broadcasted_iota(jnp.int32, (EDGE, EDGE), 1)

    @pl.when(s == 0)
    def _():
        def clear(k):
            head[k] = -1

        over(0, R, clear)

        def link(k, used):
            where = landing[1 + slots + k]

            @pl.when(where >= 0)
            def _():
                follow[k] = head[where]
                head[where] = k

            return jnp.where(where >= 0, k + 1, used)

        used = lax.fori_loop(0, slots, link, 0)
        batches = lax.div(used + batch - 1, batch)

        def load(b):
            at = pl.ds(pl.multiple_of(b * batch, batch), batch)
            return pltpu.make_async_copy(source.at[:, at], arrived.at[:, at], sem.at[b])

        over(0, batches, lambda b: load(b).start())

        def split(jl):
            at = pl.ds(pl.multiple_of(jl * EDGE, EDGE), EDGE)
            for n in range(2):
                high, low = halves(qrow[n, jl])
                for m, part in ((0, high), (2, high), (4, low)):
                    left[at, (m + n) * EDGE : (m + n + 1) * EDGE] = part

        over(0, C, split)
        over(0, batches, lambda b: load(b).wait())

    for n in range(2):
        high, low = halves(qcol[n, 0])
        for m, part in ((0, high.T), (2, low.T), (4, high.T)):
            right[(m + n) * EDGE : (m + n + 1) * EDGE, :] = part

    many = min(4, C)
    for g in range(C // many):
        last = (g * many + many - 1) * R + r

        @pl.when((last >= j) & (j >= 2))
        def _():
            product = dot16(left[g * many * EDGE : (g + 1) * many * EDGE, :], right[...], NN)
            for u in range(many):
                out[g * many + u, 0] = grid[g * many + u, 0] - product[u * EDGE : (u + 1) * EDGE, :]

    @pl.when(j < 2)
    def _():
        for jl in range(C):
            out[jl, 0] = jnp.where(j == 0, qrow[0, jl], qrow[1, jl])

    def more(k):
        return k >= 0

    def add(k):
        jl = landing[1 + k]
        out[jl, 0] = out[jl, 0] + arrived[:, k].reshape(EDGE, EDGE)
        return follow[k]

    lax.while_loop(more, add, jnp.where(j >= 2, head[s], -1))
    for jl in range(C):
        i = jl * R + r

        @pl.when(i < j)
        def _():
            out[jl, 0] = jnp.zeros((EDGE, EDGE), F32)

        @pl.when((i == j) & (j >= 2))
        def _():
            out[jl, 0] = jnp.where(rows >= cols, out[jl, 0], 0.0)


def update(R, C, place, landing, grid, qrow, qcol, arrived):
    cap3 = arrived.shape[1]
    block = pl.BlockSpec((C, 1, EDGE, EDGE), lambda s, *_: (0, s, 0, 0))
    return pl.pallas_call(
        functools.partial(update_kernel, R, C),
        grid_spec=pltpu.PrefetchScalarGridSpec(
            num_scalar_prefetch=2,
            grid=(R,),
            in_specs=[
                block,
                pl.BlockSpec((2, C, EDGE, EDGE), lambda s, *_: (0, 0, 0, 0)),
                pl.BlockSpec((2, 1, EDGE, EDGE), lambda s, *_: (0, s, 0, 0)),
                pl.BlockSpec(memory_space=pltpu.HBM),
            ],
            out_specs=block,
            scratch_shapes=[
                pltpu.VMEM(arrived.shape, F32),
                pltpu.VMEM((C * EDGE, 6 * EDGE), BF16),
                pltpu.VMEM((6 * EDGE, EDGE), BF16),
                pltpu.SMEM((R,), jnp.int32),
                pltpu.SMEM((cap3,), jnp.int32),
                pltpu.SemaphoreType.DMA((cap3 // (PACK * 4),)),
            ],
        ),
        out_shape=jax.ShapeDtypeStruct((C, R, EDGE, EDGE), F32),
        compiler_params=pltpu.CompilerParams(vmem_limit_bytes=60 << 20),
        name="update",
    )(place, landing, grid, qrow, qcol, arrived)


def capacities(R, C, T):
    if T < 32:
        return 16, (PACK * 4, PACK * 8)
    return 104, (80, 112, 160)


def hot(values, count):
    return (values[..., None] == jnp.arange(count, dtype=jnp.int32)).astype(BF16)


def before(marks):
    n = marks.shape[-2]
    serial = jnp.arange(n, dtype=jnp.int32)
    lower = (serial[:, None] > serial[None, :]).astype(BF16)
    return jnp.einsum("pq,...qk->...pk", lower, marks, preferred_element_type=F32)


def local(front_entries, child_updates, row_maps, col_maps, target_columns, row_offsets):
    R = lax.axis_size("row")
    C = lax.axis_size("col")
    count = R * C
    T = child_updates.shape[0]
    cap2, choices = capacities(R, C, T)
    cap3 = choices[-1]
    my_row = lax.axis_index("row").astype(jnp.int32)
    my_col = lax.axis_index("col").astype(jnp.int32)

    told = jnp.concatenate([target_columns[:, 0], row_offsets[:, 0]])
    told = jnp.pad(told, (0, EDGE - 2 * T)).reshape(1, EDGE)
    front = front_entries.reshape(count, EDGE, EDGE)
    held, told, slab = begin(R, C, child_updates, row_maps, col_maps, told, front)
    told = told.reshape(C, R, EDGE).transpose(1, 0, 2).reshape(count, EDGE)
    columns, offsets = told[:, :T], told[:, T : 2 * T]
    target_rows = columns + offsets % (count - columns)
    columns = columns.reshape(R, C * T)
    target_rows = target_rows.reshape(R, C * T)
    to_row, to_col = target_rows % R, columns % C

    row_hot = hot(to_row, R)
    panel = columns < 2
    lead = row_hot * panel[..., None].astype(BF16)
    rest = row_hot - lead
    leads = jnp.sum(lead.astype(F32), axis=1, keepdims=True)
    rank2 = before(lead) * lead.astype(F32) + (before(rest) + leads) * rest.astype(F32)
    rank2 = jnp.sum(rank2, axis=-1).astype(jnp.int32)
    mine = to_row == my_row
    col_hot = hot(jnp.where(mine, to_col, -1), C)
    inside = before(col_hot)
    totals = jnp.sum(col_hot.astype(F32), axis=1)
    planes = jnp.arange(R, dtype=jnp.int32)
    ahead = jnp.sum(jnp.where((planes[:, None] > planes[None, :])[..., None], totals[None], 0.0), axis=1)
    rank3 = jnp.sum((inside + ahead[:, None, :]) * col_hot.astype(F32), axis=-1).astype(jnp.int32)
    loads2 = jnp.sum(row_hot.astype(F32), axis=1)
    loads3 = jnp.einsum("pqk,pql->kl", row_hot, hot(to_col, C), preferred_element_type=F32)
    passes2 = (jnp.max(loads2).astype(jnp.int32) + cap2 - 1) // cap2
    most3 = jnp.max(loads3).astype(jnp.int32)
    passes3 = (most3 + cap3 - 1) // cap3

    def tables(a, b):
        own_hot = lax.dynamic_index_in_dim(row_hot, my_row, 0, keepdims=False)
        own_rank = lax.dynamic_index_in_dim(rank2, my_row, 0, keepdims=False)
        serial = jnp.arange(C * T, dtype=jnp.int32)
        values = jnp.stack([serial // T, serial % T], axis=0).astype(BF16)
        marked = values[:, :, None] * own_hot[None]
        found = jnp.einsum("vqk,qn->vkn", marked, hot(own_rank - a * cap2, cap2), preferred_element_type=F32)
        found = found.astype(jnp.int32)
        index2 = (found[0] * T + found[1]).reshape(-1)
        place2 = rank2 - a * cap2
        active = (place2 >= 0) & (place2 < cap2) & mine
        source = jnp.broadcast_to(planes[:, None], (R, C * T))
        values = jnp.stack(
            [source, place2, target_rows // R, columns // C, jnp.ones_like(source)], axis=0
        )
        values = jnp.where(active, values, 0).astype(BF16)
        marked = values[..., None] * col_hot[None]
        found = jnp.einsum(
            "vpqk,pqn->vkn", marked, hot(rank3 - b * cap3, cap3), preferred_element_type=F32
        ).astype(jnp.int32)
        index3 = (found[0] * cap2 + found[1]).reshape(-1)
        here = lax.dynamic_index_in_dim(found, my_col, 1, keepdims=False)
        return index2, index3, here[2], here[3], here[4]

    index2, index3, land_row, land_col, valid = tables(0, 0)
    marks = hot(jnp.where(mine & panel, target_rows // R * 2 + columns, -1), 2 * C)
    chosen = jnp.einsum("pqv,pqn->pvn", marks, hot(rank2, cap2), preferred_element_type=F32)
    pick = chosen[:, :2].transpose(1, 0, 2).reshape(-1)
    chosen = chosen.astype(BF16)
    runs = [
        functools.partial(spread, R, C, cap2, cap3, size // (PACK * 4), 10 + at)
        for at, size in enumerate(choices)
    ]
    choice = sum((most3 > size).astype(jnp.int32) for size in choices[:-1])
    grid, arrived, low, chunk = lax.switch(
        choice, runs, held, index2, index3, pick, chosen, slab, front
    )

    def another(carry):
        p, grid = carry
        index2, index3, land_row, land_col, valid = tables(p // passes3, p % passes3)
        moved = held[index2].reshape(R, cap2, EDGE // C, EDGE)
        moved = lax.all_to_all(moved, "row", split_axis=0, concat_axis=0, tiled=True)
        moved = moved.reshape((R * cap2, EDGE // C, EDGE))[index3].reshape(C, cap3, EDGE // C, EDGE)
        moved = lax.all_to_all(moved, "col", split_axis=0, concat_axis=0, tiled=True)
        tiles = moved.transpose(1, 0, 2, 3).reshape(cap3, EDGE, EDGE)
        tiles = jnp.where((valid > 0)[:, None, None], tiles, 0.0)
        return p + 1, grid.at[land_row, land_col].add(tiles)

    _, grid = lax.while_loop(lambda carry: carry[0] < passes2 * passes3, another, (jnp.int32(1), grid))

    landing = jnp.concatenate([my_col[None], land_row, jnp.where(valid > 0, land_col, -1)])
    qrow, qcol = panels(R, C, chunk, low)
    place = jnp.stack([my_row, my_col])
    result = update(R, C, place, landing, grid, qrow, qcol, arrived)
    return result.reshape(C, 1, R, 1, EDGE, EDGE)


def solution(mesh):
    return jax.shard_map(
        local,
        mesh=mesh,
        in_specs=(
            P(None, ("row", "col")),
            P(("row", "col"), None, None),
            P(("row", "col"), None),
            P(("row", "col"), None),
            P(("row", "col"), None),
            P(("row", "col"), None),
        ),
        out_specs=P(None, "row", None, "col", None, None),
        check_vma=False,
    )
```

```python
import functools
import math

import jax
import jax.numpy as jnp
from jax import lax
from jax.experimental import pallas as pl
from jax.experimental.pallas import tpu as pltpu
from jax.sharding import PartitionSpec as P

EDGE = 128
MESH = pl.DeviceIdType.MESH
PRECISE = lax.Precision.HIGHEST
F32 = jnp.float32
BF16 = jnp.bfloat16
NN = ((1,), (0,))
NT = ((1,), (1,))
TN = ((0,), (0,))


def dot(a, b, dims):
    return lax.dot_general(a, b, (dims, ((), ())), precision=PRECISE, preferred_element_type=F32)


def dot16(a, b, dims):
    return lax.dot_general(a, b, (dims, ((), ())), preferred_element_type=F32)


def remote(src, dst, ss, rs, rr, cc):
    return pltpu.make_async_remote_copy(
        src_ref=src, dst_ref=dst, send_sem=ss, recv_sem=rs, device_id=(rr, cc), device_id_type=MESH
    )


def over(low, high, body):
    def run(i, _):
        body(i)
        return 0

    lax.fori_loop(low, high, run, 0)


def greet(R, C, r, c):
    barrier = pltpu.get_barrier_semaphore()
    for k in range(1, R):
        pl.semaphore_signal(barrier, inc=1, device_id=(lax.rem(r + k, R), c), device_id_type=MESH)
    for k in range(1, C):
        pl.semaphore_signal(barrier, inc=1, device_id=(r, lax.rem(c + k, C)), device_id_type=MESH)
    pl.semaphore_wait(barrier, R + C - 2)


PARTS = 4
GROUP = 4


def early(C):
    return C * 5 // 8


def begin_kernel(
    R, C, tiles, row_map, col_map, told, col, r1, told_all, slab,
    held, placed, told_row, stage,
    st_in, st_out, f_send, f_recv, t_sem, tr_send, tr_recv, tc_send, tc_recv, send, recv,
):
    r = lax.axis_index("row")
    c = lax.axis_index("col")
    T = tiles.shape[0]
    sub = EDGE // C
    part = T // PARTS
    load = pltpu.make_async_copy(tiles, held, t_sem)
    load.start()
    greet(R, C, r, c)

    def tell_row(k):
        return remote(told, told_row.at[r], tr_send.at[k], tr_recv.at[r], lax.rem(r + k, R), c)

    def tell_col(k):
        return remote(told_row, told_all.at[c], tc_send.at[k], tc_recv.at[c], r, lax.rem(c + k, C))

    tell_own = pltpu.make_async_copy(told, told_row.at[r], tr_recv.at[r])
    tell_own.start()
    for k in range(1, R):
        tell_row(k).start()

    def ahead(i):
        return remote(col.at[i], slab.at[i // R], f_send.at[i], f_recv.at[i // R], lax.rem(i, R), c)

    def others(body):
        def run(i):
            @pl.when(lax.rem(i, R) != 0)
            def _():
                body(i)

        over(0, R * early(C), run)

    def own_in(jl):
        return pltpu.make_async_copy(col.at[jl * R], stage.at[jl], st_in.at[jl])

    def own_out(jl):
        return pltpu.make_async_copy(stage.at[jl], slab.at[jl], st_out.at[jl])

    panel = (r == 0) & (c < 2)

    @pl.when(panel)
    def _():
        over(0, early(C), lambda jl: own_in(jl).start())
        others(lambda i: ahead(i).start())

    levels = lax.broadcasted_iota(jnp.int32, (EDGE, EDGE), 0)

    def place(t):
        for g in range(GROUP):
            k = t * GROUP + g
            col_hot = (levels == col_map[pl.ds(k, 1), :]).astype(F32).astype(BF16)
            row_hot = (levels == row_map[pl.ds(k, 1), :]).astype(F32).astype(BF16)
            x = held[k]
            first = x.astype(BF16)
            rest = x - first.astype(F32)
            second = rest.astype(BF16)
            third = (rest - second.astype(F32)).astype(BF16)
            moved = [dot16(p, col_hot, NT).astype(BF16) for p in (first, second, third)]
            full = (dot16(row_hot, moved[0], NN) + dot16(row_hot, moved[1], NN)) + dot16(
                row_hot, moved[2], NN
            )
            for q in range(C):
                placed[q, k] = full[q * sub : (q + 1) * sub, :]

    def slices(k, h):
        to = lax.rem(c + k, C)
        return remote(
            placed.at[to, pl.ds(h * part, part)], r1.at[pl.ds(c * T + h * part, part)],
            send.at[k, h], recv.at[c, h], r, to,
        )

    def slices_wait(k, h):
        src = lax.rem(c + k, C)
        remote(
            placed.at[0, pl.ds(0, part)], r1.at[pl.ds(src * T + h * part, part)],
            send.at[0, h], recv.at[src, h], r, c,
        ).wait_recv()

    load.wait()
    for h in range(PARTS):
        over(h * part // GROUP, (h + 1) * part // GROUP, place)
        if h == 0:
            tell_own.wait()
            for k in range(1, R):
                src = lax.rem(r + k, R)
                remote(told, told_row.at[src], tr_send.at[0], tr_recv.at[src], r, c).wait_recv()
            for k in range(1, C):
                tell_col(k).start()
            tell_kept = pltpu.make_async_copy(told_row, told_all.at[c], tc_recv.at[c])
            tell_kept.start()
        for k in range(1, C):
            slices(k, h).start()
    own = pltpu.make_async_copy(placed.at[c], r1.at[pl.ds(c * T, T)], recv.at[c, 0])
    own.start()

    @pl.when(panel)
    def _():
        def turn(jl):
            own_in(jl).wait()
            own_out(jl).start()

        over(0, early(C), turn)
        over(0, early(C), lambda jl: own_out(jl).wait())
        others(lambda i: ahead(i).wait_send())

    @pl.when((r != 0) & (c < 2))
    def _():
        def landed(jl):
            remote(col.at[0], slab.at[jl], f_send.at[0], f_recv.at[jl], r, c).wait_recv()

        over(0, early(C), landed)

    tell_kept.wait()
    for k in range(1, C):
        src = lax.rem(c + k, C)
        remote(told_row, told_all.at[src], tc_send.at[0], tc_recv.at[src], r, c).wait_recv()
    for h in range(PARTS):
        for k in range(1, C):
            slices_wait(k, h)
    own.wait()
    for k in range(1, R):
        tell_row(k).wait_send()
    for k in range(1, C):
        tell_col(k).wait_send()
    for h in range(PARTS):
        for k in range(1, C):
            slices(k, h).wait_send()


def begin(R, C, tiles, row_map, col_map, told, front):
    hbm = pl.BlockSpec(memory_space=pltpu.HBM)
    vmem = pl.BlockSpec(memory_space=pltpu.VMEM)
    dma = pltpu.SemaphoreType.DMA
    T, sub = tiles.shape[0], EDGE // C
    return pl.pallas_call(
        functools.partial(begin_kernel, R, C),
        in_specs=[hbm, vmem, vmem, hbm, hbm],
        out_specs=[hbm, hbm, hbm],
        out_shape=[
            jax.ShapeDtypeStruct((C * T, sub, EDGE), F32),
            jax.ShapeDtypeStruct((C, R, 1, EDGE), jnp.int32),
            jax.ShapeDtypeStruct((early(C), EDGE, EDGE), F32),
        ],
        scratch_shapes=[
            pltpu.VMEM((T, EDGE, EDGE), F32),
            pltpu.VMEM((C, T, sub, EDGE), F32),
            pltpu.VMEM((R, 1, EDGE), jnp.int32),
            pltpu.VMEM((C, EDGE, EDGE), F32),
            dma((C,)), dma((C,)), dma((R * C,)), dma((C,)),
            dma, dma((R,)), dma((R,)), dma((C,)), dma((C,)), dma((C, PARTS)), dma((C, PARTS)),
        ],
        compiler_params=pltpu.CompilerParams(
            collective_id=4, has_side_effects=True, vmem_limit_bytes=60 << 20
        ),
        name="begin",
    )(tiles, row_map, col_map, told, front)


STEP = 8


def factor(work, upper):
    rows8 = lax.broadcasted_iota(jnp.int32, (STEP, 1), 0)
    lanes = lax.broadcasted_iota(jnp.int32, (STEP, EDGE), 1)

    def block(b, _):
        first = pl.multiple_of(b * STEP, STEP)
        x = work[pl.ds(first, STEP), :]
        d = pltpu.roll(x[:, :EDGE], lax.rem(EDGE - first, EDGE), 1)
        for t in range(STEP):
            pivot = d[t : t + 1, t : t + 1]
            scale = lax.rsqrt(pivot)
            ratio = d[:, t : t + 1] / pivot
            ratio = jnp.where(rows8 > t, ratio, jnp.where(rows8 == t, 1.0 - scale, 0.0))
            x = x - ratio * x[t : t + 1, :]
            d = d - ratio * d[t : t + 1, :]
        upper[pl.ds(first, STEP), :] = x
        left = jnp.where(lanes >= first + STEP, x[:, :EDGE], 0.0)
        work[...] = work[...] - dot(left, x, TN)
        return 0

    lax.fori_loop(0, EDGE // STEP, block, 0)


PACK = 4


def spread_kernel(
    R, C, cap2, cap3, parts3, held, index2, index3, pick, chosen, slab, col, grid, out, low_out, chunk_out,
    r1, s2, r2, s3, stage, late, l_send, l_recv, chunk, sums, child, c_send, ck_recv, ch_send, ch_recv, chunk_sem, diag, mine, parts, work, upper, low,
    dr_send, dr_recv, dx_send, dx_recv, dy_send, dy_recv, m_send, m_recv, g_send, g_recv, low_sem,
    st_in, st_out, b_send, b_recv, load_sem, p2_send, p2_recv, p3_send, p3_recv,
):
    r = lax.axis_index("row")
    c = lax.axis_index("col")
    NB = R * C
    start_of = lambda column: jnp.where(column < 2, NB, column)
    i0 = start_of(r * C + c)
    X = math.isqrt(C)
    x, y = lax.rem(c, X), c // X
    greet(R, C, r, c)

    pieces = ((0, 0, 2), (1, 2, 1))

    def diag_row(p, k):
        owner, at, n = pieces[p]
        return remote(
            col.at[pl.ds(owner, n)], diag.at[pl.ds(at, n)], dr_send.at[k], dr_recv.at[p], lax.rem(r + k, R), c
        )

    def diag_own(p):
        owner, at, n = pieces[p]
        return pltpu.make_async_copy(col.at[pl.ds(owner, n)], diag.at[pl.ds(at, n)], dr_recv.at[p])

    def diag_x(p, k):
        _, at, n = pieces[p]
        here = diag.at[pl.ds(at, n)]
        return remote(here, here, dx_send.at[k], dx_recv.at[p], r, lax.rem(x + k, X))

    def diag_y(k):
        return remote(diag, diag, dy_send.at[k], dy_recv.at[0], r, k * X + x)

    for p in range(2):

        @pl.when((r == 0) & (c == pieces[p][0]))
        def _():
            for k in range(1, R):
                diag_row(p, k).start()
            diag_own(p).start()

    load = pltpu.make_async_copy(held, r1, load_sem)
    load.start()

    def b_copy(i):
        return remote(
            col.at[i], grid.at[i // R, r], b_send.at[i], b_recv.at[i // R, r], lax.rem(i, R), c
        )

    def own_in(jl):
        return pltpu.make_async_copy(col.at[jl * R + r], stage.at[jl], st_in.at[jl])

    def own_out(jl):
        return pltpu.make_async_copy(stage.at[jl], grid.at[jl, r], st_out.at[jl])

    def own_blocks(body):
        def run(jl):
            @pl.when(jl * R + r >= i0)
            def _():
                body(jl)

        over(0, C, run)

    def sent_blocks(low, high, body):
        def run(i):
            @pl.when(lax.rem(i, R) != r)
            def _():
                body(i)

        over(low, high, run)

    own_blocks(lambda jl: own_in(jl).start())

    def own_turn(jl):
        own_in(jl).wait()
        own_out(jl).start()

    own_blocks(own_turn)

    load.wait()

    for p in range(2):

        @pl.when(c == pieces[p][0])
        def _():
            diag_own(p).wait()
            for k in range(1, X):
                diag_x(p, k).start()

    def second(k):
        to = lax.rem(r + k, R)
        return remote(s2.at[to], r2.at[pl.ds(r * cap2, cap2)], p2_send.at[k], p2_recv.at[r], to, c)

    def second_wait(k):
        src = lax.rem(r + k, R)
        remote(s2.at[0], r2.at[pl.ds(src * cap2, cap2)], p2_send.at[0], p2_recv.at[src], r, c).wait_recv()

    def pack2(k):
        to = lax.rem(r + k, R)

        def run(n):
            for u in range(PACK):
                s2[to, n * PACK + u] = r1[index2[to * cap2 + n * PACK + u]]

        over(0, cap2 // PACK, run)

    for k in range(1, R):
        pack2(k)
        if k > 1:
            second(k - 1).start()

    def pack2_own(n):
        for u in range(PACK):
            r2[r * cap2 + n * PACK + u] = r1[index2[r * cap2 + n * PACK + u]]

    over(0, cap2 // PACK, pack2_own)
    second(R - 1).start()

    def scatter(jl, k):
        return remote(slab.at[jl], chunk.at[k], c_send.at[jl], ck_recv.at[k], r, jl)

    def scatter_own(jl, k):
        return pltpu.make_async_copy(slab.at[jl], chunk.at[k], ck_recv.at[k])

    for k in range(2):

        @pl.when(c == k)
        def _():
            for jl in range(early(C)):
                if jl == k:
                    scatter_own(jl, k).start()
                else:
                    scatter(jl, k).start()

    first = early(C)

    def late_row(i):
        jl = i // R - first
        return remote(col.at[i], late.at[jl], l_send.at[i - first * R], l_recv.at[jl], lax.rem(i, R), c)

    def late_own(jl):
        return pltpu.make_async_copy(col.at[(jl + first) * R], late.at[jl], l_recv.at[jl])

    def late_sent(body):
        def run(i):
            @pl.when(lax.rem(i, R) != 0)
            def _():
                body(i)

        over(first * R, NB, run)

    @pl.when((r == 0) & (c < 2))
    def _():
        late_sent(lambda i: late_row(i).start())
        over(0, C - first, lambda jl: late_own(jl).start())

    def late_scatter(jl, k):
        to = jl + first
        return remote(late.at[jl], chunk.at[k], c_send.at[to], ck_recv.at[k], r, to)

    @pl.when(y == 0)
    def _():
        for p in range(2):

            @pl.when(c != pieces[p][0])
            def _():
                _, at, n = pieces[p]
                here = diag.at[pl.ds(at, n)]
                remote(here, here, dx_send.at[0], dx_recv.at[p], r, c).wait_recv()

        for k in range(1, X):
            diag_y(k).start()

    for k in range(1, R):
        second_wait(k)

    owned = ((0, 1), (1, 2))

    def mine_own_rows(p):
        at, n = owned[p]
        return mine.at[pl.ds(at, n)]

    def mine_row(p, k):
        here = mine_own_rows(p)
        return remote(here, here, m_send.at[k], m_recv.at[p], lax.rem(r + k, R), c)

    for p in range(2):

        @pl.when(r == p)
        def _():
            at, n = owned[p]
            zero = jnp.zeros(mine.shape[1:], F32)

            def run(k, sums):
                for u in range(PACK):
                    slot = k * PACK + u
                    sums = tuple(
                        total + pick[b * R * cap2 + slot] * r2[slot] for b, total in enumerate(sums)
                    )
                return sums

            sums = lax.fori_loop(0, R * cap2 // PACK, run, (zero,) * n)
            for b in range(n):
                mine[at + b] = sums[b]
            for k in range(1, R):
                mine_row(p, k).start()

    for p in range(2):

        @pl.when(r != p)
        def _():
            here = mine_own_rows(p)
            remote(here, here, m_send.at[0], m_recv.at[p], r, c).wait_recv()

    def mine_col(k):
        to = lax.rem(c + k, C)
        return remote(mine, parts.at[c], g_send.at[k], g_recv.at[c], r, to)

    for k in range(1, C):
        mine_col(k).start()
    parts[c] = mine[...]
    sent_blocks(i0, NB, lambda i: b_copy(i).start())


    part3 = PACK * 4

    def third(k, h):
        to = lax.rem(c + k, C)
        at = pl.ds(h * part3, part3)
        return remote(s3.at[to, at], out.at[c, at], p3_send.at[k, h], p3_recv.at[c, h], r, to)

    def third_wait(k, h):
        src = lax.rem(c + k, C)
        at = pl.ds(h * part3, part3)
        remote(s3.at[0, at], out.at[src, at], p3_send.at[0, h], p3_recv.at[src, h], r, c).wait_recv()

    kept = pl.ds(0, parts3 * part3)
    third_own = pltpu.make_async_copy(s3.at[c, kept], out.at[c, kept], p3_recv.at[c, 0])

    def pack3(k, h):
        to = lax.rem(c + k, C)

        def run(n):
            for u in range(PACK):
                at = h * part3 + n * PACK + u
                s3[to, at] = r2[index3[to * cap3 + at]]

        over(0, part3 // PACK, run)

    def third_part(h):
        def step(k):
            pack3(k, h)

            @pl.when(k > 1)
            def _():
                third(k - 1, h).start()

        over(1, C, step)
        pack3(C, h)
        third(C - 1, h).start()

    over(0, parts3, third_part)

    def send_sums(k):
        to = lax.rem(c + k, C)
        return remote(sums.at[pl.ds(2 * to, 2)], child.at[c], ch_send.at[k], ch_recv.at[c], r, to)

    sums[...] = jnp.zeros(sums.shape, F32)

    def add_up(p):
        for u in range(sums.shape[1]):
            rest = r2[pl.ds(p * cap2, cap2), u, :]
            total = sums[:, u, :]
            for _ in range(3):
                piece = rest.astype(BF16)
                rest = rest - piece.astype(F32)
                total = total + dot16(chosen[p], piece, NN)
            sums[:, u, :] = total

    over(0, R, add_up)
    for k in range(1, C):
        send_sums(k).start()
    for b in range(2):
        child[c, b] = sums[2 * c + b]

    for k in range(2):

        @pl.when(c == k)
        def _():
            def run(jl):
                late_own(jl).wait()
                late_scatter(jl, k).start()

            over(0, C - first, run)

    @pl.when(y != 0)
    def _():
        remote(diag, diag, dy_send.at[0], dy_recv.at[0], r, c).wait_recv()

    sub = mine.shape[1]

    def part_wait(q):
        @pl.when(q != c)
        def _():
            remote(mine, parts.at[q], g_send.at[0], g_recv.at[q], r, c).wait_recv()

    over(0, C, part_wait)
    for k in range(1, X):

        @pl.when(y == 0)
        def _():
            diag_y(k).wait_send()

    for p in range(2):

        @pl.when(c == pieces[p][0])
        def _():
            for k in range(1, X):
                diag_x(p, k).wait_send()

    rows = lax.broadcasted_iota(jnp.int32, (EDGE, EDGE), 0)
    cols = lax.broadcasted_iota(jnp.int32, (EDGE, EDGE), 1)
    eye = (rows == cols).astype(F32)
    for q in range(C):
        for b in range(3):
            at = pl.ds(q * sub, sub)
            diag[b, at, :] = diag[b, at, :] + parts[q, b]

    def pivot(block, at):
        work[:, :EDGE] = jnp.where(rows >= cols, block, block.T)
        work[:, EDGE:] = eye
        factor(work, upper)
        low[at] = jnp.where(rows >= cols, upper[:, :EDGE].T, 0.0)
        low[at + 1] = jnp.where(rows >= cols, upper[:, EDGE:], 0.0)

    pivot(diag[0], 0)
    low[2] = dot(diag[1], low[1], NT)
    pivot(diag[2] - dot(low[2], low[2], NT), 3)
    low_copy = pltpu.make_async_copy(low, low_out, low_sem)
    low_copy.start()

    scatter_own(0, 0).wait()
    scatter_own(0, 1).wait()

    def child_wait(q):
        @pl.when(q != c)
        def _():
            remote(sums.at[pl.ds(0, 2)], child.at[q], ch_send.at[0], ch_recv.at[q], r, c).wait_recv()

    over(0, C, child_wait)
    for q in range(C):
        for b in range(2):
            at = pl.ds(q * sub, sub)
            chunk[b, at, :] = chunk[b, at, :] + child[q, b]
    chunk_copy = pltpu.make_async_copy(chunk, chunk_out, chunk_sem)
    chunk_copy.start()

    own_blocks(lambda jl: own_out(jl).wait())
    for s in range(R):
        begin = start_of(s * C + c)

        def run(jl):
            @pl.when((r != s) & (jl * R + r >= begin))
            def _():
                remote(col.at[0], grid.at[jl, s], b_send.at[0], b_recv.at[jl, s], r, c).wait_recv()

        over(0, C, run)
    third_own.start()
    sent_blocks(i0, NB, lambda i: b_copy(i).wait_send())
    for k in range(1, R):
        second(k).wait_send()
    for h in range(parts3):
        for k in range(1, C):
            third_wait(k, h)
        for k in range(1, C):
            third(k, h).wait_send()
    third_own.wait()
    low_copy.wait()
    chunk_copy.wait()
    for k in range(1, C):
        send_sums(k).wait_send()
    for k in range(2):

        @pl.when(c == k)
        def _():
            for jl in range(first):
                if jl != k:
                    scatter(jl, k).wait_send()

            over(0, C - first, lambda jl: late_scatter(jl, k).wait_send())

    @pl.when((r == 0) & (c < 2))
    def _():
        late_sent(lambda i: late_row(i).wait_send())

    for p in range(2):

        @pl.when((r == 0) & (c == pieces[p][0]))
        def _():
            for k in range(1, R):
                diag_row(p, k).wait_send()

        @pl.when(r == p)
        def _():
            for k in range(1, R):
                mine_row(p, k).wait_send()

    for k in range(1, C):
        mine_col(k).wait_send()


def spread(R, C, cap2, cap3, parts3, name, held, index2, index3, pick, chosen, slab, front):
    hbm = pl.BlockSpec(memory_space=pltpu.HBM)
    smem = pl.BlockSpec(memory_space=pltpu.SMEM)
    dma = pltpu.SemaphoreType.DMA
    sub = held.shape[1]
    return pl.pallas_call(
        functools.partial(spread_kernel, R, C, cap2, cap3, parts3),
        in_specs=[hbm, smem, smem, smem, pl.BlockSpec(memory_space=pltpu.VMEM), hbm, hbm],
        out_specs=[hbm, hbm, hbm, hbm],
        out_shape=[
            jax.ShapeDtypeStruct((C, R, EDGE, EDGE), F32),
            jax.ShapeDtypeStruct((C, cap3, sub, EDGE), F32),
            jax.ShapeDtypeStruct((5, EDGE, EDGE), F32),
            jax.ShapeDtypeStruct((2, EDGE, EDGE), F32),
        ],
        scratch_shapes=[
            pltpu.VMEM(held.shape, F32),
            pltpu.VMEM((R, cap2, sub, EDGE), F32),
            pltpu.VMEM((R * cap2, sub, EDGE), F32),
            pltpu.VMEM((C, cap3, sub, EDGE), F32),
            pltpu.VMEM((C, EDGE, EDGE), F32),
            pltpu.VMEM((C - early(C), EDGE, EDGE), F32),
            dma((R * (C - early(C)),)), dma((C - early(C),)),
            pltpu.VMEM((2, EDGE, EDGE), F32),
            pltpu.VMEM((2 * C, sub, EDGE), F32),
            pltpu.VMEM((C, 2, sub, EDGE), F32),
            dma((C,)), dma((2,)), dma((C,)), dma((C,)), dma,
            pltpu.VMEM((3, EDGE, EDGE), F32),
            pltpu.VMEM((3, sub, EDGE), F32),
            pltpu.VMEM((C, 3, sub, EDGE), F32),
            pltpu.VMEM((EDGE, 2 * EDGE), F32),
            pltpu.VMEM((EDGE, 2 * EDGE), F32),
            pltpu.VMEM((5, EDGE, EDGE), F32),
            dma((R,)), dma((2,)), dma((C,)), dma((2,)), dma((C,)), dma((1,)),
            dma((R,)), dma((2,)), dma((C,)), dma((C,)), dma,
            dma((C,)), dma((C,)), dma((R * C,)), dma((C, R)),
            dma, dma((R,)), dma((R,)), dma((C, parts3)), dma((C, parts3)),
        ],
        compiler_params=pltpu.CompilerParams(
            collective_id=name, has_side_effects=True, vmem_limit_bytes=60 << 20
        ),
        name="spread",
    )(held, index2, index3, pick, chosen, slab, front)


def panel_kernel(
    R, C, chunk, low, qrow, qcol,
    rows_q, zbuf, cols_q,
    ag_send, ag_recv, z_send, z_recv, v_send, v_recv, q_sem,
):
    r = lax.axis_index("row")
    c = lax.axis_index("col")
    ratio = C // R
    greet(R, C, r, c)

    i = c * R + r
    q0 = dot(chunk[0], low[1], NT)
    q1 = dot(chunk[1] - dot(q0, low[2], NT), low[4], NT)
    rows_q[0, c] = jnp.where(i == 0, low[0], jnp.where(i == 1, low[2], q0))
    rows_q[1, c] = jnp.where(i == 0, 0.0, jnp.where(i == 1, low[3], q1))

    def gather(k, n):
        here = rows_q.at[n, c]
        return remote(here, here, ag_send.at[n, k], ag_recv.at[n, c], r, lax.rem(c + k, C))

    def along(k, n):
        return remote(
            rows_q.at[n, c], zbuf.at[n, r], z_send.at[n, k], z_recv.at[n, r], lax.rem(r + k, R), c
        )

    for n in range(2):
        for k in range(1, R):
            along(k, n).start()
    for n in range(2):
        for k in range(1, C):
            gather(k, n).start()

    mine = lax.rem(c, ratio) * R
    place = c // ratio

    def serve(p, n):
        return remote(
            zbuf.at[n, p], cols_q.at[n, place], v_send.at[n, p], v_recv.at[n, place], r, mine + p
        )

    def serve_own(p, n):
        return pltpu.make_async_copy(zbuf.at[n, p], cols_q.at[n, place], v_recv.at[n, place])

    own_z = [pltpu.make_async_copy(rows_q.at[n, c], zbuf.at[n, r], z_recv.at[n, r]) for n in range(2)]
    for copy in own_z:
        copy.start()
    for copy in own_z:
        copy.wait()

    def pass_on(p):
        for n in range(2):

            @pl.when(p != r)
            def _():
                remote(rows_q.at[n, 0], zbuf.at[n, p], z_send.at[n, 0], z_recv.at[n, p], r, c).wait_recv()

            @pl.when(mine + p == c)
            def _():
                serve_own(p, n).start()

            @pl.when(mine + p != c)
            def _():
                serve(p, n).start()

    over(0, R, pass_on)

    def row_wait(jl):
        @pl.when(jl != c)
        def _():
            for n in range(2):
                here = rows_q.at[n, jl]
                remote(here, here, ag_send.at[n, 0], ag_recv.at[n, jl], r, c).wait_recv()

    over(0, C, row_wait)
    keep_row = pltpu.make_async_copy(rows_q, qrow, q_sem.at[1])
    keep_row.start()

    def col_wait(s):
        for n in range(2):
            pltpu.make_async_copy(zbuf.at[n, 0], cols_q.at[n, s], v_recv.at[n, s]).wait()

    over(0, R, col_wait)
    keep_col = pltpu.make_async_copy(cols_q, qcol, q_sem.at[0])
    keep_col.start()

    for n in range(2):
        for k in range(1, C):
            gather(k, n).wait_send()
        for k in range(1, R):
            along(k, n).wait_send()

    def served(p):
        @pl.when(mine + p != c)
        def _():
            for n in range(2):
                serve(p, n).wait_send()

    over(0, R, served)
    keep_col.wait()
    keep_row.wait()


def panels(R, C, chunk, low):
    hbm = pl.BlockSpec(memory_space=pltpu.HBM)
    dma = pltpu.SemaphoreType.DMA
    return pl.pallas_call(
        functools.partial(panel_kernel, R, C),
        in_specs=[pl.BlockSpec(memory_space=pltpu.VMEM)] * 2,
        out_specs=[hbm, hbm],
        out_shape=[
            jax.ShapeDtypeStruct((2, C, EDGE, EDGE), F32),
            jax.ShapeDtypeStruct((2, R, EDGE, EDGE), F32),
        ],
        scratch_shapes=[
            pltpu.VMEM((2, C, EDGE, EDGE), F32),
            pltpu.VMEM((2, R, EDGE, EDGE), F32),
            pltpu.VMEM((2, R, EDGE, EDGE), F32),
            dma((2, C)), dma((2, C)),
            dma((2, R)), dma((2, R)), dma((2, R)), dma((2, R)), dma((2,)),
        ],
        compiler_params=pltpu.CompilerParams(
            collective_id=1, has_side_effects=True, vmem_limit_bytes=60 << 20
        ),
        name="panels",
    )(chunk, low)


def halves(x):
    high = x.astype(BF16)
    return high, (x - high.astype(F32)).astype(BF16)


def update_kernel(R, C, place, landing, grid, qrow, qcol, source, out, arrived, left, right, head, follow, sem):
    s = pl.program_id(0)
    slots = arrived.shape[1]
    batch = PACK * 4
    r, c = place[0], place[1]
    j = s * C + c
    rows = lax.broadcasted_iota(jnp.int32, (EDGE, EDGE), 0)
    cols = lax.broadcasted_iota(jnp.int32, (EDGE, EDGE), 1)

    @pl.when(s == 0)
    def _():
        def clear(k):
            head[k] = -1

        over(0, R, clear)

        def link(k, used):
            where = landing[1 + slots + k]

            @pl.when(where >= 0)
            def _():
                follow[k] = head[where]
                head[where] = k

            return jnp.where(where >= 0, k + 1, used)

        used = lax.fori_loop(0, slots, link, 0)
        batches = lax.div(used + batch - 1, batch)

        def load(b):
            at = pl.ds(pl.multiple_of(b * batch, batch), batch)
            return pltpu.make_async_copy(source.at[:, at], arrived.at[:, at], sem.at[b])

        over(0, batches, lambda b: load(b).start())

        def split(jl):
            at = pl.ds(pl.multiple_of(jl * EDGE, EDGE), EDGE)
            for n in range(2):
                high, low = halves(qrow[n, jl])
                for m, part in ((0, high), (2, high), (4, low)):
                    left[at, (m + n) * EDGE : (m + n + 1) * EDGE] = part

        over(0, C, split)
        over(0, batches, lambda b: load(b).wait())

    for n in range(2):
        high, low = halves(qcol[n, 0])
        for m, part in ((0, high.T), (2, low.T), (4, high.T)):
            right[(m + n) * EDGE : (m + n + 1) * EDGE, :] = part

    many = min(4, C)
    for g in range(C // many):
        last = (g * many + many - 1) * R + r

        @pl.when((last >= j) & (j >= 2))
        def _():
            product = dot16(left[g * many * EDGE : (g + 1) * many * EDGE, :], right[...], NN)
            for u in range(many):
                out[g * many + u, 0] = grid[g * many + u, 0] - product[u * EDGE : (u + 1) * EDGE, :]

    @pl.when(j < 2)
    def _():
        for jl in range(C):
            out[jl, 0] = jnp.where(j == 0, qrow[0, jl], qrow[1, jl])

    def more(k):
        return k >= 0

    def add(k):
        jl = landing[1 + k]
        out[jl, 0] = out[jl, 0] + arrived[:, k].reshape(EDGE, EDGE)
        return follow[k]

    lax.while_loop(more, add, jnp.where(j >= 2, head[s], -1))
    for jl in range(C):
        i = jl * R + r

        @pl.when(i < j)
        def _():
            out[jl, 0] = jnp.zeros((EDGE, EDGE), F32)

        @pl.when((i == j) & (j >= 2))
        def _():
            out[jl, 0] = jnp.where(rows >= cols, out[jl, 0], 0.0)


def update(R, C, place, landing, grid, qrow, qcol, arrived):
    cap3 = arrived.shape[1]
    block = pl.BlockSpec((C, 1, EDGE, EDGE), lambda s, *_: (0, s, 0, 0))
    return pl.pallas_call(
        functools.partial(update_kernel, R, C),
        grid_spec=pltpu.PrefetchScalarGridSpec(
            num_scalar_prefetch=2,
            grid=(R,),
            in_specs=[
                block,
                pl.BlockSpec((2, C, EDGE, EDGE), lambda s, *_: (0, 0, 0, 0)),
                pl.BlockSpec((2, 1, EDGE, EDGE), lambda s, *_: (0, s, 0, 0)),
                pl.BlockSpec(memory_space=pltpu.HBM),
            ],
            out_specs=block,
            scratch_shapes=[
                pltpu.VMEM(arrived.shape, F32),
                pltpu.VMEM((C * EDGE, 6 * EDGE), BF16),
                pltpu.VMEM((6 * EDGE, EDGE), BF16),
                pltpu.SMEM((R,), jnp.int32),
                pltpu.SMEM((cap3,), jnp.int32),
                pltpu.SemaphoreType.DMA((cap3 // (PACK * 4),)),
            ],
        ),
        out_shape=jax.ShapeDtypeStruct((C, R, EDGE, EDGE), F32),
        compiler_params=pltpu.CompilerParams(vmem_limit_bytes=60 << 20),
        name="update",
    )(place, landing, grid, qrow, qcol, arrived)


def capacities(R, C, T):
    if T < 32:
        return 16, (PACK * 4, PACK * 8)
    return 104, (80, 112, 160)


def hot(values, count):
    return (values[..., None] == jnp.arange(count, dtype=jnp.int32)).astype(BF16)


def before(marks):
    n = marks.shape[-2]
    serial = jnp.arange(n, dtype=jnp.int32)
    lower = (serial[:, None] > serial[None, :]).astype(BF16)
    return jnp.einsum("pq,...qk->...pk", lower, marks, preferred_element_type=F32)


def local(front_entries, child_updates, row_maps, col_maps, target_columns, row_offsets):
    R = lax.axis_size("row")
    C = lax.axis_size("col")
    count = R * C
    T = child_updates.shape[0]
    cap2, choices = capacities(R, C, T)
    cap3 = choices[-1]
    my_row = lax.axis_index("row").astype(jnp.int32)
    my_col = lax.axis_index("col").astype(jnp.int32)

    told = jnp.concatenate([target_columns[:, 0], row_offsets[:, 0]])
    told = jnp.pad(told, (0, EDGE - 2 * T)).reshape(1, EDGE)
    front = front_entries.reshape(count, EDGE, EDGE)
    held, told, slab = begin(R, C, child_updates, row_maps, col_maps, told, front)
    told = told.reshape(C, R, EDGE).transpose(1, 0, 2).reshape(count, EDGE)
    columns, offsets = told[:, :T], told[:, T : 2 * T]
    target_rows = columns + offsets % (count - columns)
    columns = columns.reshape(R, C * T)
    target_rows = target_rows.reshape(R, C * T)
    to_row, to_col = target_rows % R, columns % C

    row_hot = hot(to_row, R)
    panel = columns < 2
    lead = row_hot * panel[..., None].astype(BF16)
    rest = row_hot - lead
    leads = jnp.sum(lead.astype(F32), axis=1, keepdims=True)
    rank2 = before(lead) * lead.astype(F32) + (before(rest) + leads) * rest.astype(F32)
    rank2 = jnp.sum(rank2, axis=-1).astype(jnp.int32)
    mine = to_row == my_row
    col_hot = hot(jnp.where(mine, to_col, -1), C)
    inside = before(col_hot)
    totals = jnp.sum(col_hot.astype(F32), axis=1)
    planes = jnp.arange(R, dtype=jnp.int32)
    ahead = jnp.sum(jnp.where((planes[:, None] > planes[None, :])[..., None], totals[None], 0.0), axis=1)
    rank3 = jnp.sum((inside + ahead[:, None, :]) * col_hot.astype(F32), axis=-1).astype(jnp.int32)
    loads2 = jnp.sum(row_hot.astype(F32), axis=1)
    loads3 = jnp.einsum("pqk,pql->kl", row_hot, hot(to_col, C), preferred_element_type=F32)
    passes2 = (jnp.max(loads2).astype(jnp.int32) + cap2 - 1) // cap2
    most3 = jnp.max(loads3).astype(jnp.int32)
    passes3 = (most3 + cap3 - 1) // cap3

    def tables(a, b):
        own_hot = lax.dynamic_index_in_dim(row_hot, my_row, 0, keepdims=False)
        own_rank = lax.dynamic_index_in_dim(rank2, my_row, 0, keepdims=False)
        serial = jnp.arange(C * T, dtype=jnp.int32)
        values = jnp.stack([serial // T, serial % T], axis=0).astype(BF16)
        marked = values[:, :, None] * own_hot[None]
        found = jnp.einsum("vqk,qn->vkn", marked, hot(own_rank - a * cap2, cap2), preferred_element_type=F32)
        found = found.astype(jnp.int32)
        index2 = (found[0] * T + found[1]).reshape(-1)
        place2 = rank2 - a * cap2
        active = (place2 >= 0) & (place2 < cap2) & mine
        source = jnp.broadcast_to(planes[:, None], (R, C * T))
        values = jnp.stack(
            [source, place2, target_rows // R, columns // C, jnp.ones_like(source)], axis=0
        )
        values = jnp.where(active, values, 0).astype(BF16)
        marked = values[..., None] * col_hot[None]
        found = jnp.einsum(
            "vpqk,pqn->vkn", marked, hot(rank3 - b * cap3, cap3), preferred_element_type=F32
        ).astype(jnp.int32)
        index3 = (found[0] * cap2 + found[1]).reshape(-1)
        here = lax.dynamic_index_in_dim(found, my_col, 1, keepdims=False)
        return index2, index3, here[2], here[3], here[4]

    index2, index3, land_row, land_col, valid = tables(0, 0)
    marks = hot(jnp.where(mine & panel, target_rows // R * 2 + columns, -1), 2 * C)
    chosen = jnp.einsum("pqv,pqn->pvn", marks, hot(rank2, cap2), preferred_element_type=F32)
    pick = chosen[:, :2].transpose(1, 0, 2).reshape(-1)
    chosen = chosen.astype(BF16)
    runs = [
        functools.partial(spread, R, C, cap2, cap3, size // (PACK * 4), 10 + at)
        for at, size in enumerate(choices)
    ]
    choice = sum((most3 > size).astype(jnp.int32) for size in choices[:-1])
    grid, arrived, low, chunk = lax.switch(
        choice, runs, held, index2, index3, pick, chosen, slab, front
    )

    def another(carry):
        p, grid = carry
        index2, index3, land_row, land_col, valid = tables(p // passes3, p % passes3)
        moved = held[index2].reshape(R, cap2, EDGE // C, EDGE)
        moved = lax.all_to_all(moved, "row", split_axis=0, concat_axis=0, tiled=True)
        moved = moved.reshape((R * cap2, EDGE // C, EDGE))[index3].reshape(C, cap3, EDGE // C, EDGE)
        moved = lax.all_to_all(moved, "col", split_axis=0, concat_axis=0, tiled=True)
        tiles = moved.transpose(1, 0, 2, 3).reshape(cap3, EDGE, EDGE)
        tiles = jnp.where((valid > 0)[:, None, None], tiles, 0.0)
        return p + 1, grid.at[land_row, land_col].add(tiles)

    _, grid = lax.while_loop(lambda carry: carry[0] < passes2 * passes3, another, (jnp.int32(1), grid))

    landing = jnp.concatenate([my_col[None], land_row, jnp.where(valid > 0, land_col, -1)])
    qrow, qcol = panels(R, C, chunk, low)
    place = jnp.stack([my_row, my_col])
    result = update(R, C, place, landing, grid, qrow, qcol, arrived)
    return result.reshape(C, 1, R, 1, EDGE, EDGE)


def solution(mesh):
    return jax.shard_map(
        local,
        mesh=mesh,
        in_specs=(
            P(None, ("row", "col")),
            P(("row", "col"), None, None),
            P(("row", "col"), None),
            P(("row", "col"), None),
            P(("row", "col"), None),
            P(("row", "col"), None),
        ),
        out_specs=P(None, "row", None, "col", None, None),
        check_vma=False,
    )
```
